32 devices in a mesh: group: 2 (over y), dp: 16 (over z, x, core).
Axes of the slice: x: 2, y: 2, z: 4, core: 2. Of those that a mesh axis runs over, the one named last changes fastest.
Arguments:
- frames: bfloat16 [2, 64, 128, 84, 336], P('group', 'dp'), may hold values from 0 to 1
- actions: int32 [2, 64, 128], P('group', 'dp'), may hold values from 0 to 17
- rewards: float32 [2, 64, 128], P('group', 'dp'), may hold values from 0 to 0.75
- old_values: float32 [2, 64, 128], P('group', 'dp'), may hold values from -6 to 6
- next_values: float32 [2, 64, 128], P('group', 'dp'), may hold values from -6 to 6
- terminal: int32 [2, 64, 128], P('group', 'dp'), may hold values 0 or 1
- truncated: int32 [2, 64, 128], P('group', 'dp'), may hold values 0 or 1
- behavior_logprob: float32 [2, 64, 128], P('group', 'dp'), may hold values from -3.5 to -2.3
- master: float32 [1695744], P('dp'), may hold values from -2 to 2
- first_moment: float32 [2, 1695744], P('group', 'dp'), may hold values from -1 to 1
- second_moment: float32 [2, 1695744], P('group', 'dp'), may hold values from 0 to 1, as said below
- outer_momentum: float32 [1695744], P('dp'), may hold values from -0.15625 to 0.15625
- step_count: int32 [1], replicated, may hold values from 2 to 20
Outputs:
- grads: float32 [2, 1695744], P('group', 'dp')
- norms: float32 [2], P('group')
- losses: float32 [2], P('group')
- first_new: float32 [2, 1695744], P('group', 'dp')
- second_new: float32 [2, 1695744], P('group', 'dp')
- moved: float32 [1695744], P('dp')
- momentum_new: float32 [1695744], P('dp')
- final: float32 [1695744], P('dp')
- final_low: bfloat16 [1695744], P('dp')
The draws below stay inside these ranges and needn't reach their ends.
Inputs may be any that keep to these rules, and one draw needn't show every extreme that they name: `second_moment`: entries are positive.
All inputs are finite; a program needn't handle non-finite values. No bound on the sum of `terminal` or of `truncated` on one device may be relied on, other than what follows from the above.
Results may differ from the reference program's by a relative error of at most 0.0011.
The reference program's roundings to bfloat16 on the way count: a program that leaves them out, or rounds other values in their place, can miss the bound.
Values may be sent and summed in bfloat16 or wider, within the bound.
No kernel may reach another device: no remote copies, remote signals or barrier semaphores. Data moves between devices by JAX's collectives and lax.ppermute only.
A program may use at most 320 MiB of HBM per device.

```python
import math
import jax
import jax.numpy as jnp
from jax import lax

C1 = 32
C2 = 64
C3 = 64
HID = 512
ACTIONS = 18
STEPS = 128
ENVS = 64
PARAMS = 1693875
FLAT = 1695744
N_GROUP = 2


def layer_pieces():
    return [(256 * C1, math.sqrt(2.0 / 256), 0), (C1, 0.0, 1), (16 * C1 * C2, math.sqrt(2.0 / (16 * C1)), 0), (C2, 0.0, 1), (9 * C2 * C3, math.sqrt(2.0 / (9 * C2)), 0), (C3, 0.0, 1), (49 * C3 * HID, math.sqrt(2.0 / (49 * C3)), 0), (HID, 0.0, 1), (HID * (ACTIONS + 1), 2.0 / math.sqrt(HID), 2), (ACTIONS + 1, 0.0, 1)]


def gradient_level():
    return 0.5 / math.sqrt(PARAMS)


def draw_master(key, part):
    drawn = jax.random.truncated_normal(jax.random.fold_in(key, 12), -4.0, 4.0, (FLAT,), jnp.float32)
    biases = jax.random.uniform(jax.random.fold_in(key, 13), (FLAT,), jnp.float32, -0.3, 0.3)
    place = jnp.arange(FLAT, dtype=jnp.int32)
    result = drawn * 0.01
    offset = 0
    for length, spread, sort_kind in layer_pieces():
        inside = (place >= offset) & (place < offset + length)
        if sort_kind == 1:
            values = biases
        elif sort_kind == 2:
            column = (place - offset) % (ACTIONS + 1)
            values = drawn * jnp.where(column == ACTIONS, spread * 0.5, spread)
        else:
            values = drawn * spread
        result = jnp.where(inside, values, result)
        offset += length
    return result


def draw_first_moment(key, part):
    level = gradient_level() * (0.1 / 0.9)
    drawn = jax.random.truncated_normal(jax.random.fold_in(key, 22), -4.0, 4.0, (N_GROUP, FLAT), jnp.float32)
    return drawn * level


def draw_second_moment(key, part):
    level = gradient_level() * gradient_level() * (0.001 / 0.999)
    factor = jnp.exp(jax.random.uniform(jax.random.fold_in(key, 32), (N_GROUP, FLAT), jnp.float32, math.log(0.5), math.log(8.0)))
    return factor * level


def draw_rewards(key, part):
    base = jax.random.uniform(jax.random.fold_in(key, 42), (N_GROUP, ENVS, STEPS), jnp.float32, 0.0, 1.0)
    ramp = 1.0 + 2.0 * jnp.arange(ENVS, dtype=jnp.float32) / max(ENVS - 1, 1)
    return base * 0.25 * ramp[None, :, None]


def touch_ends(entries, own_key, smallest, high):
    longest = entries.shape.index(max(entries.shape))
    spots = []
    for shift in (0, 1):
        where = [jax.random.randint(jax.random.fold_in(own_key, axis), (), 0, length) for axis, length in enumerate(entries.shape)]
        where[longest] = (where[longest] + shift) % entries.shape[longest]
        spots.append(tuple(where))
    return entries.at[spots[0]].set(smallest).at[spots[1]].set(high)


def steps_of(key, dims, cuts, least, high):
    def one(dim, parts):
        steps = jax.random.uniform(jax.random.fold_in(jax.random.fold_in(key, 6), dim), (parts,), jnp.float32, least / len(cuts), high / len(cuts))
        return jnp.repeat(jnp.exp(steps), dims[dim] // parts).reshape((-1,) + (1,) * (len(dims) - dim - 1))

    factor_of = one(*cuts[0])
    for cut in cuts[1:]:
        factor_of = factor_of * one(*cut)
    return factor_of


def noise(rng, dims, deviation, reach, shards=(), held_as=jnp.bfloat16):
    drawn = jax.random.normal(rng, dims, jnp.float32) * deviation
    if len(shards) > 0:
        drawn = steps_of(rng, dims, shards, -0.22, 0.18) * drawn
    return jnp.clip(drawn, min=-reach, max=reach).astype(held_as)


def setup_inputs(seed: int = 0) -> dict:
    key_of = jax.random.split(jax.random.key(seed), 14)
    frames = jnp.clip(1.0 * jax.random.uniform(key_of[0], (N_GROUP, ENVS, STEPS, 84, 336), jnp.float32) ** steps_of(key_of[0], (N_GROUP, ENVS, STEPS, 84, 336), ((0, 2), (1, 16)), -0.2, 0.2), 0.0, 1.0).astype(jnp.bfloat16)
    actions = touch_ends(jax.random.randint(key_of[1], (N_GROUP, ENVS, STEPS), 0, ACTIONS), jax.random.fold_in(key_of[1], 1), 0, ACTIONS - 1).astype(jnp.int32)
    rewards = draw_rewards(jax.random.fold_in(key_of[13], 71), 0)
    old_values = noise(key_of[3], (N_GROUP, ENVS, STEPS), 1.0, 6.0, ((0, 2), (1, 16)), jnp.float32)
    next_values = noise(key_of[4], (N_GROUP, ENVS, STEPS), 1.0, 6.0, ((0, 2), (1, 16)), jnp.float32)
    terminal = touch_ends((jax.random.randint(key_of[5], (N_GROUP, ENVS, STEPS), 0, 64) < 1).astype(jnp.int32), jax.random.fold_in(key_of[5], 1), 0, 1)
    truncated = touch_ends((jax.random.randint(key_of[6], (N_GROUP, ENVS, STEPS), 0, 32) < 1).astype(jnp.int32), jax.random.fold_in(key_of[6], 1), 0, 1)
    behavior_logprob = jnp.clip(-3.5 + 1.2 * jax.random.uniform(key_of[7], (N_GROUP, ENVS, STEPS), jnp.float32) ** steps_of(key_of[7], (N_GROUP, ENVS, STEPS), ((0, 2), (1, 16)), -0.2, 0.2), -3.5, -2.3)
    master = draw_master(jax.random.fold_in(key_of[13], 71), 0)
    first_moment = draw_first_moment(jax.random.fold_in(key_of[13], 71), 0)
    second_moment = draw_second_moment(jax.random.fold_in(key_of[13], 71), 0)
    outer_momentum = noise(key_of[11], (FLAT,), 0.01, 0.15625, ((0, 16),), jnp.float32)
    step_count = jax.random.randint(key_of[12], (1,), 2, 21).astype(jnp.int32)
    return dict(frames=frames, actions=actions, rewards=rewards, old_values=old_values, next_values=next_values, terminal=terminal, truncated=truncated, behavior_logprob=behavior_logprob, master=master, first_moment=first_moment, second_moment=second_moment, outer_momentum=outer_momentum, step_count=step_count)


@jax.custom_vjp
def low(v):
    return lax.optimization_barrier(v.astype(jnp.bfloat16)).astype(jnp.float32)

@jax.custom_vjp
def low_back(v):
    return v

def low_keep(v):
    return (low(v), None)

def low_pass(kept, grad):
    return (grad,)

def back_keep(v):
    return (v, None)

def back_low(kept, grad):
    return (low(grad),)
low.defvjp(low_keep, low_pass)
low_back.defvjp(back_keep, back_low)
BETA_ONE = 0.9
BETA_TWO = 0.999
ADAM_EPSILON = 1e-08
LEARN_RATE = 0.005
WEIGHT_DECAY = 0.01
CLIP_NORM = 0.5
OUTER_RATE = 0.7
OUTER_MOMENTUM = 0.9
DISCOUNT = 0.99
TRACE_DECAY = 0.95
RATIO_CLIP = 0.1
VALUE_COEF = 0.5
ENTROPY_COEF = 0.01

def param_shapes():
    return [(8, 8, 4, C1), (C1,), (4, 4, C1, C2), (C2,), (3, 3, C2, C3), (C3,), (49 * C3, HID), (HID,), (HID, ACTIONS + 1), (ACTIONS + 1,)]

def unpack(packed):
    pieces = []
    offset = 0
    for layout in param_shapes():
        length = math.prod(layout)
        pieces.append(packed[offset:offset + length].reshape(layout))
        offset += length
    return pieces

def trajectory_advantages(rewards, values, next_values, terminal, truncated):
    alive = 1.0 - terminal.astype(jnp.float32)
    cutoff = truncated.astype(jnp.float32)
    following = jnp.concatenate([values[:, 1:], next_values[:, -1:]], axis=1)
    following = cutoff * next_values + (1.0 - cutoff) * following
    deltas = rewards + DISCOUNT * alive * following - values
    keeping = DISCOUNT * TRACE_DECAY * alive * (1.0 - cutoff)

    def backward_step(carry, item):
        delta, keep = item
        result = delta + keep * carry
        return (result, result)
    start = jnp.zeros((rewards.shape[0],), jnp.float32)
    _, series = lax.scan(backward_step, start, (deltas.T, keeping.T), reverse=True)
    return series.T

def frame_losses(out, normed, returns, actions, behavior):
    logits = out[:, :ACTIONS]
    value = out[:, ACTIONS]
    log_probs = jax.nn.log_softmax(logits, axis=-1)
    chosen = actions[:, None] == jnp.arange(ACTIONS, dtype=jnp.int32)[None, :]
    taken = lax.optimization_barrier(jnp.sum(jnp.where(chosen, log_probs, 0.0), axis=-1))
    ratio = jnp.exp(taken - behavior)
    surrogate = jnp.minimum(ratio * normed, jnp.clip(ratio, 1.0 - RATIO_CLIP, 1.0 + RATIO_CLIP) * normed)
    entropy = -lax.optimization_barrier(jnp.sum(jnp.exp(log_probs) * log_probs, axis=-1))
    return jnp.sum(-surrogate + 0.5 * VALUE_COEF * (value - returns) ** 2 - ENTROPY_COEF * entropy)

def network(params, pixels):
    w_one, b_one, w_two, b_two, w_three, b_three, w_dense, b_dense, w_head, b_head = params
    numbers = ('NHWC', 'HWIO', 'NHWC')
    highest = lax.Precision.HIGHEST
    conv_one = lax.conv_general_dilated(pixels, w_one, (4, 4), 'VALID', dimension_numbers=numbers, precision=highest)
    act_one = low(jax.nn.relu(low_back(conv_one + b_one)))
    conv_two = lax.conv_general_dilated(act_one, w_two, (2, 2), 'VALID', dimension_numbers=numbers, precision=highest)
    act_two = low(jax.nn.relu(low_back(conv_two + b_two)))
    conv_three = lax.conv_general_dilated(act_two, w_three, (1, 1), 'VALID', dimension_numbers=numbers, precision=highest)
    act_three = low(jax.nn.relu(low_back(conv_three + b_three)))
    features = act_three.reshape(act_three.shape[0], 49 * C3)
    hidden = low(jax.nn.relu(low_back(jnp.dot(features, w_dense, precision=highest) + b_dense)))
    return low_back(jnp.dot(hidden, w_head, precision=highest) + b_head)

def reference(frames, actions, rewards, old_values, next_values, terminal, truncated, behavior_logprob, master, first_moment, second_moment, outer_momentum, step_count):
    moment_step = step_count[0].astype(jnp.float32)
    frame_count = ENVS * STEPS
    scale = 1.0 / frame_count
    grads_all, norms_all, losses_all, firsts, seconds, inners = ([], [], [], [], [], [])
    for group in range(N_GROUP):
        advantage = trajectory_advantages(rewards[group], old_values[group], next_values[group], terminal[group], truncated[group])
        mean = jnp.sum(advantage) / frame_count
        spread = jnp.sum(advantage * advantage) / frame_count - mean * mean
        normed = (advantage - mean) * lax.rsqrt(spread + 1e-05)
        returns = advantage + old_values[group]

        def accumulate(carry, item):
            loss_total, grad_total = carry
            block_frames, block_normed, block_returns, block_actions, block_prior = item

            def objective(packed):
                params = unpack(low(packed))
                out = network(params, block_frames.astype(jnp.float32).reshape(-1, 84, 84, 4))
                return frame_losses(out, block_normed, block_returns, block_actions, block_prior) * scale
            value, pullback = jax.vjp(objective, master)
            gradient = pullback(jnp.ones((), jnp.float32))[0]
            return ((loss_total + value, grad_total + gradient), None)
        start = (jnp.zeros((), jnp.float32), jnp.zeros((FLAT,), jnp.float32))
        (loss_total, grads_sum), _ = lax.scan(accumulate, start, (frames[group], normed, returns, actions[group], behavior_logprob[group]))
        norm = jnp.sqrt(jnp.sum(grads_sum * grads_sum))
        factor = jnp.minimum(1.0, CLIP_NORM / (norm + 1e-06))
        clipped = grads_sum * factor
        first_next = BETA_ONE * first_moment[group] + (1.0 - BETA_ONE) * clipped
        second_next = BETA_TWO * second_moment[group] + (1.0 - BETA_TWO) * clipped * clipped
        first_hat = first_next / (1.0 - jnp.power(BETA_ONE, moment_step))
        second_hat = second_next / (1.0 - jnp.power(BETA_TWO, moment_step))
        inner = master - LEARN_RATE * (first_hat / (jnp.sqrt(second_hat) + ADAM_EPSILON) + WEIGHT_DECAY * master)
        grads_all.append(clipped)
        norms_all.append(norm)
        losses_all.append(loss_total)
        firsts.append(first_next)
        seconds.append(second_next)
        inners.append(master - inner)
    moved = sum(inners) / N_GROUP
    momentum_new = OUTER_MOMENTUM * outer_momentum + moved
    final = master - OUTER_RATE * (moved + OUTER_MOMENTUM * momentum_new)
    return (jnp.stack(grads_all), jnp.stack(norms_all), jnp.stack(losses_all), jnp.stack(firsts), jnp.stack(seconds), moved, momentum_new, final, final.astype(jnp.bfloat16))
```

```python
import math

import jax
import jax.numpy as jnp
from jax import lax
from jax.experimental import pallas as pl
from jax.experimental.pallas import tpu as pltpu
from jax.sharding import PartitionSpec as P

C1 = 32
C2 = 64
C3 = 64
HID = 512
ACTIONS = 18
PARAMS = 1693875
FEATURES = 49 * C3
CONV_LEN = 256 * C1 + C1 + 16 * C1 * C2 + C2 + 9 * C2 * C3 + C3
TOP = CONV_LEN // HID
PHASE = CONV_LEN % HID
HEAD_LEN = HID * (ACTIONS + 1) + ACTIONS + 1

BETA_ONE = 0.9
BETA_TWO = 0.999
ADAM_EPSILON = 1e-08
LEARN_RATE = 0.005
WEIGHT_DECAY = 0.01
CLIP_NORM = 0.5
OUTER_RATE = 0.7
OUTER_MOMENTUM = 0.9
DISCOUNT = 0.99
TRACE_DECAY = 0.95
RATIO_CLIP = 0.1
VALUE_COEF = 0.5
ENTROPY_COEF = 0.01

F32 = jnp.float32
BF16 = jnp.bfloat16
VMEM_LIMIT = 63 * 1024 * 1024


def mm(a, b):
    return jnp.dot(a, b, preferred_element_type=F32)


def mm_nt(a, b):
    return lax.dot_general(a, b, (((1,), (1,)), ((), ())), preferred_element_type=F32)


def mm_tn(a, b):
    return lax.dot_general(a, b, (((0,), (0,)), ((), ())), preferred_element_type=F32)


def trajectory_advantages(rewards, values, next_values, terminal, truncated):
    alive = 1.0 - terminal.astype(F32)
    cutoff = truncated.astype(F32)
    following = jnp.concatenate([values[:, 1:], next_values[:, -1:]], axis=1)
    following = cutoff * next_values + (1.0 - cutoff) * following
    deltas = rewards + DISCOUNT * alive * following - values
    keeping = DISCOUNT * TRACE_DECAY * alive * (1.0 - cutoff)

    def backward_step(carry, item):
        delta, keep = item
        result = delta + keep * carry
        return (result, result)

    start = jnp.zeros((rewards.shape[0],), F32)
    _, series = lax.scan(backward_step, start, (deltas.T, keeping.T), reverse=True)
    return series.T


def forward_body(x_ref, t1_ref, b1_ref, t2_ref, b2_ref, t3_ref, b3_ref, a1_ref, a2_ref, a3_ref):
    def conv_one(m, carry):
        for n in range(5):
            window = jnp.concatenate(
                [
                    x_ref[e, pl.ds(8 * m, 12), 64 * n : 64 * n + 80, :].reshape(960, 128)
                    for e in range(2)
                ],
                axis=1,
            )
            out = jnp.maximum(mm(t1_ref[...], window) + b1_ref[...], 0.0).astype(BF16)
            a1_ref[pl.ds(2 * m, 2), 4 * n : 4 * n + 4] = out.reshape(2, 4, C1, 256)
        return carry

    lax.fori_loop(0, 10, conv_one, 0)

    def conv_two(p, carry):
        for g in range(3):
            window = a1_ref[pl.ds(2 * p, 4), 6 * g : 6 * g + 8].reshape(1024, 256)
            out = jnp.maximum(mm(t2_ref[...], window) + b2_ref[...], 0.0).astype(BF16)
            a2_ref[p, 3 * g : 3 * g + 3] = out.reshape(3, C2, 256)
        a2_ref[p, 9] = jnp.zeros((C2, 256), BF16)
        return carry

    lax.fori_loop(0, 9, conv_two, 0)

    def conv_three(p, carry):
        window = a2_ref[pl.ds(p, 3), 0:9].reshape(1728, 256)
        out = jnp.maximum(mm(t3_ref[...], window) + b3_ref[...], 0.0).astype(BF16)
        a3_ref[p] = out.reshape(7, C3, 256)
        return carry

    lax.fori_loop(0, 7, conv_three, 0)


def whole(shape):
    return pl.BlockSpec(shape, lambda j: (0,) * len(shape), pipeline_mode=pl.Buffered(1))


def conv_forward(x, t1, b1, t2, b2, t3, b3):
    envs = x.shape[0]
    frames = envs * 128
    return pl.pallas_call(
        forward_body,
        grid=(envs // 2,),
        in_specs=[
            pl.BlockSpec((2, 84, 336, 128), lambda j: (j, 0, 0, 0)),
            whole((256, 960)),
            whole((256, 256)),
            whole((192, 1024)),
            whole((192, 256)),
            whole((448, 1728)),
            whole((448, 256)),
        ],
        out_specs=[
            pl.BlockSpec((20, 20, C1, 256), lambda j: (0, 0, 0, j)),
            pl.BlockSpec((9, 10, C2, 256), lambda j: (0, 0, 0, j)),
            pl.BlockSpec((7, 7, C3, 256), lambda j: (0, 0, 0, j)),
        ],
        out_shape=[
            jax.ShapeDtypeStruct((20, 20, C1, frames), BF16),
            jax.ShapeDtypeStruct((9, 10, C2, frames), BF16),
            jax.ShapeDtypeStruct((7, 7, C3, frames), BF16),
        ],
        compiler_params=pltpu.CompilerParams(vmem_limit_bytes=VMEM_LIMIT),
        name="conv_forward",
    )(x, t1, b1, t2, b2, t3, b3)


def dense_body(
    scale,
    a3_ref,
    wd_ref,
    bd_ref,
    wh_ref,
    bh_ref,
    normed_ref,
    returns_ref,
    actions_ref,
    behavior_ref,
    gwd_ref,
    dc3_ref,
    gbd_ref,
    gwh_ref,
    gbh_ref,
    loss_ref,
):
    hidden_pre = mm_tn(wd_ref[...], a3_ref[...]) + bd_ref[...]
    hidden = jnp.maximum(hidden_pre, 0.0).astype(BF16)
    out = mm(wh_ref[...], hidden) + bh_ref[...]
    row = lax.broadcasted_iota(jnp.int32, out.shape, 0)
    is_logit = row < ACTIONS
    logits = jnp.where(is_logit, out, -jnp.inf)
    top = jnp.max(logits, axis=0, keepdims=True)
    shifted = out - top
    exps = jnp.where(is_logit, jnp.exp(shifted), 0.0)
    total = jnp.sum(exps, axis=0, keepdims=True)
    log_probs = jnp.where(is_logit, shifted - jnp.log(total), 0.0)
    probs = jnp.where(is_logit, jnp.exp(log_probs), 0.0)
    value = jnp.sum(jnp.where(row == ACTIONS, out, 0.0), axis=0, keepdims=True)
    normed = normed_ref[...]
    chosen = row == actions_ref[...]
    taken = jnp.sum(jnp.where(chosen, log_probs, 0.0), axis=0, keepdims=True)
    ratio = jnp.exp(taken - behavior_ref[...])
    low = 1.0 - RATIO_CLIP
    high = 1.0 + RATIO_CLIP
    clipped = jnp.clip(ratio, low, high)
    plain = ratio * normed
    cut = clipped * normed
    entropy = -jnp.sum(probs * log_probs, axis=0, keepdims=True)
    error = value - returns_ref[...]
    losses = -jnp.minimum(plain, cut) + 0.5 * VALUE_COEF * error * error - ENTROPY_COEF * entropy
    loss_ref[...] = jnp.sum(losses, axis=1, keepdims=True) * scale
    plain_share = jnp.where(plain < cut, 1.0, jnp.where(plain == cut, 0.5, 0.0))
    inside = jnp.where(
        (ratio > low) & (ratio < high), 1.0, jnp.where((ratio == low) | (ratio == high), 0.5, 0.0)
    )
    d_taken = -scale * normed * ratio * (plain_share + (1.0 - plain_share) * inside)
    d_logits = d_taken * (jnp.where(chosen, 1.0, 0.0) - probs) + (scale * ENTROPY_COEF) * probs * (
        log_probs + entropy
    )
    d_value = scale * VALUE_COEF * error
    d_out = jnp.where(is_logit, d_logits, jnp.where(row == ACTIONS, d_value, 0.0)).astype(BF16)
    gwh_ref[...] = mm_nt(d_out, hidden)
    gbh_ref[...] = jnp.sum(d_out.astype(F32), axis=1, keepdims=True)
    back = mm_tn(wh_ref[...], d_out)
    d_hidden = jnp.where(hidden_pre > 0, back, 0.0).astype(BF16)
    gbd_ref[...] = jnp.sum(d_hidden.astype(F32), axis=1, keepdims=True)
    gwd_ref[...] = mm_nt(a3_ref[...], d_hidden)
    d_a3 = mm(wd_ref[...], d_hidden)
    dc3_ref[...] = jnp.where(a3_ref[...] > 0, d_a3, 0.0).astype(BF16)


def dense_step(scale, a3, wd, bd, wh, bh, normed, returns, actions, behavior):
    frames = a3.shape[1]
    rows = wh.shape[0]
    return pl.pallas_call(
        lambda *refs: dense_body(scale, *refs),
        out_shape=[
            jax.ShapeDtypeStruct((FEATURES, HID), F32),
            jax.ShapeDtypeStruct((FEATURES, frames), BF16),
            jax.ShapeDtypeStruct((HID, 1), F32),
            jax.ShapeDtypeStruct((rows, HID), F32),
            jax.ShapeDtypeStruct((rows, 1), F32),
            jax.ShapeDtypeStruct((1, 1), F32),
        ],
        compiler_params=pltpu.CompilerParams(vmem_limit_bytes=VMEM_LIMIT),
        name="dense_step",
    )(a3, wd, bd, wh, bh, normed, returns, actions, behavior)


def backward_body(
    x_hbm,
    a1_hbm,
    a2_ref,
    dc3_ref,
    t3_ref,
    t2_ref,
    r1_ref,
    r2_ref,
    r3_ref,
    s1_ref,
    s2_ref,
    s3_ref,
    x_ref,
    a1_ref,
    d3_ref,
    d2_ref,
    d1_ref,
    sems,
):
    step = pl.program_id(0)
    load_x = pltpu.make_async_copy(x_hbm.at[pl.ds(2 * step, 2)], x_ref, sems.at[0])
    lanes = pl.ds(pl.multiple_of(256 * step, 256), 256)
    load_a1 = pltpu.make_async_copy(a1_hbm.at[:, :, :, lanes], a1_ref, sems.at[1])
    load_a1.start()
    load_x.start()

    @pl.when(step == 0)
    def _():
        for ref in (r1_ref, r2_ref, r3_ref, s1_ref, s2_ref, s3_ref):
            ref[...] = jnp.zeros(ref.shape, F32)
        for p in (0, 1, 9, 10):
            d3_ref[p] = jnp.zeros((8, C3, 256), BF16)
        for p in (0, 10):
            d2_ref[p] = jnp.zeros((11, C2, 256), BF16)

        def edge(p, carry):
            d2_ref[p, 0] = jnp.zeros((C2, 256), BF16)
            d2_ref[p, 10] = jnp.zeros((C2, 256), BF16)
            return carry

        lax.fori_loop(1, 10, edge, 0)

    def fill(p, carry):
        d3_ref[p + 2, 0:7] = dc3_ref[p]
        d3_ref[p + 2, 7] = jnp.zeros((C3, 256), BF16)
        s3_ref[...] += jnp.sum(dc3_ref[p].astype(F32), axis=0)
        return carry

    lax.fori_loop(0, 7, fill, 0)

    def three_weights(p, carry):
        left = mm_nt(a2_ref[pl.ds(p, 3), 0:6].reshape(1152, 256), d3_ref[p + 2, 0:4].reshape(256, 256))
        right = mm_nt(
            a2_ref[pl.ds(p, 3), 4:10].reshape(1152, 256), d3_ref[p + 2, 4:8].reshape(256, 256)
        )
        r3_ref[...] += left + right
        return carry

    lax.fori_loop(0, 7, three_weights, 0)

    def three_input(y, carry):
        back = mm(t3_ref[...], d3_ref[pl.ds(y, 3)].reshape(1536, 256)).reshape(9, C2, 256)
        masked = jnp.where(a2_ref[y, 0:9] > 0, back, 0.0).astype(BF16)
        d2_ref[y + 1, 1:10] = masked
        s2_ref[...] += jnp.sum(masked.astype(F32), axis=0)
        return carry

    lax.fori_loop(0, 9, three_input, 0)
    load_a1.wait()

    def two_weights(p, carry):
        total = 0.0
        for g in range(3):
            total = total + mm_nt(
                a1_ref[pl.ds(2 * p, 4), 6 * g : 6 * g + 8].reshape(1024, 256),
                d2_ref[p + 1, 1 + 3 * g : 4 + 3 * g].reshape(192, 256),
            )
        r2_ref[...] += total
        return carry

    lax.fori_loop(0, 9, two_weights, 0)
    load_x.wait()

    def one_weights(m, carry):
        total = 0.0
        sums = jnp.zeros((C1, 256), F32)
        for n in range(5):
            back = mm(t2_ref[...], d2_ref[pl.ds(m, 2), 2 * n : 2 * n + 3].reshape(384, 256))
            kept = a1_ref[pl.ds(2 * m, 2), 4 * n : 4 * n + 4].reshape(256, 256) > 0
            masked = jnp.where(kept, back, 0.0).astype(BF16)
            sums = sums + jnp.sum(masked.astype(F32).reshape(8, C1, 256), axis=0)
            window = jnp.concatenate(
                [
                    x_ref[e, pl.ds(8 * m, 12), 64 * n : 64 * n + 80, :].reshape(960, 128)
                    for e in range(2)
                ],
                axis=1,
            )
            total = total + mm_nt(window, masked)
        r1_ref[...] += total
        s1_ref[...] += sums
        return carry

    lax.fori_loop(0, 10, one_weights, 0)


def conv_backward(x, a1, a2, dc3, t3, t2):
    envs = x.shape[0]
    sums = [(960, 256), (1024, 192), (1152, 256), (C1, 256), (C2, 256), (C3, 256)]
    return pl.pallas_call(
        backward_body,
        grid=(envs // 2,),
        in_specs=[
            pl.BlockSpec(memory_space=pl.ANY),
            pl.BlockSpec(memory_space=pl.ANY),
            pl.BlockSpec((9, 10, C2, 256), lambda j: (0, 0, 0, j)),
            pl.BlockSpec((7, 7, C3, 256), lambda j: (0, 0, 0, j)),
            whole((576, 1536)),
            whole((256, 384)),
        ],
        out_specs=[whole(shape) for shape in sums],
        out_shape=[jax.ShapeDtypeStruct(shape, F32) for shape in sums],
        scratch_shapes=[
            pltpu.VMEM((2, 84, 336, 128), BF16),
            pltpu.VMEM((20, 20, C1, 256), BF16),
            pltpu.VMEM((11, 8, C3, 256), BF16),
            pltpu.VMEM((11, 11, C2, 256), BF16),
            pltpu.VMEM((8, 128), F32),
            pltpu.SemaphoreType.DMA((2,)),
        ],
        compiler_params=pltpu.CompilerParams(vmem_limit_bytes=VMEM_LIMIT),
        name="conv_backward",
    )(x, a1, a2, dc3, t3, t2)


def forward_weights(w_one, w_two, w_three):
    base = w_one.reshape(8, 32, C1).transpose(2, 0, 1)
    t1 = jnp.stack(
        [
            jnp.pad(base, ((0, 0), (4 * i, 4 - 4 * i), (16 * j, 48 - 16 * j)))
            for i in range(2)
            for j in range(4)
        ]
    ).reshape(256, 960)
    base = w_two.reshape(4, 4 * C1, C2).transpose(2, 0, 1)
    t2 = jnp.stack(
        [jnp.pad(base, ((0, 0), (0, 0), (64 * j, 128 - 64 * j))) for j in range(3)]
    ).reshape(192, 1024)
    base = w_three.reshape(3, 3 * C2, C3).transpose(2, 0, 1)
    t3 = jnp.stack(
        [jnp.pad(base, ((0, 0), (0, 0), (64 * j, 384 - 64 * j))) for j in range(7)]
    ).reshape(448, 1728)
    return t1, t2, t3


def backward_weights(w_two, w_three):
    zero = jnp.zeros((), BF16)
    base = w_three[::-1, ::-1].transpose(2, 0, 1, 3).reshape(C2, 3, 3 * C3)
    t3 = jnp.stack(
        [
            lax.pad(base, zero, ((0, 0, 0), (0, 0, 0), (64 * (x - 2), 512 - 192 - 64 * (x - 2), 0)))
            for x in range(9)
        ]
    ).reshape(576, 1536)
    empty = jnp.zeros((C1, C2), BF16)
    blocks = []
    for dy in range(2):
        for dx in range(4):
            line = []
            for r in range(2):
                for s in range(3):
                    j = dx + 2 - 2 * s
                    line.append(w_two[dy + 2 - 2 * r, j] if 0 <= j < 4 else empty)
            blocks.append(jnp.concatenate(line, axis=1))
    return t3, jnp.concatenate(blocks, axis=0)


def conv_gradients(r1, r2, r3):
    r1 = r1.reshape(12, 80, 2, 4, C1)
    g1 = 0.0
    for i in range(2):
        for j in range(4):
            g1 = g1 + r1[4 * i : 4 * i + 8, 16 * j : 16 * j + 32, i, j]
    r2 = r2.reshape(4, 8, C1, 3, C2)
    g2 = 0.0
    for j in range(3):
        g2 = g2 + r2[:, 2 * j : 2 * j + 4, :, j]
    r3 = r3.reshape(3, 6, C2, 4, C3)
    g3 = 0.0
    for j in range(4):
        g3 = g3 + r3[:, j : j + 3, :, j]
    return g1, g2, g3


def on_device(
    frames,
    actions,
    rewards,
    old_values,
    next_values,
    terminal,
    truncated,
    behavior_logprob,
    master,
    first_moment,
    second_moment,
    outer_momentum,
    step_count,
):
    lanes = lax.axis_size("dp")
    place = lax.axis_index("dp")
    shard_len = master.shape[0]
    rows = shard_len // HID
    gathered = lax.all_gather(master.reshape(rows, HID).astype(BF16), "dp", axis=0)
    gathered = gathered.reshape(lanes * rows, HID)

    advantage = trajectory_advantages(
        rewards[0], old_values[0], next_values[0], terminal[0], truncated[0]
    )
    envs_here, steps_here = advantage.shape
    batch = envs_here * steps_here
    total_frames = batch * lanes
    first_sum, square_sum = lax.psum((jnp.sum(advantage), jnp.sum(advantage * advantage)), "dp")
    mean = first_sum / total_frames
    spread = square_sum / total_frames - mean * mean
    normed = ((advantage - mean) * lax.rsqrt(spread + 1e-05)).reshape(1, batch)
    returns = (advantage + old_values[0]).reshape(1, batch)

    column = lax.broadcasted_iota(jnp.int32, (1, HID), 1)
    late = column >= PHASE
    conv_flat = gathered[: TOP + 1].reshape(-1)
    offset = 0
    pieces = []
    for shape in ((8, 8, 4, C1), (C1,), (4, 4, C1, C2), (C2,), (3, 3, C2, C3), (C3,)):
        length = math.prod(shape)
        pieces.append(conv_flat[offset : offset + length].reshape(shape))
        offset += length
    w_one, b_one, w_two, b_two, w_three, b_three = pieces
    w_dense = jnp.where(
        late, gathered[TOP : TOP + FEATURES], gathered[TOP + 1 : TOP + 1 + FEATURES]
    )
    b_dense = jnp.where(
        late[0], gathered[TOP + FEATURES], gathered[TOP + 1 + FEATURES]
    ).astype(F32)
    tail = TOP + FEATURES + 1
    head_flat = gathered[tail:].reshape(-1)[PHASE : PHASE + HEAD_LEN]
    w_head = head_flat[: HID * (ACTIONS + 1)].reshape(HID, ACTIONS + 1)
    w_head = jnp.pad(jnp.roll(w_head, PHASE, axis=0).T, ((0, 13), (0, 0)))
    b_head = jnp.pad(head_flat[HID * (ACTIONS + 1) :], (0, 13)).astype(F32)

    x = frames[0].transpose(0, 2, 3, 1)
    t1, t2, t3 = forward_weights(w_one, w_two, w_three)

    def spread_bias(bias, count):
        bias = jnp.tile(bias.astype(F32), count)
        return jnp.broadcast_to(bias[:, None], (bias.shape[0], 256))

    a1, a2, a3 = conv_forward(
        x, t1, spread_bias(b_one, 8), t2, spread_bias(b_two, 3), t3, spread_bias(b_three, 7)
    )
    g_dense, d_c3, g_dense_bias, g_head, g_head_bias, loss_local = dense_step(
        1.0 / total_frames,
        a3.reshape(FEATURES, batch),
        w_dense,
        b_dense[:, None],
        w_head,
        b_head[:, None],
        normed,
        returns,
        actions[0].reshape(1, batch),
        behavior_logprob[0].reshape(1, batch),
    )
    total_rows = lanes * rows
    extended = jnp.concatenate([g_dense, g_dense_bias.reshape(1, HID)], axis=0)
    spare = total_rows - TOP - FEATURES - 1
    dense_rows = jnp.where(
        late,
        jnp.pad(extended, ((TOP, spare), (0, 0))),
        jnp.pad(extended, ((TOP + 1, spare - 1), (0, 0))),
    )
    dense_owned = lax.psum_scatter(
        dense_rows.reshape(lanes, rows, HID), "dp", scatter_dimension=0, tiled=False
    )

    back3, back2 = backward_weights(w_two, w_three)
    r1, r2, r3, s1, s2, s3 = conv_backward(x, a1, a2, d_c3.reshape(7, 7, C3, batch), back3, back2)
    g1, g2, g3 = conv_gradients(r1, r2, r3)
    small = jnp.concatenate(
        [
            g1.reshape(-1),
            jnp.sum(s1, axis=1),
            g2.reshape(-1),
            jnp.sum(s2, axis=1),
            g3.reshape(-1),
            jnp.sum(s3, axis=1),
            jnp.roll(g_head[: ACTIONS + 1].T, -PHASE, axis=0).reshape(-1),
            g_head_bias[: ACTIONS + 1, 0],
            loss_local.reshape(-1),
        ]
    )
    small = lax.psum(small, "dp")
    loss_total = small[CONV_LEN + HEAD_LEN]
    top_blocks = -(-(TOP + 1) // rows)
    top_part = jnp.pad(small[:CONV_LEN], (0, top_blocks * shard_len - CONV_LEN))
    tail_start = tail * HID + PHASE
    tail_block = tail_start // shard_len
    tail_part = jnp.pad(
        small[CONV_LEN : CONV_LEN + HEAD_LEN],
        (
            tail_start - tail_block * shard_len,
            lanes * shard_len - tail_start - HEAD_LEN,
        ),
    )

    def own_block(part, first):
        blocks = part.shape[0] // shard_len
        here = (place >= first) & (place < first + blocks)
        start = jnp.clip(place - first, 0, blocks - 1) * shard_len
        return jnp.where(here, lax.dynamic_slice_in_dim(part, start, shard_len, 0), 0.0)

    owned = dense_owned.reshape(-1) + own_block(top_part, 0) + own_block(tail_part, tail_block)
    norm = jnp.sqrt(lax.psum(jnp.sum(owned * owned), "dp"))
    factor = jnp.minimum(1.0, CLIP_NORM / (norm + 1e-06))
    clipped = owned * factor
    moment_step = step_count[0].astype(F32)
    first_next = BETA_ONE * first_moment[0] + (1.0 - BETA_ONE) * clipped
    second_next = BETA_TWO * second_moment[0] + (1.0 - BETA_TWO) * clipped * clipped
    first_hat = first_next / (1.0 - jnp.power(BETA_ONE, moment_step))
    second_hat = second_next / (1.0 - jnp.power(BETA_TWO, moment_step))
    inner = master - LEARN_RATE * (
        first_hat / (jnp.sqrt(second_hat) + ADAM_EPSILON) + WEIGHT_DECAY * master
    )
    moved = lax.psum(master - inner, "group") / lax.axis_size("group")
    momentum_next = OUTER_MOMENTUM * outer_momentum + moved
    final = master - OUTER_RATE * (moved + OUTER_MOMENTUM * momentum_next)
    return (
        clipped[None],
        norm.reshape(1),
        loss_total.reshape(1),
        first_next[None],
        second_next[None],
        moved,
        momentum_next,
        final,
        final.astype(BF16),
    )


def solution(mesh):
    return jax.shard_map(
        on_device,
        mesh=mesh,
        in_specs=(
            P("group", "dp", None, None, None),
            P("group", "dp", None),
            P("group", "dp", None),
            P("group", "dp", None),
            P("group", "dp", None),
            P("group", "dp", None),
            P("group", "dp", None),
            P("group", "dp", None),
            P("dp"),
            P("group", "dp"),
            P("group", "dp"),
            P("dp"),
            P(),
        ),
        out_specs=(
            P("group", "dp"),
            P("group"),
            P("group"),
            P("group", "dp"),
            P("group", "dp"),
            P("dp"),
            P("dp"),
            P("dp"),
            P("dp"),
        ),
        check_vma=False,
    )
```

```python
import math

import jax
import jax.numpy as jnp
from jax import lax
from jax.experimental import pallas as pl
from jax.experimental.pallas import tpu as pltpu
from jax.sharding import PartitionSpec as P

C1 = 32
C2 = 64
C3 = 64
HID = 512
ACTIONS = 18
PARAMS = 1693875
FEATURES = 49 * C3
CONV_LEN = 256 * C1 + C1 + 16 * C1 * C2 + C2 + 9 * C2 * C3 + C3
TOP = CONV_LEN // HID
LEAD = (TOP + 8) // 8 * 8
BLOCK_ROWS = LEAD + 8
PHASE = CONV_LEN % HID
HEAD_LEN = HID * (ACTIONS + 1) + ACTIONS + 1

BETA_ONE = 0.9
BETA_TWO = 0.999
ADAM_EPSILON = 1e-08
LEARN_RATE = 0.005
WEIGHT_DECAY = 0.01
CLIP_NORM = 0.5
OUTER_RATE = 0.7
OUTER_MOMENTUM = 0.9
DISCOUNT = 0.99
TRACE_DECAY = 0.95
RATIO_CLIP = 0.1
VALUE_COEF = 0.5
ENTROPY_COEF = 0.01

F32 = jnp.float32
BF16 = jnp.bfloat16
VMEM_LIMIT = 63 * 1024 * 1024


def mm(a, b):
    return jnp.dot(a, b, preferred_element_type=F32)


def mm_nt(a, b):
    return lax.dot_general(a, b, (((1,), (1,)), ((), ())), preferred_element_type=F32)


def mm_tn(a, b):
    return lax.dot_general(a, b, (((0,), (0,)), ((), ())), preferred_element_type=F32)


def trajectory_advantages(rewards, values, next_values, terminal, truncated):
    alive = 1.0 - terminal.astype(F32)
    cutoff = truncated.astype(F32)
    following = jnp.concatenate([values[:, 1:], next_values[:, -1:]], axis=1)
    following = cutoff * next_values + (1.0 - cutoff) * following
    deltas = rewards + DISCOUNT * alive * following - values
    keeping = DISCOUNT * TRACE_DECAY * alive * (1.0 - cutoff)

    def backward_step(carry, item):
        delta, keep = item
        result = delta + keep * carry
        return (result, result)

    start = jnp.zeros((rewards.shape[0],), F32)
    _, series = lax.scan(backward_step, start, (deltas.T, keeping.T), reverse=True)
    return series.T


def unfold(block, phase, width, rows):
    lane = lax.broadcasted_iota(jnp.int32, (1, HID), 1)
    if phase:
        turned = pltpu.roll(block, HID - phase, 1)
        block = jnp.where(lane < HID - phase, turned[:rows], turned[1 : rows + 1])
    pieces = []
    for k in range(HID // width):
        start = k * width // 128 * 128
        piece = block[:rows, start : start + 128]
        turn = k * width % 128
        pieces.append(pltpu.roll(piece, 128 - turn, 1) if turn else piece)
    return pieces


def weights_body(
    conv_ref,
    t1_ref,
    b1_ref,
    t2_ref,
    b2_ref,
    t3_ref,
    b3_ref,
    back3_ref,
    back2_ref,
    wide_ref,
    w1_ref,
    w2_ref,
    w3_ref,
):
    wide_ref[...] = conv_ref[...].astype(F32)
    for k, piece in enumerate(unfold(wide_ref[0:24], 0, C1, 24)):
        w1_ref[pl.ds(k, 24, stride=16), :] = piece
    for k, piece in enumerate(unfold(wide_ref[16:96], 32, C2, 72)):
        w2_ref[pl.ds(k, 72, stride=8), :] = piece
    for k, piece in enumerate(unfold(wide_ref[80:168], 96, C3, 80)):
        w3_ref[pl.ds(k, 80, stride=8), :] = piece
    w1 = w1_ref[...].T
    w2 = w2_ref[...].T
    w3 = w3_ref[...].T
    w1_low = w1.astype(BF16)
    w2_low = w2.astype(BF16)
    w3_low = w3.astype(BF16)
    for ref in (t1_ref, t2_ref, t3_ref, back3_ref, back2_ref):
        ref[...] = jnp.zeros(ref.shape, BF16)
    for p in range(2):
        for q in range(4):
            d = 4 * p + q
            for i in range(8):
                lane = (i + 4 * p) * 80 + 16 * q
                t1_ref[32 * d : 32 * d + 32, lane : lane + 32] = w1_low[0:32, 32 * i : 32 * i + 32]
            b1_ref[32 * d : 32 * d + 32] = jnp.broadcast_to(w1[0:32, 256:257], (32, 256))
    for q in range(3):
        for i in range(4):
            lane = 256 * i + 64 * q
            t2_ref[64 * q : 64 * q + 64, lane : lane + 128] = w2_low[0:64, 128 * i : 128 * i + 128]
        b2_ref[64 * q : 64 * q + 64] = jnp.broadcast_to(w2[0:64, 512:513], (64, 256))
    for q in range(7):
        for i in range(3):
            lane = 576 * i + 64 * q
            t3_ref[64 * q : 64 * q + 64, lane : lane + 192] = w3_low[0:64, 192 * i : 192 * i + 192]
        b3_ref[64 * q : 64 * q + 64] = jnp.broadcast_to(w3[0:64, 576:577], (64, 256))
    for x in range(9):
        for r in range(3):
            for q in range(max(0, x - 2), min(6, x) + 1):
                k = ((2 - r) * 3 + x - q) * 64
                lane = 512 * r + 64 * q
                back3_ref[64 * x : 64 * x + 64, lane : lane + 64] = w3_ref[k : k + 64, 0:64].astype(
                    BF16
                )
    for y in range(2):
        for x in range(4):
            for r in range(2):
                for q in range(3):
                    j = x + 2 - 2 * q
                    if 0 <= j < 4:
                        k = ((y + 2 - 2 * r) * 4 + j) * 32
                        row = 32 * (4 * y + x)
                        lane = 64 * (3 * r + q)
                        back2_ref[row : row + 32, lane : lane + 64] = w2_ref[
                            k : k + 32, 0:64
                        ].astype(BF16)


def conv_weights(block):
    shapes = [
        ((256, 960), BF16),
        ((256, 256), F32),
        ((192, 1024), BF16),
        ((192, 256), F32),
        ((448, 1728), BF16),
        ((448, 256), F32),
        ((576, 1536), BF16),
        ((256, 384), BF16),
    ]
    return pl.pallas_call(
        weights_body,
        out_shape=[jax.ShapeDtypeStruct(shape, kind) for shape, kind in shapes],
        scratch_shapes=[
            pltpu.VMEM((BLOCK_ROWS, HID), F32),
            pltpu.VMEM((384, 128), F32),
            pltpu.VMEM((640, 128), F32),
            pltpu.VMEM((640, 128), F32),
        ],
        compiler_params=pltpu.CompilerParams(vmem_limit_bytes=VMEM_LIMIT),
        name="conv_weights",
    )(block)


def pixel_window(x_refs, first, n):
    sides = []
    for e in range(2):
        parts = [x_refs[first + k][e, :, 64 * n : 64 * n + 80, :] for k in range(3)]
        sides.append(jnp.concatenate(parts, axis=0).reshape(960, 128))
    return jnp.concatenate(sides, axis=1)


def forward_body(
    x0, x1, x2, x3, x4, t1_ref, b1_ref, t2_ref, b2_ref, t3_ref, b3_ref, a1_ref, a2_ref, a3_ref
):
    x_refs = (x0, x1, x2, x3, x4)
    t = pl.program_id(1)
    for h in range(2):
        for n in range(5):
            window = pixel_window(x_refs, 2 * h, n)
            out = jnp.maximum(mm(t1_ref[...], window) + b1_ref[...], 0.0).astype(BF16)
            a1_ref[pl.ds(4 * t + 2 * h, 2), 4 * n : 4 * n + 4] = out.reshape(2, 4, C1, 256)

    @pl.when(t == 4)
    def _():
        def conv_two(p, carry):
            for g in range(3):
                window = a1_ref[pl.ds(2 * p, 4), 6 * g : 6 * g + 8].reshape(1024, 256)
                out = jnp.maximum(mm(t2_ref[...], window) + b2_ref[...], 0.0).astype(BF16)
                a2_ref[p, 3 * g : 3 * g + 3] = out.reshape(3, C2, 256)
            a2_ref[p, 9] = jnp.zeros((C2, 256), BF16)
            return carry

        lax.fori_loop(0, 9, conv_two, 0)

        def conv_three(p, carry):
            window = a2_ref[pl.ds(p, 3), 0:9].reshape(1728, 256)
            out = jnp.maximum(mm(t3_ref[...], window) + b3_ref[...], 0.0).astype(BF16)
            a3_ref[p] = out.reshape(7, C3, 256)
            return carry

        lax.fori_loop(0, 7, conv_three, 0)


def whole(shape):
    return pl.BlockSpec(shape, lambda *j: (0,) * len(shape), pipeline_mode=pl.Buffered(1))


def pixel_specs():
    def spec(k):
        return pl.BlockSpec((2, 4, 336, 128), lambda j, t: (j, 4 * t + k, 0, 0))

    return [spec(k) for k in range(5)]


def conv_forward(x, t1, b1, t2, b2, t3, b3):
    envs = x.shape[0]
    frames = envs * 128
    return pl.pallas_call(
        forward_body,
        grid=(envs // 2, 5),
        in_specs=pixel_specs()
        + [
            whole((256, 960)),
            whole((256, 256)),
            whole((192, 1024)),
            whole((192, 256)),
            whole((448, 1728)),
            whole((448, 256)),
        ],
        out_specs=[
            pl.BlockSpec((20, 20, C1, 256), lambda j, t: (0, 0, 0, j)),
            pl.BlockSpec((9, 10, C2, 256), lambda j, t: (0, 0, 0, j)),
            pl.BlockSpec((7, 7, C3, 256), lambda j, t: (0, 0, 0, j)),
        ],
        out_shape=[
            jax.ShapeDtypeStruct((20, 20, C1, frames), BF16),
            jax.ShapeDtypeStruct((9, 10, C2, frames), BF16),
            jax.ShapeDtypeStruct((7, 7, C3, frames), BF16),
        ],
        compiler_params=pltpu.CompilerParams(vmem_limit_bytes=VMEM_LIMIT),
        name="conv_forward",
    )(x, x, x, x, x, t1, b1, t2, b2, t3, b3)


def dense_body(
    scale,
    a3_ref,
    wd_ref,
    bd_ref,
    wh_ref,
    bh_ref,
    normed_ref,
    returns_ref,
    actions_ref,
    behavior_ref,
    packed_ref,
    dc3_ref,
    gwh_ref,
    gbh_ref,
    loss_ref,
    wide_ref,
):
    hidden_pre = mm_tn(wd_ref[...], a3_ref[...]) + bd_ref[...]
    hidden = jnp.maximum(hidden_pre, 0.0).astype(BF16)
    out = mm(wh_ref[...], hidden) + bh_ref[...]
    row = lax.broadcasted_iota(jnp.int32, out.shape, 0)
    is_logit = row < ACTIONS
    logits = jnp.where(is_logit, out, -jnp.inf)
    top = jnp.max(logits, axis=0, keepdims=True)
    shifted = out - top
    exps = jnp.where(is_logit, jnp.exp(shifted), 0.0)
    total = jnp.sum(exps, axis=0, keepdims=True)
    log_probs = jnp.where(is_logit, shifted - jnp.log(total), 0.0)
    probs = jnp.where(is_logit, jnp.exp(log_probs), 0.0)
    value = jnp.sum(jnp.where(row == ACTIONS, out, 0.0), axis=0, keepdims=True)
    normed = normed_ref[...]
    chosen = row == actions_ref[...]
    taken = jnp.sum(jnp.where(chosen, log_probs, 0.0), axis=0, keepdims=True)
    ratio = jnp.exp(taken - behavior_ref[...])
    low = 1.0 - RATIO_CLIP
    high = 1.0 + RATIO_CLIP
    clipped = jnp.clip(ratio, low, high)
    plain = ratio * normed
    cut = clipped * normed
    entropy = -jnp.sum(probs * log_probs, axis=0, keepdims=True)
    error = value - returns_ref[...]
    losses = -jnp.minimum(plain, cut) + 0.5 * VALUE_COEF * error * error - ENTROPY_COEF * entropy
    loss_ref[...] = jnp.sum(losses, axis=1, keepdims=True) * scale
    plain_share = jnp.where(plain < cut, 1.0, jnp.where(plain == cut, 0.5, 0.0))
    inside = jnp.where(
        (ratio > low) & (ratio < high), 1.0, jnp.where((ratio == low) | (ratio == high), 0.5, 0.0)
    )
    d_taken = -scale * normed * ratio * (plain_share + (1.0 - plain_share) * inside)
    d_logits = d_taken * (jnp.where(chosen, 1.0, 0.0) - probs) + (scale * ENTROPY_COEF) * probs * (
        log_probs + entropy
    )
    d_value = scale * VALUE_COEF * error
    d_out = jnp.where(is_logit, d_logits, jnp.where(row == ACTIONS, d_value, 0.0)).astype(BF16)
    gwh_ref[...] = mm_nt(d_out, hidden)
    gbh_ref[...] = jnp.sum(d_out.astype(F32), axis=1, keepdims=True)
    back = mm_tn(wh_ref[...], d_out)
    d_hidden = jnp.where(hidden_pre > 0, back, 0.0).astype(BF16)
    last = LEAD + FEATURES
    wide_ref[0:LEAD] = jnp.zeros((LEAD, HID), F32)
    wide_ref[LEAD:last] = mm_nt(a3_ref[...], d_hidden)
    wide_ref[last:] = jnp.zeros((wide_ref.shape[0] - last, HID), F32)
    ones = jnp.ones((8, d_hidden.shape[1]), BF16)
    wide_ref[last : last + 1] = mm_nt(ones, d_hidden)[0:1]
    late = lax.broadcasted_iota(jnp.int32, (1, HID), 1) >= PHASE
    shards, rows, _ = packed_ref.shape
    for k in range(shards):
        first = rows * k + LEAD - TOP - 1
        packed_ref[k] = jnp.where(
            late, wide_ref[first + 1 : first + 1 + rows], wide_ref[first : first + rows]
        )
    d_a3 = mm(wd_ref[...], d_hidden)
    dc3_ref[...] = jnp.where(a3_ref[...] > 0, d_a3, 0.0).astype(BF16)


def dense_step(scale, shards, shard_rows, a3, wd, bd, wh, bh, normed, returns, actions, behavior):
    frames = a3.shape[1]
    rows = wh.shape[0]
    return pl.pallas_call(
        lambda *refs: dense_body(scale, *refs),
        out_shape=[
            jax.ShapeDtypeStruct((shards, shard_rows, HID), F32),
            jax.ShapeDtypeStruct((FEATURES, frames), BF16),
            jax.ShapeDtypeStruct((rows, HID), F32),
            jax.ShapeDtypeStruct((rows, 1), F32),
            jax.ShapeDtypeStruct((1, 1), F32),
        ],
        scratch_shapes=[
            pltpu.VMEM((max(shards * shard_rows, TOP + 1 + FEATURES) + 2 * LEAD - TOP, HID), F32)
        ],
        compiler_params=pltpu.CompilerParams(vmem_limit_bytes=VMEM_LIMIT),
        name="dense_step",
    )(a3, wd, bd, wh, bh, normed, returns, actions, behavior)


def fold(g_ref, width, rows):
    step = HID // width
    lane = lax.broadcasted_iota(jnp.int32, (1, 128), 1)
    columns = []
    for m in range(4):
        total = 0.0
        for t in range(128 // width):
            piece = g_ref[pl.ds(m * 128 // width + t, rows, stride=step), :]
            piece = jnp.where(lane < width, piece, 0.0)
            total = total + (pltpu.roll(piece, width * t, 1) if t else piece)
        columns.append(total)
    return jnp.concatenate(columns, axis=1)


def upper_body(
    a1_hbm,
    a2_ref,
    dc3_ref,
    t3_ref,
    d2_ref,
    packed_ref,
    r2_ref,
    r3_ref,
    s2_ref,
    s3_ref,
    a1_ref,
    d3_ref,
    g2_ref,
    g3_ref,
    sems,
):
    step = pl.program_id(0)
    lanes = pl.ds(pl.multiple_of(256 * step, 256), 256)
    load_a1 = pltpu.make_async_copy(a1_hbm.at[:, :, :, lanes], a1_ref, sems.at[0])
    load_a1.start()

    @pl.when(step == 0)
    def _():
        for ref in (r2_ref, r3_ref, s2_ref, s3_ref):
            ref[...] = jnp.zeros(ref.shape, F32)
        for p in (0, 1, 9, 10):
            d3_ref[p] = jnp.zeros((8, C3, 256), BF16)

    for p in (0, 10):
        d2_ref[p] = jnp.zeros((11, C2, 256), BF16)

    def edge(p, carry):
        d2_ref[p, 0] = jnp.zeros((C2, 256), BF16)
        d2_ref[p, 10] = jnp.zeros((C2, 256), BF16)
        return carry

    lax.fori_loop(1, 10, edge, 0)

    def fill(p, carry):
        d3_ref[p + 2, 0:7] = dc3_ref[p]
        d3_ref[p + 2, 7] = jnp.zeros((C3, 256), BF16)
        s3_ref[...] += jnp.sum(dc3_ref[p].astype(F32), axis=0)
        return carry

    lax.fori_loop(0, 7, fill, 0)

    def three_weights(p, carry):
        left = mm_nt(a2_ref[pl.ds(p, 3), 0:6].reshape(1152, 256), d3_ref[p + 2, 0:4].reshape(256, 256))
        right = mm_nt(
            a2_ref[pl.ds(p, 3), 4:10].reshape(1152, 256), d3_ref[p + 2, 4:8].reshape(256, 256)
        )
        r3_ref[...] += left + right
        return carry

    lax.fori_loop(0, 7, three_weights, 0)

    def three_input(y, carry):
        back = mm(t3_ref[...], d3_ref[pl.ds(y, 3)].reshape(1536, 256)).reshape(9, C2, 256)
        masked = jnp.where(a2_ref[y, 0:9] > 0, back, 0.0).astype(BF16)
        d2_ref[y + 1, 1:10] = masked
        s2_ref[...] += jnp.sum(masked.astype(F32), axis=0)
        return carry

    lax.fori_loop(0, 9, three_input, 0)
    load_a1.wait()

    def two_weights(p, carry):
        total = 0.0
        for g in range(3):
            total = total + mm_nt(
                a1_ref[pl.ds(2 * p, 4), 6 * g : 6 * g + 8].reshape(1024, 256),
                d2_ref[p + 1, 1 + 3 * g : 4 + 3 * g].reshape(192, 256),
            )
        r2_ref[:, 0:192] += total
        return carry

    lax.fori_loop(0, 9, two_weights, 0)

    @pl.when(step == pl.num_programs(0) - 1)
    def _():
        g2_ref[...] = jnp.zeros(g2_ref.shape, F32)
        g3_ref[...] = jnp.zeros(g3_ref.shape, F32)
        for i in range(4):
            k = 256 * i
            total = r2_ref[k : k + 128, 0:128]
            total = total + pltpu.roll(r2_ref[k + 64 : k + 192, 0:128], 64, 1)
            g2_ref[128 * i : 128 * i + 128] = total + r2_ref[k + 128 : k + 256, 128:256]
        for i in range(3):
            k = 384 * i
            total = r3_ref[k : k + 192, 0:128]
            total = total + pltpu.roll(r3_ref[k + 64 : k + 256, 0:128], 64, 1)
            total = total + r3_ref[k + 128 : k + 320, 128:256]
            total = total + pltpu.roll(r3_ref[k + 192 : k + 384, 128:256], 64, 1)
            g3_ref[192 * i : 192 * i + 192] = total
        g2_ref[512:513, 0:64] = jnp.sum(s2_ref[...].T, axis=0, keepdims=True)
        g3_ref[576:577, 0:64] = jnp.sum(s3_ref[...].T, axis=0, keepdims=True)
        lane = lax.broadcasted_iota(jnp.int32, (1, HID), 1)
        packed_ref[...] = jnp.zeros(packed_ref.shape, F32)
        for ref, rows, base, phase in ((g2_ref, 72, 16, 32), (g3_ref, 80, 80, 96)):
            turned = pltpu.roll(fold(ref, 64, rows), phase, 1)
            packed_ref[base : base + rows] += jnp.where(lane >= phase, turned, 0.0)
            packed_ref[base + 1 : base + 1 + rows] += jnp.where(lane < phase, turned, 0.0)


def upper_backward(a1, a2, dc3, t3):
    frames = a1.shape[3]
    return pl.pallas_call(
        upper_body,
        grid=(frames // 256,),
        in_specs=[
            pl.BlockSpec(memory_space=pl.ANY),
            pl.BlockSpec((9, 10, C2, 256), lambda j: (0, 0, 0, j)),
            pl.BlockSpec((7, 7, C3, 256), lambda j: (0, 0, 0, j)),
            whole((576, 1536)),
        ],
        out_specs=[
            pl.BlockSpec((11, 11, C2, 256), lambda j: (0, 0, 0, j)),
            whole((BLOCK_ROWS, HID)),
        ],
        out_shape=[
            jax.ShapeDtypeStruct((11, 11, C2, frames), BF16),
            jax.ShapeDtypeStruct((BLOCK_ROWS, HID), F32),
        ],
        scratch_shapes=[
            pltpu.VMEM((1024, 256), F32),
            pltpu.VMEM((1152, 256), F32),
            pltpu.VMEM((C2, 256), F32),
            pltpu.VMEM((C3, 256), F32),
            pltpu.VMEM((20, 20, C1, 256), BF16),
            pltpu.VMEM((11, 8, C3, 256), BF16),
            pltpu.VMEM((640, 128), F32),
            pltpu.VMEM((640, 128), F32),
            pltpu.SemaphoreType.DMA((1,)),
        ],
        compiler_params=pltpu.CompilerParams(vmem_limit_bytes=VMEM_LIMIT),
        name="upper_backward",
    )(a1, a2, dc3, t3)


def lower_body(x0, x1, x2, x3, x4, a1_ref, d2_ref, t2_ref, packed_ref, r1_ref, s1_ref, g1_ref):
    x_refs = (x0, x1, x2, x3, x4)
    t = pl.program_id(1)

    @pl.when((pl.program_id(0) == 0) & (t == 0))
    def _():
        r1_ref[...] = jnp.zeros(r1_ref.shape, F32)
        s1_ref[...] = jnp.zeros(s1_ref.shape, F32)

    total = 0.0
    sums = jnp.zeros((C1, 256), F32)
    for h in range(2):
        for n in range(5):
            back = mm(
                t2_ref[...],
                d2_ref[pl.ds(2 * t + h, 2), 2 * n : 2 * n + 3].reshape(384, 256),
            )
            kept = a1_ref[2 * h : 2 * h + 2, 4 * n : 4 * n + 4].reshape(256, 256) > 0
            masked = jnp.where(kept, back, 0.0).astype(BF16)
            sums = sums + jnp.sum(masked.astype(F32).reshape(8, C1, 256), axis=0)
            total = total + mm_nt(pixel_window(x_refs, 2 * h, n), masked)
    r1_ref[...] += total
    s1_ref[...] += sums

    @pl.when((pl.program_id(0) == pl.num_programs(0) - 1) & (t == 4))
    def _():
        g1_ref[...] = jnp.zeros(g1_ref.shape, F32)
        for i in range(8):
            total = 0.0
            for p in range(2):
                for q in range(4):
                    k = (i + 4 * p) * 80 + 16 * q
                    slab = r1_ref[k : k + 32, 128 * p : 128 * p + 128]
                    total = total + (pltpu.roll(slab, 128 - 32 * q, 1) if q else slab)
            g1_ref[32 * i : 32 * i + 32] = total
        g1_ref[256:257, 0:32] = jnp.sum(s1_ref[...].T, axis=0, keepdims=True)
        packed_ref[...] = fold(g1_ref, 32, 24)


def lower_backward(x, a1, d2, t2):
    envs = x.shape[0]
    return pl.pallas_call(
        lower_body,
        grid=(envs // 2, 5),
        in_specs=pixel_specs()
        + [
            pl.BlockSpec((4, 20, C1, 256), lambda j, t: (t, 0, 0, j)),
            pl.BlockSpec((11, 11, C2, 256), lambda j, t: (0, 0, 0, j)),
            whole((256, 384)),
        ],
        out_specs=whole((24, HID)),
        out_shape=jax.ShapeDtypeStruct((24, HID), F32),
        scratch_shapes=[
            pltpu.VMEM((960, 256), F32),
            pltpu.VMEM((C1, 256), F32),
            pltpu.VMEM((384, 128), F32),
        ],
        compiler_params=pltpu.CompilerParams(vmem_limit_bytes=VMEM_LIMIT),
        name="lower_backward",
    )(x, x, x, x, x, a1, d2, t2)


def swap(value, lanes, step):
    return lax.ppermute(value, "dp", [(i, i ^ step) for i in range(lanes)])


def halving_order(lanes):
    return [1 << k for k in range(lanes.bit_length() - 1)]


def sum_everywhere(value, lanes):
    for step in halving_order(lanes):
        value = value + swap(value, lanes, step)
    return value


def scatter_sum(blocks, lanes, place):
    for step in halving_order(lanes):
        pairs = blocks.reshape((blocks.shape[0] // 2, 2) + blocks.shape[1:])
        high = (place // step) % 2 == 1
        kept = jnp.where(high, pairs[:, 1], pairs[:, 0])
        sent = jnp.where(high, pairs[:, 0], pairs[:, 1])
        blocks = kept + swap(sent, lanes, step)
    return blocks[0]


def gather_blocks(block, lanes, place):
    blocks = block[None]
    for step in reversed(halving_order(lanes)):
        other = swap(blocks, lanes, step)
        high = (place // step) % 2 == 1
        blocks = jnp.stack(
            [jnp.where(high, other, blocks), jnp.where(high, blocks, other)], axis=1
        ).reshape((2 * blocks.shape[0],) + blocks.shape[1:])
    return blocks


def first_rows_everywhere(local, lanes, place):
    rows = local.shape[0]
    owners = -(-(TOP + 1) // rows)
    if owners == 1:
        block = jnp.pad(local[: TOP + 1], ((0, BLOCK_ROWS - TOP - 1), (0, 0)))
        block = jnp.where(place == 0, block, jnp.zeros((), BF16))
        for step in reversed(halving_order(lanes)):
            pairs = [(i, i + step) for i in range(0, lanes, 2 * step)]
            block = block + lax.ppermute(block, "dp", pairs)
        return block
    block = jnp.zeros((owners, rows, HID), BF16)
    block = jnp.where(jnp.arange(owners)[:, None, None] == place, local[None], block)
    block = sum_everywhere(block, lanes).reshape(owners * rows, HID)[: TOP + 1]
    return jnp.pad(block, ((0, BLOCK_ROWS - TOP - 1), (0, 0)))


def on_device(
    frames,
    actions,
    rewards,
    old_values,
    next_values,
    terminal,
    truncated,
    behavior_logprob,
    master,
    first_moment,
    second_moment,
    outer_momentum,
    step_count,
):
    lanes = lax.axis_size("dp")
    place = lax.axis_index("dp")
    shard_len = master.shape[0]
    rows = shard_len // HID
    groups = lax.axis_size("group")
    assert groups == 2 and rows * HID == shard_len and frames.shape[2] == 128

    def other_group(value):
        return lax.ppermute(value, "group", [(0, 1), (1, 0)])

    master_rows = master.reshape(rows, HID)
    low_rows = master_rows.astype(BF16)
    block = first_rows_everywhere(low_rows, lanes, place)
    gathered = lax.all_gather(low_rows, "dp", axis=0).reshape(lanes * rows, HID)

    advantage = trajectory_advantages(
        rewards[0], old_values[0], next_values[0], terminal[0], truncated[0]
    )
    envs_here, steps_here = advantage.shape
    batch = envs_here * steps_here
    total_frames = batch * lanes
    sums = jnp.stack([jnp.sum(advantage), jnp.sum(advantage * advantage)])
    first_sum, square_sum = sum_everywhere(sums, lanes)
    mean = first_sum / total_frames
    spread = square_sum / total_frames - mean * mean
    normed = ((advantage - mean) * lax.rsqrt(spread + 1e-05)).reshape(1, batch)
    returns = (advantage + old_values[0]).reshape(1, batch)

    x = frames[0].transpose(0, 2, 3, 1)
    t1, b1, t2, b2, t3, b3, back3, back2 = conv_weights(block)
    a1, a2, a3 = conv_forward(x, t1, b1, t2, b2, t3, b3)

    column = lax.broadcasted_iota(jnp.int32, (1, HID), 1)
    late = column >= PHASE
    w_dense = jnp.where(
        late, gathered[TOP : TOP + FEATURES], gathered[TOP + 1 : TOP + 1 + FEATURES]
    )
    b_dense = jnp.where(
        late[0], gathered[TOP + FEATURES], gathered[TOP + 1 + FEATURES]
    ).astype(F32)
    tail = TOP + FEATURES + 1
    head_flat = gathered[tail:].reshape(-1)[PHASE : PHASE + HEAD_LEN]
    w_head = head_flat[: HID * (ACTIONS + 1)].reshape(HID, ACTIONS + 1)
    w_head = jnp.pad(jnp.roll(w_head, PHASE, axis=0).T, ((0, 13), (0, 0)))
    b_head = jnp.pad(head_flat[HID * (ACTIONS + 1) :], (0, 13)).astype(F32)
    packed_dense, d_c3, g_head, g_head_bias, loss_local = dense_step(
        1.0 / total_frames,
        lanes,
        rows,
        a3.reshape(FEATURES, batch),
        w_dense,
        b_dense[:, None],
        w_head,
        b_head[:, None],
        normed,
        returns,
        actions[0].reshape(1, batch),
        behavior_logprob[0].reshape(1, batch),
    )
    dense_owned = lax.psum_scatter(packed_dense, "dp", scatter_dimension=0, tiled=False)
    d2, upper = upper_backward(a1, a2, d_c3.reshape(7, 7, C3, batch), back3)
    lower = lower_backward(x, a1, d2, back2)

    tail_rows = lanes * rows - tail
    head_part = jnp.concatenate(
        [
            jnp.zeros((PHASE,), F32),
            jnp.roll(g_head[: ACTIONS + 1].T, -PHASE, axis=0).reshape(-1),
            g_head_bias[: ACTIONS + 1, 0],
            jnp.zeros((tail_rows * HID - PHASE - HEAD_LEN,), F32),
        ]
    ).reshape(tail_rows, HID)
    small = jnp.concatenate(
        [jnp.pad(lower, ((0, BLOCK_ROWS - 24), (0, 0))) + upper, head_part], axis=0
    )
    unit = lanes * 8 // math.gcd(lanes * 8, 4)
    count = -(-small.shape[0] // unit) * unit
    small = jnp.pad(small, ((0, count - small.shape[0]), (0, 0)))
    piece = scatter_sum(small.reshape(lanes, count * 4 // lanes, 128), lanes, place)
    squares = jnp.sum(dense_owned * dense_owned) + jnp.sum(piece * piece)
    facts = jnp.zeros((8, 128), F32).at[0, 0].set(squares).at[0, 1].set(loss_local[0, 0])
    message = jnp.concatenate([piece, facts], axis=0)
    message = jnp.stack([message, other_group(message)])
    messages = gather_blocks(message, lanes, place)
    own_facts = jnp.sum(messages[:, :, -8], axis=0)
    norm = jnp.sqrt(own_facts[:, 0])
    loss_total = own_facts[0, 1]
    smalls = messages[:, :, :-8].transpose(1, 0, 2, 3).reshape(2, count, HID)

    def own_rows(part, first_row):
        first = first_row // rows
        blocks = -(-(first_row + part.shape[1]) // rows) - first
        part = jnp.pad(
            part,
            (
                (0, 0),
                (first_row - first * rows, (first + blocks) * rows - first_row - part.shape[1]),
                (0, 0),
            ),
        )
        here = (place >= first) & (place < first + blocks)
        start = jnp.clip(place - first, 0, blocks - 1) * rows
        return jnp.where(here, lax.dynamic_slice_in_dim(part, start, rows, 1), 0.0)

    owned = jnp.stack([dense_owned, other_group(dense_owned)])
    owned = owned + own_rows(smalls[:, : TOP + 1], 0)
    owned = owned + own_rows(smalls[:, BLOCK_ROWS : BLOCK_ROWS + tail_rows], tail)
    firsts = jnp.stack([first_moment[0], other_group(first_moment[0])])
    seconds = jnp.stack([second_moment[0], other_group(second_moment[0])])
    factor = jnp.minimum(1.0, CLIP_NORM / (norm + 1e-06))
    clipped = owned.reshape(2, shard_len) * factor[:, None]
    moment_step = step_count[0].astype(F32)
    first_next = BETA_ONE * firsts + (1.0 - BETA_ONE) * clipped
    second_next = BETA_TWO * seconds + (1.0 - BETA_TWO) * clipped * clipped
    first_hat = first_next / (1.0 - jnp.power(BETA_ONE, moment_step))
    second_hat = second_next / (1.0 - jnp.power(BETA_TWO, moment_step))
    inner = master - LEARN_RATE * (
        first_hat / (jnp.sqrt(second_hat) + ADAM_EPSILON) + WEIGHT_DECAY * master
    )
    drift = master - inner
    moved = (drift[0] + drift[1]) / groups
    momentum_next = OUTER_MOMENTUM * outer_momentum + moved
    final = master - OUTER_RATE * (moved + OUTER_MOMENTUM * momentum_next)
    return (
        clipped[:1],
        norm[:1],
        loss_total.reshape(1),
        first_next[:1],
        second_next[:1],
        moved,
        momentum_next,
        final,
        final.astype(BF16),
    )


def solution(mesh):
    return jax.shard_map(
        on_device,
        mesh=mesh,
        in_specs=(
            P("group", "dp", None, None, None),
            P("group", "dp", None),
            P("group", "dp", None),
            P("group", "dp", None),
            P("group", "dp", None),
            P("group", "dp", None),
            P("group", "dp", None),
            P("group", "dp", None),
            P("dp"),
            P("group", "dp"),
            P("group", "dp"),
            P("dp"),
            P(),
        ),
        out_specs=(
            P("group", "dp"),
            P("group"),
            P("group"),
            P("group", "dp"),
            P("group", "dp"),
            P("dp"),
            P("dp"),
            P("dp"),
            P("dp"),
        ),
        check_vma=False,
    )
```

```python
import math

import jax
import jax.numpy as jnp
from jax import lax
from jax.experimental import pallas as pl
from jax.experimental.pallas import tpu as pltpu
from jax.sharding import PartitionSpec as P

C1 = 32
C2 = 64
C3 = 64
HID = 512
ACTIONS = 18
PARAMS = 1693875
FEATURES = 49 * C3
CONV_LEN = 256 * C1 + C1 + 16 * C1 * C2 + C2 + 9 * C2 * C3 + C3
TOP = CONV_LEN // HID
LEAD = (TOP + 8) // 8 * 8
BLOCK_ROWS = LEAD + 8
PHASE = CONV_LEN % HID
HEAD_LEN = HID * (ACTIONS + 1) + ACTIONS + 1

BETA_ONE = 0.9
BETA_TWO = 0.999
ADAM_EPSILON = 1e-08
LEARN_RATE = 0.005
WEIGHT_DECAY = 0.01
CLIP_NORM = 0.5
OUTER_RATE = 0.7
OUTER_MOMENTUM = 0.9
DISCOUNT = 0.99
TRACE_DECAY = 0.95
RATIO_CLIP = 0.1
VALUE_COEF = 0.5
ENTROPY_COEF = 0.01

F32 = jnp.float32
BF16 = jnp.bfloat16
VMEM_LIMIT = 63 * 1024 * 1024


def mm(a, b):
    return jnp.dot(a, b, preferred_element_type=F32)


def mm_nt(a, b):
    return lax.dot_general(a, b, (((1,), (1,)), ((), ())), preferred_element_type=F32)


def mm_tn(a, b):
    return lax.dot_general(a, b, (((0,), (0,)), ((), ())), preferred_element_type=F32)


def advantage_body(rewards_ref, values_ref, next_ref, terminal_ref, truncated_ref, out_ref, sums_ref):
    values = values_ref[...]
    steps = values.shape[1]
    lane = lax.broadcasted_iota(jnp.int32, values.shape, 1)
    alive = 1.0 - terminal_ref[...].astype(F32)
    cutoff = truncated_ref[...].astype(F32)
    following = jnp.where(lane < steps - 1, pltpu.roll(values, steps - 1, 1), next_ref[...])
    following = cutoff * next_ref[...] + (1.0 - cutoff) * following
    series = rewards_ref[...] + DISCOUNT * alive * following - values
    keeping = DISCOUNT * TRACE_DECAY * alive * (1.0 - cutoff)
    step = 1
    while step < steps:
        inside = lane < steps - step
        series = series + keeping * jnp.where(inside, pltpu.roll(series, steps - step, 1), 0.0)
        keeping = keeping * jnp.where(inside, pltpu.roll(keeping, steps - step, 1), 0.0)
        step *= 2
    out_ref[...] = series
    first = jnp.sum(jnp.sum(series, axis=0, keepdims=True), axis=1, keepdims=True)
    square = jnp.sum(jnp.sum(series * series, axis=0, keepdims=True), axis=1, keepdims=True)
    place = lax.broadcasted_iota(jnp.int32, (8, 128), 0)
    sums_ref[...] = jnp.where(place == 0, first, square)


def trajectory_advantages(rewards, values, next_values, terminal, truncated):
    return pl.pallas_call(
        advantage_body,
        out_shape=[
            jax.ShapeDtypeStruct(rewards.shape, F32),
            jax.ShapeDtypeStruct((8, 128), F32),
        ],
        name="advantages",
    )(rewards, values, next_values, terminal, truncated)


def unfold(block, phase, width, rows):
    lane = lax.broadcasted_iota(jnp.int32, (1, HID), 1)
    if phase:
        turned = pltpu.roll(block, HID - phase, 1)
        block = jnp.where(lane < HID - phase, turned[:rows], turned[1 : rows + 1])
    pieces = []
    for k in range(HID // width):
        start = k * width // 128 * 128
        piece = block[:rows, start : start + 128]
        turn = k * width % 128
        pieces.append(pltpu.roll(piece, 128 - turn, 1) if turn else piece)
    return pieces


def weights_body(
    conv_ref,
    t1_ref,
    b1_ref,
    t2_ref,
    b2_ref,
    t3_ref,
    b3_ref,
    back3_ref,
    back2_ref,
    wide_ref,
    w1_ref,
    w2_ref,
    w3_ref,
):
    wide_ref[...] = conv_ref[...].astype(F32)
    for k, piece in enumerate(unfold(wide_ref[0:24], 0, C1, 24)):
        w1_ref[pl.ds(k, 24, stride=16), :] = piece
    for k, piece in enumerate(unfold(wide_ref[16:96], 32, C2, 72)):
        w2_ref[pl.ds(k, 72, stride=8), :] = piece
    for k, piece in enumerate(unfold(wide_ref[80:168], 96, C3, 80)):
        w3_ref[pl.ds(k, 80, stride=8), :] = piece
    w1 = w1_ref[...].T
    w2 = w2_ref[...].T
    w3 = w3_ref[...].T
    w1_low = w1.astype(BF16)
    w2_low = w2.astype(BF16)
    w3_low = w3.astype(BF16)
    t1_ref[...] = jnp.zeros(t1_ref.shape, BF16)
    for q in range(2):
        for p in range(2):
            row = 64 * q + 32 * p
            for i in range(8):
                lane = (i + 4 * p) * 16
                k = 32 * i + 16 * q
                t1_ref[row : row + 32, lane : lane + 16] = w1_low[0:32, k : k + 16]
    for p in range(2):
        b1_ref[32 * p : 32 * p + 32] = jnp.broadcast_to(w1[0:32, 256:257], (32, 256))
    b2_ref[...] = jnp.broadcast_to(w2[0:64, 512:513], (64, 256))
    b3_ref[...] = jnp.broadcast_to(w3[0:64, 576:577], (64, 256))
    for q in range(2):
        for i in range(4):
            k = 128 * i + 64 * q
            t2_ref[64 * q : 64 * q + 64, 64 * i : 64 * i + 64] = w2_low[0:64, k : k + 64]
    for j in range(3):
        for i in range(3):
            here = (slice(64 * j, 64 * j + 64), slice(64 * i, 64 * i + 64))
            k = (3 * i + j) * 64
            t3_ref[here] = w3_low[0:64, k : k + 64]
            k = (3 * (2 - i) + j) * 64
            back3_ref[here] = w3_ref[k : k + 64, 0:64].astype(BF16)
    for x in range(4):
        for y in range(2):
            for r in range(2):
                k = ((y + 2 - 2 * r) * 4 + x) * 32
                row = 32 * (2 * x + y)
                back2_ref[row : row + 32, 64 * r : 64 * r + 64] = w2_ref[k : k + 32, 0:64].astype(
                    BF16
                )


def conv_weights(block):
    shapes = [
        ((128, 192), BF16),
        ((64, 256), F32),
        ((128, 256), BF16),
        ((64, 256), F32),
        ((192, 192), BF16),
        ((64, 256), F32),
        ((192, 192), BF16),
        ((256, 128), BF16),
    ]
    return pl.pallas_call(
        weights_body,
        out_shape=[jax.ShapeDtypeStruct(shape, kind) for shape, kind in shapes],
        scratch_shapes=[
            pltpu.VMEM((BLOCK_ROWS, HID), F32),
            pltpu.VMEM((384, 128), F32),
            pltpu.VMEM((640, 128), F32),
            pltpu.VMEM((640, 128), F32),
        ],
        compiler_params=pltpu.CompilerParams(vmem_limit_bytes=VMEM_LIMIT),
        name="conv_weights",
    )(block)


def pixel_window(x_refs, first, start, width):
    sides = []
    for e in range(2):
        parts = [x_refs[first + k][e, :, start : start + width, :] for k in range(3)]
        sides.append(jnp.concatenate(parts, axis=0).reshape(12 * width, 128))
    return jnp.concatenate(sides, axis=1)


def forward_body(
    x0, x1, x2, x3, x4, t1_ref, b1_ref, t2_ref, b2_ref, t3_ref, b3_ref, a1_ref, a2_ref, a3_ref
):
    x_refs = (x0, x1, x2, x3, x4)
    t = pl.program_id(1)

    def low(value, bias_ref):
        return jnp.maximum(value + bias_ref[...], 0.0).astype(BF16)

    for h in range(2):
        held = None
        for n in range(21):
            got = mm(t1_ref[...], pixel_window(x_refs, 2 * h, 16 * n, 16))
            if n > 0:
                out = low(held + got[64:128], b1_ref)
                a1_ref[pl.ds(4 * t + 2 * h, 2), n - 1] = out.reshape(2, C1, 256)
            held = got[0:64]

    @pl.when(t == 4)
    def _():
        def conv_two(p, carry):
            held = None
            for n in range(10):
                window = a1_ref[pl.ds(2 * p, 4), 2 * n : 2 * n + 2].reshape(256, 256)
                got = mm(t2_ref[...], window)
                if n > 0:
                    a2_ref[p, n - 1] = low(held + got[64:128], b2_ref)
                held = got[0:64]
            a2_ref[p, 9] = jnp.zeros((C2, 256), BF16)
            return carry

        lax.fori_loop(0, 9, conv_two, 0, unroll=3)

        def conv_three(p, carry):
            held, older = None, None
            for x in range(9):
                got = mm(t3_ref[...], a2_ref[pl.ds(p, 3), x].reshape(192, 256))
                if x > 1:
                    a3_ref[p, x - 2] = low(older + got[128:192], b3_ref)
                older = held + got[64:128] if x > 0 else None
                held = got[0:64]
            return carry

        lax.fori_loop(0, 7, conv_three, 0, unroll=7)


def whole(shape):
    return pl.BlockSpec(shape, lambda *j: (0,) * len(shape), pipeline_mode=pl.Buffered(1))


def pixel_specs():
    def spec(k):
        return pl.BlockSpec((2, 4, 336, 128), lambda j, t: (j, 4 * t + k, 0, 0))

    return [spec(k) for k in range(5)]


def conv_forward(x, t1, b1, t2, b2, t3, b3):
    envs = x.shape[0]
    frames = envs * 128
    return pl.pallas_call(
        forward_body,
        grid=(envs // 2, 5),
        in_specs=pixel_specs()
        + [
            whole((128, 192)),
            whole((64, 256)),
            whole((128, 256)),
            whole((64, 256)),
            whole((192, 192)),
            whole((64, 256)),
        ],
        out_specs=[
            pl.BlockSpec((20, 20, C1, 256), lambda j, t: (0, 0, 0, j)),
            pl.BlockSpec((9, 10, C2, 256), lambda j, t: (0, 0, 0, j)),
            pl.BlockSpec((7, 7, C3, 256), lambda j, t: (0, 0, 0, j)),
        ],
        out_shape=[
            jax.ShapeDtypeStruct((20, 20, C1, frames), BF16),
            jax.ShapeDtypeStruct((9, 10, C2, frames), BF16),
            jax.ShapeDtypeStruct((7, 7, C3, frames), BF16),
        ],
        compiler_params=pltpu.CompilerParams(vmem_limit_bytes=VMEM_LIMIT),
        name="conv_forward",
    )(x, x, x, x, x, t1, b1, t2, b2, t3, b3)


def dense_body(
    scale,
    a3_ref,
    gathered_ref,
    wh_ref,
    bh_ref,
    normed_ref,
    returns_ref,
    actions_ref,
    behavior_ref,
    packed_ref,
    dc3_ref,
    gwh_ref,
    gbh_ref,
    loss_ref,
    wide_ref,
    wd_ref,
):
    late = lax.broadcasted_iota(jnp.int32, (1, HID), 1) >= PHASE
    shards, rows, _ = gathered_ref.shape
    for k in range(shards):
        if rows * k <= TOP + 1 + FEATURES and rows * (k + 1) > TOP:
            wide_ref[rows * k : rows * k + rows] = gathered_ref[k].astype(F32)
    for i in range(0, FEATURES, 448):
        wd_ref[i : i + 448] = jnp.where(
            late, wide_ref[TOP + i : TOP + i + 448], wide_ref[TOP + 1 + i : TOP + 449 + i]
        ).astype(BF16)
    bias = jnp.where(
        late,
        wide_ref[TOP + FEATURES : TOP + 1 + FEATURES],
        wide_ref[TOP + 1 + FEATURES : TOP + 2 + FEATURES],
    )
    bias = jnp.broadcast_to(bias, (8, HID)).T[:, 0:1]
    hidden_pre = mm_tn(wd_ref[...], a3_ref[...]) + bias
    hidden = jnp.maximum(hidden_pre, 0.0).astype(BF16)
    out = mm(wh_ref[...], hidden) + bh_ref[...]
    row = lax.broadcasted_iota(jnp.int32, out.shape, 0)
    is_logit = row < ACTIONS
    logits = jnp.where(is_logit, out, -jnp.inf)
    top = jnp.max(logits, axis=0, keepdims=True)
    shifted = out - top
    exps = jnp.where(is_logit, jnp.exp(shifted), 0.0)
    total = jnp.sum(exps, axis=0, keepdims=True)
    log_probs = jnp.where(is_logit, shifted - jnp.log(total), 0.0)
    probs = jnp.where(is_logit, jnp.exp(log_probs), 0.0)
    value = jnp.sum(jnp.where(row == ACTIONS, out, 0.0), axis=0, keepdims=True)
    normed = normed_ref[...]
    chosen = row == actions_ref[...]
    taken = jnp.sum(jnp.where(chosen, log_probs, 0.0), axis=0, keepdims=True)
    ratio = jnp.exp(taken - behavior_ref[...])
    low = 1.0 - RATIO_CLIP
    high = 1.0 + RATIO_CLIP
    clipped = jnp.clip(ratio, low, high)
    plain = ratio * normed
    cut = clipped * normed
    entropy = -jnp.sum(probs * log_probs, axis=0, keepdims=True)
    error = value - returns_ref[...]
    losses = -jnp.minimum(plain, cut) + 0.5 * VALUE_COEF * error * error - ENTROPY_COEF * entropy
    loss_ref[...] = jnp.sum(losses, axis=1, keepdims=True) * scale
    plain_share = jnp.where(plain < cut, 1.0, jnp.where(plain == cut, 0.5, 0.0))
    inside = jnp.where(
        (ratio > low) & (ratio < high), 1.0, jnp.where((ratio == low) | (ratio == high), 0.5, 0.0)
    )
    d_taken = -scale * normed * ratio * (plain_share + (1.0 - plain_share) * inside)
    d_logits = d_taken * (jnp.where(chosen, 1.0, 0.0) - probs) + (scale * ENTROPY_COEF) * probs * (
        log_probs + entropy
    )
    d_value = scale * VALUE_COEF * error
    d_out = jnp.where(is_logit, d_logits, jnp.where(row == ACTIONS, d_value, 0.0)).astype(BF16)
    gwh_ref[...] = mm_nt(d_out, hidden)
    gbh_ref[...] = jnp.sum(d_out.astype(F32), axis=1, keepdims=True)
    back = mm_tn(wh_ref[...], d_out)
    d_hidden = jnp.where(hidden_pre > 0, back, 0.0).astype(BF16)
    last = LEAD + FEATURES
    wide_ref[0:LEAD] = jnp.zeros((LEAD, HID), F32)
    wide_ref[LEAD:last] = mm_nt(a3_ref[...], d_hidden)
    wide_ref[last:] = jnp.zeros((wide_ref.shape[0] - last, HID), F32)
    ones = jnp.ones((8, d_hidden.shape[1]), BF16)
    wide_ref[last : last + 1] = mm_nt(ones, d_hidden)[0:1]
    for k in range(shards):
        first = rows * k + LEAD - TOP - 1
        for j in range(4):
            cols = slice(128 * j, 128 * j + 128)
            early_part = wide_ref[first : first + rows, cols]
            if 128 * j + 128 <= PHASE:
                part = early_part
            elif 128 * j >= PHASE:
                part = wide_ref[first + 1 : first + 1 + rows, cols]
            else:
                part = jnp.where(
                    late[:, cols], wide_ref[first + 1 : first + 1 + rows, cols], early_part
                )
            packed_ref[k, pl.ds(j, rows, stride=4), :] = part
    d_a3 = mm(wd_ref[...], d_hidden)
    dc3_ref[...] = jnp.where(a3_ref[...] > 0, d_a3, 0.0).astype(BF16)


def dense_step(scale, a3, gathered, wh, bh, normed, returns, actions, behavior):
    frames = a3.shape[1]
    shards, shard_rows, _ = gathered.shape
    rows = wh.shape[0]
    return pl.pallas_call(
        lambda *refs: dense_body(scale, *refs),
        out_shape=[
            jax.ShapeDtypeStruct((shards, 4 * shard_rows, 128), F32),
            jax.ShapeDtypeStruct((FEATURES, frames), BF16),
            jax.ShapeDtypeStruct((rows, HID), F32),
            jax.ShapeDtypeStruct((rows, 1), F32),
            jax.ShapeDtypeStruct((1, 1), F32),
        ],
        scratch_shapes=[
            pltpu.VMEM((max(shards * shard_rows, TOP + 1 + FEATURES) + 2 * LEAD - TOP, HID), F32),
            pltpu.VMEM((FEATURES, HID), BF16),
        ],
        compiler_params=pltpu.CompilerParams(vmem_limit_bytes=VMEM_LIMIT),
        name="dense_step",
    )(a3, gathered, wh, bh, normed, returns, actions, behavior)


def fold(g_ref, width, rows):
    step = HID // width
    lane = lax.broadcasted_iota(jnp.int32, (1, 128), 1)
    columns = []
    for m in range(4):
        total = 0.0
        for t in range(128 // width):
            piece = g_ref[pl.ds(m * 128 // width + t, rows, stride=step), :]
            piece = jnp.where(lane < width, piece, 0.0)
            total = total + (pltpu.roll(piece, width * t, 1) if t else piece)
        columns.append(total)
    return columns


def upper_body(
    a1_hbm,
    a2_ref,
    dc3_ref,
    t3_ref,
    d2_ref,
    packed_ref,
    r2_ref,
    r3_ref,
    s2_ref,
    s3_ref,
    a1_ref,
    d3_ref,
    g2_ref,
    g3_ref,
    sems,
):
    step = pl.program_id(0)
    lanes = pl.ds(pl.multiple_of(256 * step, 256), 256)
    load_a1 = pltpu.make_async_copy(a1_hbm.at[:, :, :, lanes], a1_ref, sems.at[0])
    load_a1.start()

    @pl.when(step == 0)
    def _():
        for ref in (r2_ref, r3_ref, s2_ref, s3_ref):
            ref[...] = jnp.zeros(ref.shape, F32)
        for p in (0, 1, 9, 10):
            d3_ref[p] = jnp.zeros((8, C3, 256), BF16)

    for p in (0, 10):
        d2_ref[p] = jnp.zeros((11, C2, 256), BF16)

    def edge(p, carry):
        d2_ref[p, 0] = jnp.zeros((C2, 256), BF16)
        d2_ref[p, 10] = jnp.zeros((C2, 256), BF16)
        return carry

    lax.fori_loop(1, 10, edge, 0)

    def fill(p, carry):
        d3_ref[p + 2, 0:7] = dc3_ref[p]
        d3_ref[p + 2, 7] = jnp.zeros((C3, 256), BF16)
        s3_ref[...] += jnp.sum(dc3_ref[p].astype(F32), axis=0)
        return carry

    lax.fori_loop(0, 7, fill, 0)

    left = [a2_ref[p : p + 3, 4 * g : 4 * g + 6].reshape(1152, 256) for p in range(7) for g in range(2)]
    right = [d3_ref[p + 2, 4 * g : 4 * g + 4].reshape(256, 256) for p in range(7) for g in range(2)]
    r3_ref[...] += mm_nt(jnp.concatenate(left, axis=1), jnp.concatenate(right, axis=1))

    def three_input(y, carry):
        total = jnp.zeros((C2, 256), F32)
        parts = []
        for x in range(9):
            if x < 7:
                parts.append(mm(t3_ref[...], d3_ref[pl.ds(y, 3), x].reshape(192, 256)))
            back = 0.0
            for j in range(3):
                if 0 <= x - j < 7:
                    back = back + parts[x - j][64 * j : 64 * j + 64]
            masked = jnp.where(a2_ref[y, x] > 0, back, 0.0).astype(BF16)
            d2_ref[y + 1, x + 1] = masked
            total = total + masked.astype(F32)
        s2_ref[...] += total
        return carry

    lax.fori_loop(0, 9, three_input, 0, unroll=3)
    load_a1.wait()

    def two_weights(r, carry):
        left, right = [], []
        for k in range(3):
            p = 3 * r + k
            for g in range(3):
                left.append(a1_ref[pl.ds(2 * p, 4), 6 * g : 6 * g + 8].reshape(1024, 256))
                right.append(d2_ref[p + 1, 1 + 3 * g : 4 + 3 * g].reshape(192, 256))
        r2_ref[:, 0:192] += mm_nt(jnp.concatenate(left, axis=1), jnp.concatenate(right, axis=1))
        return carry

    lax.fori_loop(0, 3, two_weights, 0)

    @pl.when(step == pl.num_programs(0) - 1)
    def _():
        g2_ref[...] = jnp.zeros(g2_ref.shape, F32)
        g3_ref[...] = jnp.zeros(g3_ref.shape, F32)
        for i in range(4):
            k = 256 * i
            total = r2_ref[k : k + 128, 0:128]
            total = total + pltpu.roll(r2_ref[k + 64 : k + 192, 0:128], 64, 1)
            g2_ref[128 * i : 128 * i + 128] = total + r2_ref[k + 128 : k + 256, 128:256]
        for i in range(3):
            k = 384 * i
            total = r3_ref[k : k + 192, 0:128]
            total = total + pltpu.roll(r3_ref[k + 64 : k + 256, 0:128], 64, 1)
            total = total + r3_ref[k + 128 : k + 320, 128:256]
            total = total + pltpu.roll(r3_ref[k + 192 : k + 384, 128:256], 64, 1)
            g3_ref[192 * i : 192 * i + 192] = total
        g2_ref[512:513, 0:64] = jnp.sum(s2_ref[...].T, axis=0, keepdims=True)
        g3_ref[576:577, 0:64] = jnp.sum(s3_ref[...].T, axis=0, keepdims=True)
        lane = lax.broadcasted_iota(jnp.int32, (1, HID), 1)
        packed_ref[...] = jnp.zeros(packed_ref.shape, F32)
        for ref, rows, base, phase in ((g2_ref, 72, 16, 32), (g3_ref, 80, 80, 96)):
            turned = pltpu.roll(jnp.concatenate(fold(ref, 64, rows), axis=1), phase, 1)
            for j in range(4):
                cols = slice(128 * j, 128 * j + 128)
                here = pl.ds(4 * base + j, rows, stride=4)
                packed_ref[here, :] += jnp.where(lane >= phase, turned, 0.0)[:, cols]
                if j == 0:
                    below = pl.ds(4 * base + 4, rows, stride=4)
                    packed_ref[below, :] += jnp.where(lane < phase, turned, 0.0)[:, cols]


def upper_backward(a1, a2, dc3, t3):
    frames = a1.shape[3]
    return pl.pallas_call(
        upper_body,
        grid=(frames // 256,),
        in_specs=[
            pl.BlockSpec(memory_space=pl.ANY),
            pl.BlockSpec((9, 10, C2, 256), lambda j: (0, 0, 0, j)),
            pl.BlockSpec((7, 7, C3, 256), lambda j: (0, 0, 0, j)),
            whole((192, 192)),
        ],
        out_specs=[
            pl.BlockSpec((11, 11, C2, 256), lambda j: (0, 0, 0, j)),
            whole((4 * BLOCK_ROWS, 128)),
        ],
        out_shape=[
            jax.ShapeDtypeStruct((11, 11, C2, frames), BF16),
            jax.ShapeDtypeStruct((4 * BLOCK_ROWS, 128), F32),
        ],
        scratch_shapes=[
            pltpu.VMEM((1024, 256), F32),
            pltpu.VMEM((1152, 256), F32),
            pltpu.VMEM((C2, 256), F32),
            pltpu.VMEM((C3, 256), F32),
            pltpu.VMEM((20, 20, C1, 256), BF16),
            pltpu.VMEM((11, 8, C3, 256), BF16),
            pltpu.VMEM((640, 128), F32),
            pltpu.VMEM((640, 128), F32),
            pltpu.SemaphoreType.DMA((1,)),
        ],
        compiler_params=pltpu.CompilerParams(vmem_limit_bytes=VMEM_LIMIT),
        name="upper_backward",
    )(a1, a2, dc3, t3)


def lower_body(
    x0, x1, x2, x3, x4, a1_ref, d2_ref, t2_ref, packed_ref, r1_ref, s1_ref, g1_ref, d1_ref
):
    x_refs = (x0, x1, x2, x3, x4)
    t = pl.program_id(1)

    @pl.when((pl.program_id(0) == 0) & (t == 0))
    def _():
        r1_ref[...] = jnp.zeros(r1_ref.shape, F32)
        s1_ref[...] = jnp.zeros(s1_ref.shape, F32)

    sums = jnp.zeros((C1, 256), F32)
    for h in range(2):
        held = None
        for n in range(10):
            back = held
            if n < 9:
                got = mm(t2_ref[...], d2_ref[pl.ds(2 * t + h, 2), n + 1].reshape(128, 256))
                back = got[0:128] if n == 0 else held + got[0:128]
                held = got[128:256]
            for x in range(2):
                for y in range(2):
                    k = 32 * (2 * x + y)
                    kept = a1_ref[2 * h + y, 2 * n + x] > 0
                    masked = jnp.where(kept, back[k : k + 32], 0.0).astype(BF16)
                    sums = sums + masked.astype(F32)
                    row = 128 * (n % 2) + k
                    d1_ref[row : row + 32, 256 * (n // 2) : 256 * (n // 2) + 256] = masked
        window = jnp.concatenate(
            [pixel_window(x_refs, 2 * h, 64 * n, 80) for n in range(5)], axis=1
        )
        r1_ref[...] += mm_nt(window, d1_ref[...])
    s1_ref[...] += sums

    @pl.when((pl.program_id(0) == pl.num_programs(0) - 1) & (t == 4))
    def _():
        g1_ref[...] = jnp.zeros(g1_ref.shape, F32)
        for i in range(8):
            total = 0.0
            for p in range(2):
                for q in range(4):
                    k = (i + 4 * p) * 80 + 16 * q
                    col = 128 * (q // 2)
                    turn = 64 * (q % 2) + 32 * p
                    slab = r1_ref[k : k + 32, col : col + 128]
                    total = total + (pltpu.roll(slab, 128 - turn, 1) if turn else slab)
            g1_ref[32 * i : 32 * i + 32] = total
        g1_ref[256:257, 0:32] = jnp.sum(s1_ref[...].T, axis=0, keepdims=True)
        packed_ref[...] = jnp.zeros(packed_ref.shape, F32)
        for j, part in enumerate(fold(g1_ref, 32, 24)):
            packed_ref[pl.ds(j, 24, stride=4), :] = part


def lower_backward(x, a1, d2, t2):
    envs = x.shape[0]
    return pl.pallas_call(
        lower_body,
        grid=(envs // 2, 5),
        in_specs=pixel_specs()
        + [
            pl.BlockSpec((4, 20, C1, 256), lambda j, t: (t, 0, 0, j)),
            pl.BlockSpec((11, 11, C2, 256), lambda j, t: (0, 0, 0, j)),
            whole((256, 128)),
        ],
        out_specs=whole((4 * BLOCK_ROWS, 128)),
        out_shape=jax.ShapeDtypeStruct((4 * BLOCK_ROWS, 128), F32),
        scratch_shapes=[
            pltpu.VMEM((960, 256), F32),
            pltpu.VMEM((C1, 256), F32),
            pltpu.VMEM((384, 128), F32),
            pltpu.VMEM((256, 1280), BF16),
        ],
        compiler_params=pltpu.CompilerParams(vmem_limit_bytes=VMEM_LIMIT),
        name="lower_backward",
    )(x, x, x, x, x, a1, d2, t2)


def swap(value, lanes, step):
    return lax.ppermute(value, "dp", [(i, i ^ step) for i in range(lanes)])


def halving_order(lanes):
    return [1 << k for k in range(lanes.bit_length() - 1)]


def sum_everywhere(value, lanes):
    for step in halving_order(lanes):
        value = value + swap(value, lanes, step)
    return value


def scatter_sum(blocks, lanes, place):
    for step in halving_order(lanes):
        pairs = blocks.reshape((blocks.shape[0] // 2, 2) + blocks.shape[1:])
        high = (place // step) % 2 == 1
        kept = jnp.where(high, pairs[:, 1], pairs[:, 0])
        sent = jnp.where(high, pairs[:, 0], pairs[:, 1])
        blocks = kept + swap(sent, lanes, step)
    return blocks[0]


def gather_blocks(block, lanes, place):
    blocks = block[None]
    for step in reversed(halving_order(lanes)):
        other = swap(blocks, lanes, step)
        high = (place // step) % 2 == 1
        blocks = jnp.stack(
            [jnp.where(high, other, blocks), jnp.where(high, blocks, other)], axis=1
        ).reshape((2 * blocks.shape[0],) + blocks.shape[1:])
    return blocks


def first_rows_everywhere(local, sums, lanes, place):
    rows = local.shape[0]
    owners = -(-(TOP + 1) // rows)
    order = halving_order(lanes)
    if owners == 1:
        block = jnp.pad(local[: TOP + 1], ((0, BLOCK_ROWS - TOP - 1), (0, 0)))
        block = jnp.where(place == 0, block, jnp.zeros((), BF16))
        for step in reversed(order):
            pairs = [(i, i + step) for i in range(0, lanes, 2 * step)]
            came = lax.ppermute(block, "dp", pairs)
            block, sums = lax.optimization_barrier((block + came, sums + swap(sums, lanes, step)))
        return block, sums
    block = jnp.zeros((owners, rows, HID), BF16)
    block = jnp.where(jnp.arange(owners)[:, None, None] == place, local[None], block)
    block = sum_everywhere(block, lanes).reshape(owners * rows, HID)[: TOP + 1]
    return jnp.pad(block, ((0, BLOCK_ROWS - TOP - 1), (0, 0))), sum_everywhere(sums, lanes)


def finish_body(
    scalars_ref,
    mine_ref,
    other_ref,
    mine_extra_ref,
    other_extra_ref,
    first_ref,
    other_first_ref,
    second_ref,
    other_second_ref,
    master_ref,
    momentum_ref,
    clipped_ref,
    first_out,
    second_out,
    moved_ref,
    momentum_out,
    final_ref,
    low_ref,
):
    master = master_ref[...]

    def inner_step(factor, dense_ref, extra_ref, one_ref, two_ref):
        clipped = (dense_ref[...] + extra_ref[...]) * factor
        first_next = BETA_ONE * one_ref[...] + (1.0 - BETA_ONE) * clipped
        second_next = BETA_TWO * two_ref[...] + (1.0 - BETA_TWO) * clipped * clipped
        first_hat = first_next / scalars_ref[2]
        second_hat = second_next / scalars_ref[3]
        inner = master - LEARN_RATE * (
            first_hat / (jnp.sqrt(second_hat) + ADAM_EPSILON) + WEIGHT_DECAY * master
        )
        return clipped, first_next, second_next, master - inner

    clipped, first_next, second_next, drift = inner_step(
        scalars_ref[0], mine_ref, mine_extra_ref, first_ref, second_ref
    )
    clipped_ref[...] = clipped
    first_out[...] = first_next
    second_out[...] = second_next
    _, _, _, other_drift = inner_step(
        scalars_ref[1], other_ref, other_extra_ref, other_first_ref, other_second_ref
    )
    moved = (drift + other_drift) / 2.0
    moved_ref[...] = moved
    momentum_next = OUTER_MOMENTUM * momentum_ref[...] + moved
    momentum_out[...] = momentum_next
    final = master - OUTER_RATE * (moved + OUTER_MOMENTUM * momentum_next)
    final_ref[...] = final
    low_ref[...] = final.astype(BF16)


def finish(scalars, *arrays):
    shape = arrays[0].shape
    return pl.pallas_call(
        finish_body,
        in_specs=[pl.BlockSpec(memory_space=pltpu.SMEM)]
        + [pl.BlockSpec(memory_space=pltpu.VMEM)] * len(arrays),
        out_shape=[jax.ShapeDtypeStruct(shape, F32)] * 6 + [jax.ShapeDtypeStruct(shape, BF16)],
        name="finish",
    )(scalars, *arrays)


def on_device(
    frames,
    actions,
    rewards,
    old_values,
    next_values,
    terminal,
    truncated,
    behavior_logprob,
    master,
    first_moment,
    second_moment,
    outer_momentum,
    step_count,
):
    lanes = lax.axis_size("dp")
    place = lax.axis_index("dp")
    shard_len = master.shape[0]
    rows = shard_len // HID
    groups = lax.axis_size("group")
    assert groups == 2 and rows * HID == shard_len and frames.shape[2] == 128

    def other_group(value):
        return lax.ppermute(value, "group", [(0, 1), (1, 0)])

    master_rows = master.reshape(rows, HID)
    low_rows = master_rows.astype(BF16)
    gathered = lax.all_gather(low_rows, "dp", axis=0)

    advantage, sums = trajectory_advantages(
        rewards[0], old_values[0], next_values[0], terminal[0], truncated[0]
    )
    envs_here, steps_here = advantage.shape
    batch = envs_here * steps_here
    total_frames = batch * lanes
    block, sums = first_rows_everywhere(low_rows, sums, lanes, place)
    mean = sums[0, 0] / total_frames
    spread = sums[1, 0] / total_frames - mean * mean
    normed = ((advantage - mean) * lax.rsqrt(spread + 1e-05)).reshape(1, batch)
    returns = (advantage + old_values[0]).reshape(1, batch)

    x = frames[0].transpose(0, 2, 3, 1)
    t1, b1, t2, b2, t3, b3, back3, back2 = conv_weights(block)
    a1, a2, a3 = conv_forward(x, t1, b1, t2, b2, t3, b3)
    _, first_sent, second_sent = lax.optimization_barrier((block, first_moment[0], second_moment[0]))
    a3, other_first, other_second = lax.optimization_barrier(
        (a3, other_group(first_sent), other_group(second_sent))
    )

    tail = TOP + FEATURES + 1
    head_owner = tail // rows
    head_flat = gathered[head_owner:].reshape((lanes - head_owner) * rows, HID)
    head_flat = head_flat[tail - head_owner * rows :].reshape(-1)[PHASE : PHASE + HEAD_LEN]
    w_head = head_flat[: HID * (ACTIONS + 1)].reshape(HID, ACTIONS + 1)
    w_head = jnp.pad(jnp.roll(w_head, PHASE, axis=0).T, ((0, 13), (0, 0)))
    b_head = jnp.pad(head_flat[HID * (ACTIONS + 1) :], (0, 13)).astype(F32)
    packed_dense, d_c3, g_head, g_head_bias, loss_local = dense_step(
        1.0 / total_frames,
        a3.reshape(FEATURES, batch),
        gathered,
        w_head,
        b_head[:, None],
        normed,
        returns,
        actions[0].reshape(1, batch),
        behavior_logprob[0].reshape(1, batch),
    )
    dense_owned = lax.psum_scatter(packed_dense, "dp", scatter_dimension=0, tiled=False)
    d2, upper = upper_backward(a1, a2, d_c3.reshape(7, 7, C3, batch), back3)
    lower = lower_backward(x, a1, d2, back2)

    tail_rows = lanes * rows - tail
    head_part = jnp.concatenate(
        [
            jnp.zeros((PHASE,), F32),
            jnp.roll(g_head[: ACTIONS + 1].T, -PHASE, axis=0).reshape(-1),
            g_head_bias[: ACTIONS + 1, 0],
            jnp.zeros((tail_rows * HID - PHASE - HEAD_LEN,), F32),
        ]
    ).reshape(4 * tail_rows, 128)
    real = 4 * (BLOCK_ROWS + tail_rows)
    count = -(-real // (8 * lanes)) * 8 * lanes
    head_part = jnp.pad(head_part, ((0, count - real), (0, 0)))
    small = jnp.concatenate([lower + upper, head_part], axis=0)
    piece = scatter_sum(small.reshape(lanes, count // lanes, 128), lanes, place)
    squares = jnp.sum(dense_owned * dense_owned) + jnp.sum(piece * piece)
    row = lax.broadcasted_iota(jnp.int32, (8, 128), 0)
    message = jnp.concatenate([piece, jnp.where(row == 0, squares, loss_local)], axis=0)
    messages = gather_blocks(jnp.stack([message, other_group(message)]), lanes, place)
    facts = jnp.sum(messages[:, :, -8:-6, 0], axis=0)
    norm = jnp.sqrt(facts[:, 0])
    loss_total = facts[0, 1]
    smalls = messages[:, :, :-8].transpose(1, 0, 2, 3).reshape(2, count, 128)

    own_len = 4 * rows

    def own_rows(part, first_row):
        first = first_row // own_len
        blocks = -(-(first_row + part.shape[1]) // own_len) - first
        before = first_row - first * own_len
        part = jnp.pad(
            part, ((0, 0), (before, blocks * own_len - before - part.shape[1]), (0, 0))
        )
        here = (place >= first) & (place < first + blocks)
        start = jnp.clip(place - first, 0, blocks - 1) * own_len
        return jnp.where(here, lax.dynamic_slice_in_dim(part, start, own_len, 1), 0.0)

    extra = own_rows(smalls[:, : 4 * (TOP + 1)], 0)
    extra = extra + own_rows(smalls[:, 4 * BLOCK_ROWS : real], 4 * tail)
    factor = jnp.minimum(1.0, CLIP_NORM / (norm + 1e-06))
    moment_step = step_count[0].astype(F32)
    scalars = jnp.stack(
        [
            factor[0],
            factor[1],
            1.0 - jnp.power(BETA_ONE, moment_step),
            1.0 - jnp.power(BETA_TWO, moment_step),
        ]
    )

    def view(value):
        return value.reshape(own_len, 128)

    results = finish(
        scalars,
        dense_owned,
        other_group(dense_owned),
        extra[0],
        extra[1],
        view(first_moment),
        view(other_first),
        view(second_moment),
        view(other_second),
        view(master),
        view(outer_momentum),
    )
    clipped, first_next, second_next, moved, momentum_next, final, final_low = results
    return (
        clipped.reshape(1, shard_len),
        norm[:1],
        loss_total.reshape(1),
        first_next.reshape(1, shard_len),
        second_next.reshape(1, shard_len),
        moved.reshape(shard_len),
        momentum_next.reshape(shard_len),
        final.reshape(shard_len),
        final_low.reshape(shard_len),
    )


def solution(mesh):
    return jax.shard_map(
        on_device,
        mesh=mesh,
        in_specs=(
            P("group", "dp", None, None, None),
            P("group", "dp", None),
            P("group", "dp", None),
            P("group", "dp", None),
            P("group", "dp", None),
            P("group", "dp", None),
            P("group", "dp", None),
            P("group", "dp", None),
            P("dp"),
            P("group", "dp"),
            P("group", "dp"),
            P("dp"),
            P(),
        ),
        out_specs=(
            P("group", "dp"),
            P("group"),
            P("group"),
            P("group", "dp"),
            P("group", "dp"),
            P("dp"),
            P("dp"),
            P("dp"),
            P("dp"),
        ),
        check_vma=False,
    )
```

```python
import math

import jax
import jax.numpy as jnp
from jax import lax
from jax.experimental import pallas as pl
from jax.experimental.pallas import tpu as pltpu
from jax.sharding import PartitionSpec as P

C1 = 32
C2 = 64
C3 = 64
HID = 512
ACTIONS = 18
PARAMS = 1693875
FEATURES = 49 * C3
CONV_LEN = 256 * C1 + C1 + 16 * C1 * C2 + C2 + 9 * C2 * C3 + C3
TOP = CONV_LEN // HID
LEAD = (TOP + 8) // 8 * 8
BLOCK_ROWS = LEAD + 8
PHASE = CONV_LEN % HID
HEAD_LEN = HID * (ACTIONS + 1) + ACTIONS + 1

BETA_ONE = 0.9
BETA_TWO = 0.999
ADAM_EPSILON = 1e-08
LEARN_RATE = 0.005
WEIGHT_DECAY = 0.01
CLIP_NORM = 0.5
OUTER_RATE = 0.7
OUTER_MOMENTUM = 0.9
DISCOUNT = 0.99
TRACE_DECAY = 0.95
RATIO_CLIP = 0.1
VALUE_COEF = 0.5
ENTROPY_COEF = 0.01

F32 = jnp.float32
BF16 = jnp.bfloat16
VMEM_LIMIT = 63 * 1024 * 1024


def mm(a, b):
    return jnp.dot(a, b, preferred_element_type=F32)


def mm_nt(a, b):
    return lax.dot_general(a, b, (((1,), (1,)), ((), ())), preferred_element_type=F32)


def mm_tn(a, b):
    return lax.dot_general(a, b, (((0,), (0,)), ((), ())), preferred_element_type=F32)


def advantage_body(rewards_ref, values_ref, next_ref, terminal_ref, truncated_ref, out_ref, sums_ref):
    values = values_ref[...]
    steps = values.shape[1]
    lane = lax.broadcasted_iota(jnp.int32, values.shape, 1)
    alive = 1.0 - terminal_ref[...].astype(F32)
    cutoff = truncated_ref[...].astype(F32)
    following = jnp.where(lane < steps - 1, pltpu.roll(values, steps - 1, 1), next_ref[...])
    following = cutoff * next_ref[...] + (1.0 - cutoff) * following
    series = rewards_ref[...] + DISCOUNT * alive * following - values
    keeping = DISCOUNT * TRACE_DECAY * alive * (1.0 - cutoff)
    step = 1
    while step < steps:
        inside = lane < steps - step
        series = series + keeping * jnp.where(inside, pltpu.roll(series, steps - step, 1), 0.0)
        keeping = keeping * jnp.where(inside, pltpu.roll(keeping, steps - step, 1), 0.0)
        step *= 2
    out_ref[...] = series
    first = jnp.sum(jnp.sum(series, axis=0, keepdims=True), axis=1, keepdims=True)
    square = jnp.sum(jnp.sum(series * series, axis=0, keepdims=True), axis=1, keepdims=True)
    place = lax.broadcasted_iota(jnp.int32, (8, 128), 0)
    sums_ref[...] = jnp.where(place == 0, first, square)


def trajectory_advantages(rewards, values, next_values, terminal, truncated):
    return pl.pallas_call(
        advantage_body,
        out_shape=[
            jax.ShapeDtypeStruct(rewards.shape, F32),
            jax.ShapeDtypeStruct((8, 128), F32),
        ],
        name="advantages",
    )(rewards, values, next_values, terminal, truncated)


def unfold(block, phase, width, rows):
    lane = lax.broadcasted_iota(jnp.int32, (1, HID), 1)
    if phase:
        turned = pltpu.roll(block, HID - phase, 1)
        block = jnp.where(lane < HID - phase, turned[:rows], turned[1 : rows + 1])
    pieces = []
    for k in range(HID // width):
        start = k * width // 128 * 128
        piece = block[:rows, start : start + 128]
        turn = k * width % 128
        pieces.append(pltpu.roll(piece, 128 - turn, 1) if turn else piece)
    return pieces


def weights_body(
    conv_ref,
    t1_ref,
    b1_ref,
    t2_ref,
    b2_ref,
    t3_ref,
    b3_ref,
    back3_ref,
    back2_ref,
    wide_ref,
    w1_ref,
    w2_ref,
    w3_ref,
):
    wide_ref[...] = conv_ref[...].astype(F32)
    for k, piece in enumerate(unfold(wide_ref[0:24], 0, C1, 24)):
        w1_ref[pl.ds(k, 24, stride=16), :] = piece
    for k, piece in enumerate(unfold(wide_ref[16:96], 32, C2, 72)):
        w2_ref[pl.ds(k, 72, stride=8), :] = piece
    for k, piece in enumerate(unfold(wide_ref[80:168], 96, C3, 80)):
        w3_ref[pl.ds(k, 80, stride=8), :] = piece
    w1 = w1_ref[...].T
    w2 = w2_ref[...].T
    w3 = w3_ref[...].T
    w1_low = w1.astype(BF16)
    w2_low = w2.astype(BF16)
    w3_low = w3.astype(BF16)
    t1_ref[...] = jnp.zeros(t1_ref.shape, BF16)
    for q in range(2):
        for p in range(2):
            row = 64 * q + 32 * p
            for i in range(8):
                lane = (i + 4 * p) * 16
                k = 32 * i + 16 * q
                t1_ref[row : row + 32, lane : lane + 16] = w1_low[0:32, k : k + 16]
    for p in range(2):
        b1_ref[32 * p : 32 * p + 32] = jnp.broadcast_to(w1[0:32, 256:257], (32, 256))
    b2_ref[...] = jnp.broadcast_to(w2[0:64, 512:513], (64, 256))
    b3_ref[...] = jnp.broadcast_to(w3[0:64, 576:577], (64, 256))
    for q in range(2):
        for i in range(4):
            k = 128 * i + 64 * q
            t2_ref[64 * q : 64 * q + 64, 64 * i : 64 * i + 64] = w2_low[0:64, k : k + 64]
    for j in range(3):
        for i in range(3):
            here = (slice(64 * j, 64 * j + 64), slice(64 * i, 64 * i + 64))
            k = (3 * i + j) * 64
            t3_ref[here] = w3_low[0:64, k : k + 64]
            k = (3 * (2 - i) + j) * 64
            back3_ref[here] = w3_ref[k : k + 64, 0:64].astype(BF16)
    for x in range(4):
        for y in range(2):
            for r in range(2):
                k = ((y + 2 - 2 * r) * 4 + x) * 32
                row = 32 * (2 * x + y)
                back2_ref[row : row + 32, 64 * r : 64 * r + 64] = w2_ref[k : k + 32, 0:64].astype(
                    BF16
                )


def conv_weights(block):
    shapes = [
        ((128, 192), BF16),
        ((64, 256), F32),
        ((128, 256), BF16),
        ((64, 256), F32),
        ((192, 192), BF16),
        ((64, 256), F32),
        ((192, 192), BF16),
        ((256, 128), BF16),
    ]
    return pl.pallas_call(
        weights_body,
        out_shape=[jax.ShapeDtypeStruct(shape, kind) for shape, kind in shapes],
        scratch_shapes=[
            pltpu.VMEM((BLOCK_ROWS, HID), F32),
            pltpu.VMEM((384, 128), F32),
            pltpu.VMEM((640, 128), F32),
            pltpu.VMEM((640, 128), F32),
        ],
        compiler_params=pltpu.CompilerParams(vmem_limit_bytes=VMEM_LIMIT),
        name="conv_weights",
    )(block)


def pixel_window(x_refs, first, start, width):
    sides = []
    for e in range(2):
        parts = [x_refs[first + k][e, :, start : start + width, :] for k in range(3)]
        sides.append(jnp.concatenate(parts, axis=0).reshape(12 * width, 128))
    return jnp.concatenate(sides, axis=1)


def forward_body(
    x_hbm,
    t1_ref,
    b1_ref,
    t2_ref,
    b2_ref,
    t3_ref,
    b3_ref,
    a1_hbm,
    a2_ref,
    a3_ref,
    x_ref,
    a1_ref,
    x_sems,
    sem,
):
    pair = pl.program_id(0)
    lanes = pl.ds(pl.multiple_of(256 * pair, 256), 256)

    def load(j, c):
        part = pl.ds(12 * c, 12)
        return pltpu.make_async_copy(
            x_hbm.at[pl.ds(2 * j, 2), part], x_ref.at[j, :, part], x_sems.at[7 * j + c]
        )

    @pl.when(pair == 0)
    def _():
        for j in range(x_ref.shape[0]):
            for c in range(7):
                load(j, c).start()

    def low(value, bias_ref):
        return jnp.maximum(value + bias_ref[...], 0.0).astype(BF16)

    ready = 0
    for m in range(10):
        while m % 2 == 0 and 12 * ready < 8 * m + 20:
            load(pair, ready).wait()
            ready += 1
        held = None
        for n in range(21):
            window = jnp.concatenate(
                [
                    x_ref[pair, e, 8 * m : 8 * m + 12, 16 * n : 16 * n + 16, :].reshape(192, 128)
                    for e in range(2)
                ],
                axis=1,
            )
            got = mm(t1_ref[...], window)
            if n > 0:
                out = low(held + got[64:128], b1_ref)
                a1_ref[2 * m : 2 * m + 2, n - 1] = out.reshape(2, C1, 256)
            held = got[0:64]
        if m % 2 == 1:
            here = pl.ds(2 * m - 2, 4)
            pltpu.make_async_copy(a1_ref.at[here], a1_hbm.at[here, :, :, lanes], sem.at[0]).start()

    def conv_two(p, carry):
        held = None
        for n in range(10):
            window = a1_ref[pl.ds(2 * p, 4), 2 * n : 2 * n + 2].reshape(256, 256)
            got = mm(t2_ref[...], window)
            if n > 0:
                a2_ref[p, n - 1] = low(held + got[64:128], b2_ref)
            held = got[0:64]
        a2_ref[p, 9] = jnp.zeros((C2, 256), BF16)
        return carry

    lax.fori_loop(0, 9, conv_two, 0, unroll=3)

    for p in range(7):
        held, older = None, None
        for x in range(9):
            got = mm(t3_ref[...], a2_ref[p : p + 3, x].reshape(192, 256))
            if x > 1:
                a3_ref[p, x - 2] = low(older + got[128:192], b3_ref)
            older = held + got[64:128] if x > 0 else None
            held = got[0:64]
    pltpu.make_async_copy(a1_ref, a1_hbm.at[:, :, :, lanes], sem.at[0]).wait()


def whole(shape):
    return pl.BlockSpec(shape, lambda *j: (0,) * len(shape), pipeline_mode=pl.Buffered(1))


def pixel_specs():
    def spec(k):
        return pl.BlockSpec((2, 4, 336, 128), lambda j, t: (j, 4 * t + k, 0, 0))

    return [spec(k) for k in range(5)]


def conv_forward(x, t1, b1, t2, b2, t3, b3):
    envs = x.shape[0]
    frames = envs * 128
    return pl.pallas_call(
        forward_body,
        grid=(envs // 2,),
        in_specs=[
            pl.BlockSpec(memory_space=pl.ANY),
            whole((128, 192)),
            whole((64, 256)),
            whole((128, 256)),
            whole((64, 256)),
            whole((192, 192)),
            whole((64, 256)),
        ],
        out_specs=[
            pl.BlockSpec(memory_space=pl.ANY),
            pl.BlockSpec((9, 10, C2, 256), lambda j: (0, 0, 0, j)),
            pl.BlockSpec((7, 7, C3, 256), lambda j: (0, 0, 0, j)),
        ],
        out_shape=[
            jax.ShapeDtypeStruct((20, 20, C1, frames), BF16),
            jax.ShapeDtypeStruct((9, 10, C2, frames), BF16),
            jax.ShapeDtypeStruct((7, 7, C3, frames), BF16),
        ],
        scratch_shapes=[
            pltpu.VMEM((envs // 2, 2, 84, 336, 128), BF16),
            pltpu.VMEM((20, 20, C1, 256), BF16),
            pltpu.SemaphoreType.DMA((7 * envs // 2,)),
            pltpu.SemaphoreType.DMA((1,)),
        ],
        compiler_params=pltpu.CompilerParams(vmem_limit_bytes=VMEM_LIMIT),
        name="conv_forward",
    )(x, t1, b1, t2, b2, t3, b3)


def dense_body(
    scale,
    a3_hbm,
    gathered_hbm,
    head_ref,
    sums_ref,
    advantage_ref,
    values_ref,
    actions_ref,
    behavior_ref,
    packed_hbm,
    wd_hbm,
    d_hidden_ref,
    gwh_ref,
    gbh_ref,
    loss_ref,
    wide_ref,
    a3_ref,
    gathered_ref,
    wd_ref,
    packed_ref,
    sems,
):
    shards, rows, _ = gathered_ref.shape
    halves = [slice(0, shards // 2), slice(shards // 2, shards)]
    loads = []
    for h, part in enumerate(halves):
        loads.append(
            pltpu.make_async_copy(gathered_hbm.at[part], gathered_ref.at[part], sems.at[h])
        )
        loads[h].start()
    load_a3 = pltpu.make_async_copy(a3_hbm, a3_ref, sems.at[2])
    load_a3.start()
    late = lax.broadcasted_iota(jnp.int32, (1, HID), 1) >= PHASE
    for h, part in enumerate(halves):
        loads[h].wait()
        for k in range(part.start, part.stop):
            if rows * k <= TOP + 1 + FEATURES and rows * (k + 1) > TOP:
                wide_ref[rows * k : rows * k + rows] = gathered_ref[k].astype(F32)
    for i in range(0, FEATURES, 448):
        wd_ref[i : i + 448] = jnp.where(
            late, wide_ref[TOP + i : TOP + i + 448], wide_ref[TOP + 1 + i : TOP + 449 + i]
        ).astype(BF16)
    store_wd = pltpu.make_async_copy(wd_ref, wd_hbm, sems.at[3])
    store_wd.start()
    bias = jnp.where(
        late,
        wide_ref[TOP + FEATURES : TOP + 1 + FEATURES],
        wide_ref[TOP + 1 + FEATURES : TOP + 2 + FEATURES],
    )
    bias = jnp.broadcast_to(bias, (8, HID)).T[:, 0:1]
    load_a3.wait()
    hidden_pre = mm_tn(wd_ref[...], a3_ref[...]) + bias
    hidden = jnp.maximum(hidden_pre, 0.0).astype(BF16)
    head = head_ref[...].astype(F32).T
    weights = pltpu.roll(head[0:32, 0:HID], PHASE, 1).astype(BF16)
    out = mm(weights, hidden) + head[0:32, HID : HID + 1]
    row = lax.broadcasted_iota(jnp.int32, out.shape, 0)
    is_logit = row < ACTIONS
    logits = jnp.where(is_logit, out, -jnp.inf)
    top = jnp.max(logits, axis=0, keepdims=True)
    shifted = out - top
    exps = jnp.where(is_logit, jnp.exp(shifted), 0.0)
    total = jnp.sum(exps, axis=0, keepdims=True)
    log_probs = jnp.where(is_logit, shifted - jnp.log(total), 0.0)
    probs = jnp.where(is_logit, jnp.exp(log_probs), 0.0)
    value = jnp.sum(jnp.where(row == ACTIONS, out, 0.0), axis=0, keepdims=True)

    def flat(array):
        return jnp.concatenate([array[e : e + 1] for e in range(array.shape[0])], axis=1)

    advantage = flat(advantage_ref[...])
    sums = sums_ref[...]
    mean = sums[0:1, 0:1] * scale
    spread = sums[1:2, 0:1] * scale - mean * mean
    normed = (advantage - mean) * lax.rsqrt(spread + 1e-05)
    returns = advantage + flat(values_ref[...])
    chosen = row == flat(actions_ref[...])
    taken = jnp.sum(jnp.where(chosen, log_probs, 0.0), axis=0, keepdims=True)
    ratio = jnp.exp(taken - flat(behavior_ref[...]))
    low = 1.0 - RATIO_CLIP
    high = 1.0 + RATIO_CLIP
    clipped = jnp.clip(ratio, low, high)
    plain = ratio * normed
    cut = clipped * normed
    entropy = -jnp.sum(probs * log_probs, axis=0, keepdims=True)
    error = value - returns
    losses = -jnp.minimum(plain, cut) + 0.5 * VALUE_COEF * error * error - ENTROPY_COEF * entropy
    loss_ref[...] = jnp.sum(losses, axis=1, keepdims=True) * scale
    plain_share = jnp.where(plain < cut, 1.0, jnp.where(plain == cut, 0.5, 0.0))
    inside = jnp.where(
        (ratio > low) & (ratio < high), 1.0, jnp.where((ratio == low) | (ratio == high), 0.5, 0.0)
    )
    d_taken = -scale * normed * ratio * (plain_share + (1.0 - plain_share) * inside)
    d_logits = d_taken * (jnp.where(chosen, 1.0, 0.0) - probs) + (scale * ENTROPY_COEF) * probs * (
        log_probs + entropy
    )
    d_value = scale * VALUE_COEF * error
    d_out = jnp.where(is_logit, d_logits, jnp.where(row == ACTIONS, d_value, 0.0)).astype(BF16)
    gwh_ref[...] = mm_nt(d_out, hidden)
    gbh_ref[...] = jnp.sum(d_out.astype(F32), axis=1, keepdims=True)
    back = mm_tn(weights, d_out)
    d_hidden = jnp.where(hidden > 0, back, 0.0).astype(BF16)
    d_hidden_ref[...] = d_hidden
    last = LEAD + FEATURES
    wide_ref[0:LEAD] = jnp.zeros((LEAD, HID), F32)
    wide_ref[last:] = jnp.zeros((wide_ref.shape[0] - last, HID), F32)
    ones = jnp.ones((8, d_hidden.shape[1]), BF16)
    wide_ref[last : last + 1] = mm_nt(ones, d_hidden)[0:1]
    done = 0
    for i in range(0, FEATURES, 448):
        wide_ref[LEAD + i : LEAD + i + 448] = mm_nt(a3_ref[i : i + 448], d_hidden)
        for k in range(done, shards):
            first = rows * k + LEAD - TOP - 1
            if first + rows >= LEAD + i + 448 and i + 448 < FEATURES:
                break
            done = k + 1
            for j in range(4):
                cols = slice(128 * j, 128 * j + 128)
                early_part = wide_ref[first : first + rows, cols]
                if 128 * j + 128 <= PHASE:
                    part = early_part
                elif 128 * j >= PHASE:
                    part = wide_ref[first + 1 : first + 1 + rows, cols]
                else:
                    part = jnp.where(
                        late[:, cols], wide_ref[first + 1 : first + 1 + rows, cols], early_part
                    )
                packed_ref[k, pl.ds(j, rows, stride=4), :] = part
            pltpu.make_async_copy(packed_ref.at[k], packed_hbm.at[k], sems.at[4]).start()
    store_wd.wait()
    pltpu.make_async_copy(packed_ref, packed_hbm, sems.at[4]).wait()


def dense_step(scale, a3, gathered, head, sums, advantage, values, actions, behavior):
    frames = a3.shape[1]
    shards, shard_rows, _ = gathered.shape
    rows = 32
    here = pl.BlockSpec(memory_space=pltpu.VMEM)
    away = pl.BlockSpec(memory_space=pl.ANY)
    return pl.pallas_call(
        lambda *refs: dense_body(scale, *refs),
        in_specs=[away, away] + [here] * 6,
        out_specs=[away, away] + [here] * 4,
        out_shape=[
            jax.ShapeDtypeStruct((shards, 4 * shard_rows, 128), F32),
            jax.ShapeDtypeStruct((FEATURES, HID), BF16),
            jax.ShapeDtypeStruct((HID, frames), BF16),
            jax.ShapeDtypeStruct((rows, HID), F32),
            jax.ShapeDtypeStruct((rows, 1), F32),
            jax.ShapeDtypeStruct((1, 1), F32),
        ],
        scratch_shapes=[
            pltpu.VMEM((max(shards * shard_rows, TOP + 1 + FEATURES) + 2 * LEAD - TOP, HID), F32),
            pltpu.VMEM(a3.shape, BF16),
            pltpu.VMEM(gathered.shape, BF16),
            pltpu.VMEM((FEATURES, HID), BF16),
            pltpu.VMEM((shards, 4 * shard_rows, 128), F32),
            pltpu.SemaphoreType.DMA((5,)),
        ],
        compiler_params=pltpu.CompilerParams(vmem_limit_bytes=VMEM_LIMIT),
        name="dense_step",
    )(a3, gathered, head, sums, advantage, values, actions, behavior)


def fold(g_ref, width, rows):
    step = HID // width
    lane = lax.broadcasted_iota(jnp.int32, (1, 128), 1)
    columns = []
    for m in range(4):
        total = 0.0
        for t in range(128 // width):
            piece = g_ref[pl.ds(m * 128 // width + t, rows, stride=step), :]
            piece = jnp.where(lane < width, piece, 0.0)
            total = total + (pltpu.roll(piece, width * t, 1) if t else piece)
        columns.append(total)
    return columns


def upper_body(
    a1_hbm,
    a2_ref,
    a3_ref,
    wd_ref,
    d_hidden_ref,
    t3_ref,
    d2_ref,
    packed_ref,
    r2_ref,
    r3_ref,
    s2_ref,
    s3_ref,
    a1_ref,
    d3_ref,
    g2_ref,
    g3_ref,
    sems,
):
    step = pl.program_id(0)
    lanes = pl.ds(pl.multiple_of(256 * step, 256), 256)
    load_a1 = pltpu.make_async_copy(a1_hbm.at[:, :, :, lanes], a1_ref, sems.at[0])
    load_a1.start()

    @pl.when(step == 0)
    def _():
        for ref in (r2_ref, r3_ref, s2_ref, s3_ref):
            ref[...] = jnp.zeros(ref.shape, F32)
        for p in (0, 1, 9, 10):
            d3_ref[p] = jnp.zeros((8, C3, 256), BF16)

    for p in (0, 10):
        d2_ref[p] = jnp.zeros((11, C2, 256), BF16)

    def edge(p, carry):
        d2_ref[p, 0] = jnp.zeros((C2, 256), BF16)
        d2_ref[p, 10] = jnp.zeros((C2, 256), BF16)
        return carry

    lax.fori_loop(1, 10, edge, 0)

    sums = jnp.zeros((C3, 256), F32)
    for p in range(7):
        back = mm(wd_ref[448 * p : 448 * p + 448], d_hidden_ref[...]).reshape(7, C3, 256)
        masked = jnp.where(a3_ref[p] > 0, back, 0.0).astype(BF16)
        d3_ref[p + 2, 0:7] = masked
        d3_ref[p + 2, 7] = jnp.zeros((C3, 256), BF16)
        sums = sums + jnp.sum(masked.astype(F32), axis=0)
    s3_ref[...] += sums

    left = [a2_ref[p : p + 3, 4 * g : 4 * g + 6].reshape(1152, 256) for p in range(7) for g in range(2)]
    right = [d3_ref[p + 2, 4 * g : 4 * g + 4].reshape(256, 256) for p in range(7) for g in range(2)]
    r3_ref[...] += mm_nt(jnp.concatenate(left, axis=1), jnp.concatenate(right, axis=1))

    def three_input(y, carry):
        total = jnp.zeros((C2, 256), F32)
        parts = []
        for x in range(9):
            if x < 7:
                parts.append(mm(t3_ref[...], d3_ref[pl.ds(y, 3), x].reshape(192, 256)))
            back = 0.0
            for j in range(3):
                if 0 <= x - j < 7:
                    back = back + parts[x - j][64 * j : 64 * j + 64]
            masked = jnp.where(a2_ref[y, x] > 0, back, 0.0).astype(BF16)
            d2_ref[y + 1, x + 1] = masked
            total = total + masked.astype(F32)
        s2_ref[...] += total
        return carry

    lax.fori_loop(0, 9, three_input, 0, unroll=3)
    load_a1.wait()

    def two_weights(r, carry):
        left, right = [], []
        for k in range(3):
            p = 3 * r + k
            for g in range(3):
                left.append(a1_ref[pl.ds(2 * p, 4), 6 * g : 6 * g + 8].reshape(1024, 256))
                right.append(d2_ref[p + 1, 1 + 3 * g : 4 + 3 * g].reshape(192, 256))
        r2_ref[:, 0:192] += mm_nt(jnp.concatenate(left, axis=1), jnp.concatenate(right, axis=1))
        return carry

    lax.fori_loop(0, 3, two_weights, 0)

    @pl.when(step == pl.num_programs(0) - 1)
    def _():
        g2_ref[...] = jnp.zeros(g2_ref.shape, F32)
        g3_ref[...] = jnp.zeros(g3_ref.shape, F32)
        for i in range(4):
            k = 256 * i
            total = r2_ref[k : k + 128, 0:128]
            total = total + pltpu.roll(r2_ref[k + 64 : k + 192, 0:128], 64, 1)
            g2_ref[128 * i : 128 * i + 128] = total + r2_ref[k + 128 : k + 256, 128:256]
        for i in range(3):
            k = 384 * i
            total = r3_ref[k : k + 192, 0:128]
            total = total + pltpu.roll(r3_ref[k + 64 : k + 256, 0:128], 64, 1)
            total = total + r3_ref[k + 128 : k + 320, 128:256]
            total = total + pltpu.roll(r3_ref[k + 192 : k + 384, 128:256], 64, 1)
            g3_ref[192 * i : 192 * i + 192] = total
        g2_ref[512:513, 0:64] = jnp.sum(s2_ref[...].T, axis=0, keepdims=True)
        g3_ref[576:577, 0:64] = jnp.sum(s3_ref[...].T, axis=0, keepdims=True)
        lane = lax.broadcasted_iota(jnp.int32, (1, HID), 1)
        packed_ref[...] = jnp.zeros(packed_ref.shape, F32)
        for ref, rows, base, phase in ((g2_ref, 72, 16, 32), (g3_ref, 80, 80, 96)):
            turned = pltpu.roll(jnp.concatenate(fold(ref, 64, rows), axis=1), phase, 1)
            for j in range(4):
                cols = slice(128 * j, 128 * j + 128)
                here = pl.ds(4 * base + j, rows, stride=4)
                packed_ref[here, :] += jnp.where(lane >= phase, turned, 0.0)[:, cols]
                if j == 0:
                    below = pl.ds(4 * base + 4, rows, stride=4)
                    packed_ref[below, :] += jnp.where(lane < phase, turned, 0.0)[:, cols]


def upper_backward(a1, a2, a3, w_dense, d_hidden, t3):
    frames = a1.shape[3]
    return pl.pallas_call(
        upper_body,
        grid=(frames // 256,),
        in_specs=[
            pl.BlockSpec(memory_space=pl.ANY),
            pl.BlockSpec((9, 10, C2, 256), lambda j: (0, 0, 0, j)),
            pl.BlockSpec((7, 7, C3, 256), lambda j: (0, 0, 0, j)),
            whole((FEATURES, HID)),
            pl.BlockSpec((HID, 256), lambda j: (0, j)),
            whole((192, 192)),
        ],
        out_specs=[
            pl.BlockSpec((11, 11, C2, 256), lambda j: (0, 0, 0, j)),
            whole((4 * BLOCK_ROWS, 128)),
        ],
        out_shape=[
            jax.ShapeDtypeStruct((11, 11, C2, frames), BF16),
            jax.ShapeDtypeStruct((4 * BLOCK_ROWS, 128), F32),
        ],
        scratch_shapes=[
            pltpu.VMEM((1024, 256), F32),
            pltpu.VMEM((1152, 256), F32),
            pltpu.VMEM((C2, 256), F32),
            pltpu.VMEM((C3, 256), F32),
            pltpu.VMEM((20, 20, C1, 256), BF16),
            pltpu.VMEM((11, 8, C3, 256), BF16),
            pltpu.VMEM((640, 128), F32),
            pltpu.VMEM((640, 128), F32),
            pltpu.SemaphoreType.DMA((1,)),
        ],
        compiler_params=pltpu.CompilerParams(vmem_limit_bytes=VMEM_LIMIT),
        name="upper_backward",
    )(a1, a2, a3, w_dense, d_hidden, t3)


def lower_body(
    x0, x1, x2, x3, x4, a1_ref, d2_ref, t2_ref, packed_ref, r1_ref, s1_ref, g1_ref, d1_ref
):
    x_refs = (x0, x1, x2, x3, x4)
    t = pl.program_id(1)

    @pl.when((pl.program_id(0) == 0) & (t == 0))
    def _():
        r1_ref[...] = jnp.zeros(r1_ref.shape, F32)
        s1_ref[...] = jnp.zeros(s1_ref.shape, F32)

    sums = jnp.zeros((C1, 256), F32)
    for h in range(2):
        held = None
        for n in range(10):
            back = held
            if n < 9:
                got = mm(t2_ref[...], d2_ref[pl.ds(2 * t + h, 2), n + 1].reshape(128, 256))
                back = got[0:128] if n == 0 else held + got[0:128]
                held = got[128:256]
            for x in range(2):
                for y in range(2):
                    k = 32 * (2 * x + y)
                    kept = a1_ref[2 * h + y, 2 * n + x] > 0
                    masked = jnp.where(kept, back[k : k + 32], 0.0).astype(BF16)
                    sums = sums + masked.astype(F32)
                    row = 128 * (n % 2) + k
                    d1_ref[row : row + 32, 256 * (n // 2) : 256 * (n // 2) + 256] = masked
        window = jnp.concatenate(
            [pixel_window(x_refs, 2 * h, 64 * n, 80) for n in range(5)], axis=1
        )
        r1_ref[...] += mm_nt(window, d1_ref[...])
    s1_ref[...] += sums

    @pl.when((pl.program_id(0) == pl.num_programs(0) - 1) & (t == 4))
    def _():
        g1_ref[...] = jnp.zeros(g1_ref.shape, F32)
        for i in range(8):
            total = 0.0
            for p in range(2):
                for q in range(4):
                    k = (i + 4 * p) * 80 + 16 * q
                    col = 128 * (q // 2)
                    turn = 64 * (q % 2) + 32 * p
                    slab = r1_ref[k : k + 32, col : col + 128]
                    total = total + (pltpu.roll(slab, 128 - turn, 1) if turn else slab)
            g1_ref[32 * i : 32 * i + 32] = total
        g1_ref[256:257, 0:32] = jnp.sum(s1_ref[...].T, axis=0, keepdims=True)
        packed_ref[...] = jnp.zeros(packed_ref.shape, F32)
        for j, part in enumerate(fold(g1_ref, 32, 24)):
            packed_ref[pl.ds(j, 24, stride=4), :] = part


def lower_backward(x, a1, d2, t2):
    envs = x.shape[0]
    return pl.pallas_call(
        lower_body,
        grid=(envs // 2, 5),
        in_specs=pixel_specs()
        + [
            pl.BlockSpec((4, 20, C1, 256), lambda j, t: (t, 0, 0, j)),
            pl.BlockSpec((11, 11, C2, 256), lambda j, t: (0, 0, 0, j)),
            whole((256, 128)),
        ],
        out_specs=whole((4 * BLOCK_ROWS, 128)),
        out_shape=jax.ShapeDtypeStruct((4 * BLOCK_ROWS, 128), F32),
        scratch_shapes=[
            pltpu.VMEM((960, 256), F32),
            pltpu.VMEM((C1, 256), F32),
            pltpu.VMEM((384, 128), F32),
            pltpu.VMEM((256, 1280), BF16),
        ],
        compiler_params=pltpu.CompilerParams(vmem_limit_bytes=VMEM_LIMIT),
        name="lower_backward",
    )(x, x, x, x, x, a1, d2, t2)


def swap(value, lanes, step):
    return lax.ppermute(value, "dp", [(i, i ^ step) for i in range(lanes)])


def halving_order(lanes):
    return [1 << k for k in range(lanes.bit_length() - 1)]


def sum_everywhere(value, lanes):
    for step in halving_order(lanes):
        value = value + swap(value, lanes, step)
    return value


def scatter_sum(blocks, lanes, place):
    for step in halving_order(lanes):
        pairs = blocks.reshape((blocks.shape[0] // 2, 2) + blocks.shape[1:])
        high = (place // step) % 2 == 1
        kept = jnp.where(high, pairs[:, 1], pairs[:, 0])
        sent = jnp.where(high, pairs[:, 0], pairs[:, 1])
        blocks = kept + swap(sent, lanes, step)
    return blocks[0]


def gather_blocks(block, beside, lanes, place):
    blocks = block[None]
    for step in reversed(halving_order(lanes)):
        if step == 1:
            blocks, beside = lax.optimization_barrier((blocks, beside))
        other = swap(blocks, lanes, step)
        high = (place // step) % 2 == 1
        blocks = jnp.stack(
            [jnp.where(high, other, blocks), jnp.where(high, blocks, other)], axis=1
        ).reshape((2 * blocks.shape[0],) + blocks.shape[1:])
    return blocks, beside


def first_rows_everywhere(local, sums, lanes, place):
    rows = local.shape[0]
    owners = -(-(TOP + 1) // rows)
    order = halving_order(lanes)
    if owners == 1:
        block = jnp.pad(local[: TOP + 1], ((0, BLOCK_ROWS - TOP - 1), (0, 0)))
        block = jnp.where(place == 0, block, jnp.zeros((), BF16))
        for step in reversed(order):
            pairs = [(i, i + step) for i in range(0, lanes, 2 * step)]
            came = lax.ppermute(block, "dp", pairs)
            block, sums = lax.optimization_barrier((block + came, sums + swap(sums, lanes, step)))
        return block, sums
    block = jnp.zeros((owners, rows, HID), BF16)
    block = jnp.where(jnp.arange(owners)[:, None, None] == place, local[None], block)
    block = sum_everywhere(block, lanes).reshape(owners * rows, HID)[: TOP + 1]
    return jnp.pad(block, ((0, BLOCK_ROWS - TOP - 1), (0, 0))), sum_everywhere(sums, lanes)


def facts_body(dense_ref, piece_ref, loss_ref, message_ref):
    dense = dense_ref[...]
    piece = piece_ref[...]
    squares = jnp.sum(dense * dense, axis=0, keepdims=True)
    squares = squares + jnp.sum(piece * piece, axis=0, keepdims=True)
    squares = jnp.sum(squares, axis=1, keepdims=True)
    height = piece.shape[0]
    message_ref[0:height] = piece
    row = lax.broadcasted_iota(jnp.int32, (8, 128), 0)
    message_ref[height : height + 8] = jnp.where(row == 0, squares, loss_ref[...])


def facts_message(dense, piece, loss):
    return pl.pallas_call(
        facts_body,
        out_shape=jax.ShapeDtypeStruct((piece.shape[0] + 8, 128), F32),
        name="facts_message",
    )(dense, piece, loss)


def finish_body(
    parts,
    own_len,
    place_ref,
    scalars_ref,
    messages_ref,
    mine_ref,
    other_ref,
    first_ref,
    other_first_ref,
    second_ref,
    other_second_ref,
    master_ref,
    momentum_ref,
    clipped_ref,
    first_out,
    second_out,
    moved_ref,
    momentum_out,
    final_ref,
    low_ref,
    norm_ref,
    loss_ref,
    extra_ref,
):
    height = messages_ref.shape[2] - 8
    place = place_ref[0]
    first_step = pl.program_id(0) == 0

    @pl.when(first_step)
    def _():
        extra_ref[...] = jnp.zeros(extra_ref.shape, F32)

    for start, stop, target in parts:
        for owner in range(target // own_len, (target + stop - start - 1) // own_len + 1):
            shift = target - start - owner * own_len
            low = max(start, -shift)
            high = min(stop, own_len - shift)

            @pl.when(first_step & (place == owner))
            def _(shift=shift, low=low, high=high):
                for k in range(low // height, (high - 1) // height + 1):
                    a = max(low, k * height)
                    b = min(high, (k + 1) * height)
                    for g in range(2):
                        extra_ref[g, a + shift : b + shift] = messages_ref[
                            k, g, a - k * height : b - k * height
                        ]

    block = master_ref.shape[0]
    here = pl.ds(pl.multiple_of(block * pl.program_id(0), 8), block)

    factors = []
    for g in range(2):
        facts = jnp.sum(messages_ref[:, g, height : height + 8, :], axis=0)
        norm = jnp.sqrt(facts[0:1, 0:1])
        factors.append(jnp.minimum(1.0, CLIP_NORM / (norm + 1e-06)))
        if g == 0:
            norm_ref[...] = norm
            loss_ref[...] = facts[1:2, 0:1]
    master = master_ref[...]

    def inner_step(g, dense_ref, one_ref, two_ref):
        clipped = (dense_ref[...] + extra_ref[g, here]) * factors[g]
        first_next = BETA_ONE * one_ref[...] + (1.0 - BETA_ONE) * clipped
        second_next = BETA_TWO * two_ref[...] + (1.0 - BETA_TWO) * clipped * clipped
        first_hat = first_next / scalars_ref[0]
        second_hat = second_next / scalars_ref[1]
        inner = master - LEARN_RATE * (
            first_hat / (jnp.sqrt(second_hat) + ADAM_EPSILON) + WEIGHT_DECAY * master
        )
        return clipped, first_next, second_next, master - inner

    clipped, first_next, second_next, drift = inner_step(0, mine_ref, first_ref, second_ref)
    clipped_ref[:, 0, :] = clipped
    first_out[:, 0, :] = first_next
    second_out[:, 0, :] = second_next
    _, _, _, other_drift = inner_step(1, other_ref, other_first_ref, other_second_ref)
    moved = (drift + other_drift) / 2.0
    moved_ref[...] = moved
    momentum_next = OUTER_MOMENTUM * momentum_ref[...] + moved
    momentum_out[...] = momentum_next
    final = master - OUTER_RATE * (moved + OUTER_MOMENTUM * momentum_next)
    final_ref[...] = final
    low_ref[...] = final.astype(BF16)


def finish(parts, place, scalars, messages, *arrays):
    own_len = arrays[0].shape[0]
    block = min(208, -(-own_len // 8) * 8)
    steps = -(-own_len // block)
    scalar = pl.BlockSpec(memory_space=pltpu.SMEM)

    def spec(array):
        if len(array.shape) == 3:
            return pl.BlockSpec((block, 1, 128), lambda k: (k, 0, 0))
        return pl.BlockSpec((block, 128), lambda k: (k, 0))

    outs = [jax.ShapeDtypeStruct((own_len, 1, 128), F32)] * 3
    outs += [jax.ShapeDtypeStruct((own_len, 128), F32)] * 3
    outs += [jax.ShapeDtypeStruct((own_len, 128), BF16)]
    return pl.pallas_call(
        lambda *refs: finish_body(parts, own_len, *refs),
        grid=(steps,),
        in_specs=[scalar, scalar, whole(messages.shape)] + [spec(array) for array in arrays],
        out_specs=[spec(array) for array in outs] + [whole((1, 1))] * 2,
        out_shape=outs + [jax.ShapeDtypeStruct((1, 1), F32)] * 2,
        scratch_shapes=[pltpu.VMEM((2, block * steps, 128), F32)],
        name="finish",
    )(place, scalars, messages, *arrays)


def on_device(
    frames,
    actions,
    rewards,
    old_values,
    next_values,
    terminal,
    truncated,
    behavior_logprob,
    master,
    first_moment,
    second_moment,
    outer_momentum,
    step_count,
):
    lanes = lax.axis_size("dp")
    place = lax.axis_index("dp")
    shard_len = master.shape[0]
    rows = shard_len // HID
    groups = lax.axis_size("group")
    assert groups == 2 and rows * HID == shard_len and frames.shape[2] == 128

    def other_group(value):
        return lax.ppermute(value, "group", [(0, 1), (1, 0)])

    master_rows = master.reshape(rows, HID)
    low_rows = master_rows.astype(BF16)
    gathered = lax.all_gather(low_rows, "dp", axis=0)

    advantage, sums = trajectory_advantages(
        rewards[0], old_values[0], next_values[0], terminal[0], truncated[0]
    )
    envs_here, steps_here = advantage.shape
    batch = envs_here * steps_here
    total_frames = batch * lanes
    block, sums = first_rows_everywhere(low_rows, sums, lanes, place)
    x = frames[0].transpose(0, 2, 3, 1)
    t1, b1, t2, b2, t3, b3, back3, back2 = conv_weights(block)
    a1, a2, a3 = conv_forward(x, t1, b1, t2, b2, t3, b3)
    tail = TOP + FEATURES + 1
    head_owner = tail // rows
    head_flat = gathered[head_owner:].reshape((lanes - head_owner) * rows, HID)
    head_flat = head_flat[tail - head_owner * rows :].reshape(-1)[PHASE : PHASE + HEAD_LEN]
    head = jnp.pad(head_flat.reshape(HID + 1, ACTIONS + 1), ((0, 7), (0, 127 - ACTIONS)))
    packed_dense, w_dense, d_hidden, g_head, g_head_bias, loss_local = dense_step(
        1.0 / total_frames,
        a3.reshape(FEATURES, batch),
        gathered,
        head,
        sums,
        advantage,
        old_values[0],
        actions[0],
        behavior_logprob[0],
    )
    dense_owned = lax.psum_scatter(packed_dense, "dp", scatter_dimension=0, tiled=False)
    d_hidden, first_sent, second_sent = lax.optimization_barrier(
        (d_hidden, first_moment, second_moment)
    )
    d2, upper = upper_backward(a1, a2, a3, w_dense, d_hidden, back3)
    first_flat = first_sent.reshape(shard_len)
    second_flat = second_sent.reshape(shard_len)
    d2, other_first, other_second = lax.optimization_barrier(
        (d2, other_group(first_flat), other_group(second_flat))
    )
    lower = lower_backward(x, a1, d2, back2)

    tail_rows = lanes * rows - tail
    head_part = jnp.concatenate(
        [
            jnp.zeros((PHASE,), F32),
            jnp.roll(g_head[: ACTIONS + 1].T, -PHASE, axis=0).reshape(-1),
            g_head_bias[: ACTIONS + 1, 0],
            jnp.zeros((tail_rows * HID - PHASE - HEAD_LEN,), F32),
        ]
    ).reshape(4 * tail_rows, 128)
    real = 4 * (BLOCK_ROWS + tail_rows)
    count = -(-real // (8 * lanes)) * 8 * lanes
    head_part = jnp.pad(head_part, ((0, count - real), (0, 0)))
    small = jnp.concatenate([lower + upper, head_part], axis=0)
    piece = scatter_sum(small.reshape(lanes, count // lanes, 128), lanes, place)
    message = facts_message(dense_owned, piece, loss_local)
    messages, dense_other = gather_blocks(
        jnp.stack([message, other_group(message)]), other_group(dense_owned), lanes, place
    )

    own_len = 4 * rows
    moment_step = step_count[0].astype(F32)
    scalars = jnp.stack(
        [1.0 - jnp.power(BETA_ONE, moment_step), 1.0 - jnp.power(BETA_TWO, moment_step)]
    )
    parts = ((0, 4 * (TOP + 1), 0), (4 * BLOCK_ROWS, real, 4 * tail))

    def view(value):
        return value.reshape(own_len, 128)

    results = finish(
        parts,
        place.reshape(1),
        scalars,
        messages,
        dense_owned,
        dense_other,
        view(first_flat),
        view(other_first),
        view(second_flat),
        view(other_second),
        view(master),
        view(outer_momentum),
    )
    clipped, first_next, second_next, moved, momentum_next, final, final_low, norm, loss = results
    return (
        clipped.reshape(1, shard_len),
        norm.reshape(1),
        loss.reshape(1),
        first_next.reshape(1, shard_len),
        second_next.reshape(1, shard_len),
        moved.reshape(shard_len),
        momentum_next.reshape(shard_len),
        final.reshape(shard_len),
        final_low.reshape(shard_len),
    )


def solution(mesh):
    return jax.shard_map(
        on_device,
        mesh=mesh,
        in_specs=(
            P("group", "dp", None, None, None),
            P("group", "dp", None),
            P("group", "dp", None),
            P("group", "dp", None),
            P("group", "dp", None),
            P("group", "dp", None),
            P("group", "dp", None),
            P("group", "dp", None),
            P("dp"),
            P("group", "dp"),
            P("group", "dp"),
            P("dp"),
            P(),
        ),
        out_specs=(
            P("group", "dp"),
            P("group"),
            P("group"),
            P("group", "dp"),
            P("group", "dp"),
            P("dp"),
            P("dp"),
            P("dp"),
            P("dp"),
        ),
        check_vma=False,
    )
```

```python
import math

import jax
import jax.numpy as jnp
from jax import lax
from jax.experimental import pallas as pl
from jax.experimental.pallas import tpu as pltpu
from jax.sharding import PartitionSpec as P

C1 = 32
C2 = 64
C3 = 64
HID = 512
ACTIONS = 18
PARAMS = 1693875
FEATURES = 49 * C3
CONV_LEN = 256 * C1 + C1 + 16 * C1 * C2 + C2 + 9 * C2 * C3 + C3
TOP = CONV_LEN // HID
LEAD = (TOP + 8) // 8 * 8
BLOCK_ROWS = LEAD + 8
PHASE = CONV_LEN % HID
HEAD_LEN = HID * (ACTIONS + 1) + ACTIONS + 1

BETA_ONE = 0.9
BETA_TWO = 0.999
ADAM_EPSILON = 1e-08
LEARN_RATE = 0.005
WEIGHT_DECAY = 0.01
CLIP_NORM = 0.5
OUTER_RATE = 0.7
OUTER_MOMENTUM = 0.9
DISCOUNT = 0.99
TRACE_DECAY = 0.95
RATIO_CLIP = 0.1
VALUE_COEF = 0.5
ENTROPY_COEF = 0.01

F32 = jnp.float32
BF16 = jnp.bfloat16
VMEM_LIMIT = 63 * 1024 * 1024


def mm(a, b):
    return jnp.dot(a, b, preferred_element_type=F32)


def mm_nt(a, b):
    return lax.dot_general(a, b, (((1,), (1,)), ((), ())), preferred_element_type=F32)


def mm_tn(a, b):
    return lax.dot_general(a, b, (((0,), (0,)), ((), ())), preferred_element_type=F32)


def advantage_body(rewards_ref, values_ref, next_ref, terminal_ref, truncated_ref, out_ref, sums_ref):
    values = values_ref[...]
    steps = values.shape[1]
    lane = lax.broadcasted_iota(jnp.int32, values.shape, 1)
    alive = 1.0 - terminal_ref[...].astype(F32)
    cutoff = truncated_ref[...].astype(F32)
    following = jnp.where(lane < steps - 1, pltpu.roll(values, steps - 1, 1), next_ref[...])
    following = cutoff * next_ref[...] + (1.0 - cutoff) * following
    series = rewards_ref[...] + DISCOUNT * alive * following - values
    keeping = DISCOUNT * TRACE_DECAY * alive * (1.0 - cutoff)
    step = 1
    while step < steps:
        inside = lane < steps - step
        series = series + keeping * jnp.where(inside, pltpu.roll(series, steps - step, 1), 0.0)
        keeping = keeping * jnp.where(inside, pltpu.roll(keeping, steps - step, 1), 0.0)
        step *= 2
    out_ref[...] = series
    first = jnp.sum(jnp.sum(series, axis=0, keepdims=True), axis=1, keepdims=True)
    square = jnp.sum(jnp.sum(series * series, axis=0, keepdims=True), axis=1, keepdims=True)
    place = lax.broadcasted_iota(jnp.int32, (8, 128), 0)
    sums_ref[...] = jnp.where(place == 0, first, square)


def trajectory_advantages(rewards, values, next_values, terminal, truncated):
    return pl.pallas_call(
        advantage_body,
        out_shape=[
            jax.ShapeDtypeStruct(rewards.shape, F32),
            jax.ShapeDtypeStruct((8, 128), F32),
        ],
        name="advantages",
    )(rewards, values, next_values, terminal, truncated)


def unfold(block, phase, width, rows):
    lane = lax.broadcasted_iota(jnp.int32, (1, HID), 1)
    if phase:
        turned = pltpu.roll(block, HID - phase, 1)
        block = jnp.where(lane < HID - phase, turned[:rows], turned[1 : rows + 1])
    pieces = []
    for k in range(HID // width):
        start = k * width // 128 * 128
        piece = block[:rows, start : start + 128]
        turn = k * width % 128
        pieces.append(pltpu.roll(piece, 128 - turn, 1) if turn else piece)
    return pieces


def weights_body(
    conv_ref,
    t1_ref,
    b1_ref,
    t2_ref,
    b2_ref,
    t3_ref,
    b3_ref,
    back3_ref,
    back2_ref,
    wide_ref,
    w1_ref,
    w2_ref,
    w3_ref,
):
    wide_ref[...] = conv_ref[...].astype(F32)
    for k, piece in enumerate(unfold(wide_ref[0:24], 0, C1, 24)):
        w1_ref[pl.ds(k, 24, stride=16), :] = piece
    for k, piece in enumerate(unfold(wide_ref[16:96], 32, C2, 72)):
        w2_ref[pl.ds(k, 72, stride=8), :] = piece
    for k, piece in enumerate(unfold(wide_ref[80:168], 96, C3, 80)):
        w3_ref[pl.ds(k, 80, stride=8), :] = piece
    w1 = w1_ref[...].T
    w2 = w2_ref[...].T
    w3 = w3_ref[...].T
    w1_low = w1.astype(BF16)
    w2_low = w2.astype(BF16)
    w3_low = w3.astype(BF16)
    t1_ref[...] = jnp.zeros(t1_ref.shape, BF16)
    for q in range(2):
        for p in range(2):
            row = 64 * q + 32 * p
            for i in range(8):
                lane = (i + 4 * p) * 16
                k = 32 * i + 16 * q
                t1_ref[row : row + 32, lane : lane + 16] = w1_low[0:32, k : k + 16]
    for p in range(2):
        b1_ref[32 * p : 32 * p + 32] = jnp.broadcast_to(w1[0:32, 256:257], (32, 256))
    b2_ref[...] = jnp.broadcast_to(w2[0:64, 512:513], (64, 256))
    b3_ref[...] = jnp.broadcast_to(w3[0:64, 576:577], (64, 256))
    for q in range(2):
        for i in range(4):
            k = 128 * i + 64 * q
            t2_ref[64 * q : 64 * q + 64, 64 * i : 64 * i + 64] = w2_low[0:64, k : k + 64]
    for j in range(3):
        for i in range(3):
            here = (slice(64 * j, 64 * j + 64), slice(64 * i, 64 * i + 64))
            k = (3 * i + j) * 64
            t3_ref[here] = w3_low[0:64, k : k + 64]
            k = (3 * (2 - i) + j) * 64
            back3_ref[here] = w3_ref[k : k + 64, 0:64].astype(BF16)
    for x in range(4):
        for y in range(2):
            for r in range(2):
                k = ((y + 2 - 2 * r) * 4 + x) * 32
                row = 32 * (2 * x + y)
                back2_ref[row : row + 32, 64 * r : 64 * r + 64] = w2_ref[k : k + 32, 0:64].astype(
                    BF16
                )


def conv_weights(block):
    shapes = [
        ((128, 192), BF16),
        ((64, 256), F32),
        ((128, 256), BF16),
        ((64, 256), F32),
        ((192, 192), BF16),
        ((64, 256), F32),
        ((192, 192), BF16),
        ((256, 128), BF16),
    ]
    return pl.pallas_call(
        weights_body,
        out_shape=[jax.ShapeDtypeStruct(shape, kind) for shape, kind in shapes],
        scratch_shapes=[
            pltpu.VMEM((BLOCK_ROWS, HID), F32),
            pltpu.VMEM((384, 128), F32),
            pltpu.VMEM((640, 128), F32),
            pltpu.VMEM((640, 128), F32),
        ],
        compiler_params=pltpu.CompilerParams(vmem_limit_bytes=VMEM_LIMIT),
        name="conv_weights",
    )(block)


def pixel_window(x_refs, first, start, width):
    sides = []
    for e in range(2):
        parts = [x_refs[first + k][e, :, start : start + width, :] for k in range(3)]
        sides.append(jnp.concatenate(parts, axis=0).reshape(12 * width, 128))
    return jnp.concatenate(sides, axis=1)


def forward_body(
    x_hbm,
    t1_ref,
    b1_ref,
    t2_ref,
    b2_ref,
    t3_ref,
    b3_ref,
    a1_hbm,
    a2_ref,
    a3_ref,
    x_ref,
    a1_ref,
    x_sems,
    sem,
):
    pair = pl.program_id(0)
    lanes = pl.ds(pl.multiple_of(256 * pair, 256), 256)

    def load(j, c):
        part = pl.ds(12 * c, 12)
        return pltpu.make_async_copy(
            x_hbm.at[pl.ds(2 * j, 2), part], x_ref.at[j, :, part], x_sems.at[7 * j + c]
        )

    @pl.when(pair == 0)
    def _():
        for j in range(x_ref.shape[0]):
            for c in range(7):
                load(j, c).start()

    def low(value, bias_ref):
        return jnp.maximum(value + bias_ref[...], 0.0).astype(BF16)

    ready = 0
    for m in range(10):
        while m % 2 == 0 and 12 * ready < 8 * m + 20:
            load(pair, ready).wait()
            ready += 1
        held = None
        for n in range(21):
            window = jnp.concatenate(
                [
                    x_ref[pair, e, 8 * m : 8 * m + 12, 16 * n : 16 * n + 16, :].reshape(192, 128)
                    for e in range(2)
                ],
                axis=1,
            )
            got = mm(t1_ref[...], window)
            if n > 0:
                out = low(held + got[64:128], b1_ref)
                a1_ref[2 * m : 2 * m + 2, n - 1] = out.reshape(2, C1, 256)
            held = got[0:64]
        if m % 2 == 1:
            here = pl.ds(2 * m - 2, 4)
            pltpu.make_async_copy(a1_ref.at[here], a1_hbm.at[here, :, :, lanes], sem.at[0]).start()

    def conv_two(p, carry):
        held = None
        for n in range(10):
            window = a1_ref[pl.ds(2 * p, 4), 2 * n : 2 * n + 2].reshape(256, 256)
            got = mm(t2_ref[...], window)
            if n > 0:
                a2_ref[p, n - 1] = low(held + got[64:128], b2_ref)
            held = got[0:64]
        a2_ref[p, 9] = jnp.zeros((C2, 256), BF16)
        return carry

    lax.fori_loop(0, 9, conv_two, 0, unroll=3)

    for p in range(7):
        held, older = None, None
        for x in range(9):
            got = mm(t3_ref[...], a2_ref[p : p + 3, x].reshape(192, 256))
            if x > 1:
                a3_ref[p, x - 2] = low(older + got[128:192], b3_ref)
            older = held + got[64:128] if x > 0 else None
            held = got[0:64]
    pltpu.make_async_copy(a1_ref, a1_hbm.at[:, :, :, lanes], sem.at[0]).wait()


def whole(shape):
    return pl.BlockSpec(shape, lambda *j: (0,) * len(shape), pipeline_mode=pl.Buffered(1))


def pixel_specs():
    def spec(k):
        return pl.BlockSpec((2, 4, 336, 128), lambda j, t: (j, 4 * t + k, 0, 0))

    return [spec(k) for k in range(5)]


def conv_forward(x, t1, b1, t2, b2, t3, b3):
    envs = x.shape[0]
    frames = envs * 128
    return pl.pallas_call(
        forward_body,
        grid=(envs // 2,),
        in_specs=[
            pl.BlockSpec(memory_space=pl.ANY),
            whole((128, 192)),
            whole((64, 256)),
            whole((128, 256)),
            whole((64, 256)),
            whole((192, 192)),
            whole((64, 256)),
        ],
        out_specs=[
            pl.BlockSpec(memory_space=pl.ANY),
            pl.BlockSpec((9, 10, C2, 256), lambda j: (0, 0, 0, j)),
            pl.BlockSpec((7, 7, C3, 256), lambda j: (0, 0, 0, j)),
        ],
        out_shape=[
            jax.ShapeDtypeStruct((20, 20, C1, frames), BF16),
            jax.ShapeDtypeStruct((9, 10, C2, frames), BF16),
            jax.ShapeDtypeStruct((7, 7, C3, frames), BF16),
        ],
        scratch_shapes=[
            pltpu.VMEM((envs // 2, 2, 84, 336, 128), BF16),
            pltpu.VMEM((20, 20, C1, 256), BF16),
            pltpu.SemaphoreType.DMA((7 * envs // 2,)),
            pltpu.SemaphoreType.DMA((1,)),
        ],
        compiler_params=pltpu.CompilerParams(vmem_limit_bytes=VMEM_LIMIT),
        name="conv_forward",
    )(x, t1, b1, t2, b2, t3, b3)


def dense_body(
    scale,
    a3_hbm,
    gathered_hbm,
    head_ref,
    sums_ref,
    advantage_ref,
    values_ref,
    actions_ref,
    behavior_ref,
    packed_hbm,
    wd_hbm,
    d_hidden_ref,
    gwh_ref,
    gbh_ref,
    loss_ref,
    wide_ref,
    a3_ref,
    gathered_ref,
    wd_ref,
    packed_ref,
    sems,
):
    shards, rows, _ = gathered_ref.shape
    halves = [slice(0, shards // 2), slice(shards // 2, shards)]
    loads = []
    for h, part in enumerate(halves):
        loads.append(
            pltpu.make_async_copy(gathered_hbm.at[part], gathered_ref.at[part], sems.at[h])
        )
        loads[h].start()
    load_a3 = pltpu.make_async_copy(a3_hbm, a3_ref, sems.at[2])
    load_a3.start()
    late = lax.broadcasted_iota(jnp.int32, (1, HID), 1) >= PHASE
    for h, part in enumerate(halves):
        loads[h].wait()
        for k in range(part.start, part.stop):
            if rows * k <= TOP + 1 + FEATURES and rows * (k + 1) > TOP:
                wide_ref[rows * k : rows * k + rows] = gathered_ref[k].astype(F32)
    for i in range(0, FEATURES, 448):
        wd_ref[i : i + 448] = jnp.where(
            late, wide_ref[TOP + i : TOP + i + 448], wide_ref[TOP + 1 + i : TOP + 449 + i]
        ).astype(BF16)
    store_wd = pltpu.make_async_copy(wd_ref, wd_hbm, sems.at[3])
    store_wd.start()
    bias = jnp.where(
        late,
        wide_ref[TOP + FEATURES : TOP + 1 + FEATURES],
        wide_ref[TOP + 1 + FEATURES : TOP + 2 + FEATURES],
    )
    bias = jnp.broadcast_to(bias, (8, HID)).T[:, 0:1]
    load_a3.wait()
    hidden_pre = mm_tn(wd_ref[...], a3_ref[...]) + bias
    hidden = jnp.maximum(hidden_pre, 0.0).astype(BF16)
    head = head_ref[...].astype(F32).T
    weights = pltpu.roll(head[0:32, 0:HID], PHASE, 1).astype(BF16)
    out = mm(weights, hidden) + head[0:32, HID : HID + 1]
    row = lax.broadcasted_iota(jnp.int32, out.shape, 0)
    is_logit = row < ACTIONS
    logits = jnp.where(is_logit, out, -jnp.inf)
    top = jnp.max(logits, axis=0, keepdims=True)
    shifted = out - top
    exps = jnp.where(is_logit, jnp.exp(shifted), 0.0)
    total = jnp.sum(exps, axis=0, keepdims=True)
    log_probs = jnp.where(is_logit, shifted - jnp.log(total), 0.0)
    probs = jnp.where(is_logit, jnp.exp(log_probs), 0.0)
    value = jnp.sum(jnp.where(row == ACTIONS, out, 0.0), axis=0, keepdims=True)

    def flat(array):
        return jnp.concatenate([array[e : e + 1] for e in range(array.shape[0])], axis=1)

    advantage = flat(advantage_ref[...])
    sums = sums_ref[...]
    mean = sums[0:1, 0:1] * scale
    spread = sums[1:2, 0:1] * scale - mean * mean
    normed = (advantage - mean) * lax.rsqrt(spread + 1e-05)
    returns = advantage + flat(values_ref[...])
    chosen = row == flat(actions_ref[...])
    taken = jnp.sum(jnp.where(chosen, log_probs, 0.0), axis=0, keepdims=True)
    ratio = jnp.exp(taken - flat(behavior_ref[...]))
    low = 1.0 - RATIO_CLIP
    high = 1.0 + RATIO_CLIP
    clipped = jnp.clip(ratio, low, high)
    plain = ratio * normed
    cut = clipped * normed
    entropy = -jnp.sum(probs * log_probs, axis=0, keepdims=True)
    error = value - returns
    losses = -jnp.minimum(plain, cut) + 0.5 * VALUE_COEF * error * error - ENTROPY_COEF * entropy
    loss_ref[...] = jnp.sum(losses, axis=1, keepdims=True) * scale
    plain_share = jnp.where(plain < cut, 1.0, jnp.where(plain == cut, 0.5, 0.0))
    inside = jnp.where(
        (ratio > low) & (ratio < high), 1.0, jnp.where((ratio == low) | (ratio == high), 0.5, 0.0)
    )
    d_taken = -scale * normed * ratio * (plain_share + (1.0 - plain_share) * inside)
    d_logits = d_taken * (jnp.where(chosen, 1.0, 0.0) - probs) + (scale * ENTROPY_COEF) * probs * (
        log_probs + entropy
    )
    d_value = scale * VALUE_COEF * error
    d_out = jnp.where(is_logit, d_logits, jnp.where(row == ACTIONS, d_value, 0.0)).astype(BF16)
    gwh_ref[...] = mm_nt(d_out, hidden)
    gbh_ref[...] = jnp.sum(d_out.astype(F32), axis=1, keepdims=True)
    back = mm_tn(weights, d_out)
    d_hidden = jnp.where(hidden > 0, back, 0.0).astype(BF16)
    d_hidden_ref[...] = d_hidden
    last = LEAD + FEATURES
    wide_ref[0:LEAD] = jnp.zeros((LEAD, HID), F32)
    wide_ref[last:] = jnp.zeros((wide_ref.shape[0] - last, HID), F32)
    ones = jnp.ones((8, d_hidden.shape[1]), BF16)
    wide_ref[last : last + 1] = mm_nt(ones, d_hidden)[0:1]
    done = 0
    for i in range(0, FEATURES, 448):
        wide_ref[LEAD + i : LEAD + i + 448] = mm_nt(a3_ref[i : i + 448], d_hidden)
        for k in range(done, shards):
            first = rows * k + LEAD - TOP - 1
            if first + rows >= LEAD + i + 448 and i + 448 < FEATURES:
                break
            done = k + 1
            for j in range(4):
                cols = slice(128 * j, 128 * j + 128)
                early_part = wide_ref[first : first + rows, cols]
                if 128 * j + 128 <= PHASE:
                    part = early_part
                elif 128 * j >= PHASE:
                    part = wide_ref[first + 1 : first + 1 + rows, cols]
                else:
                    part = jnp.where(
                        late[:, cols], wide_ref[first + 1 : first + 1 + rows, cols], early_part
                    )
                packed_ref[k, pl.ds(j, rows, stride=4), :] = part
            pltpu.make_async_copy(packed_ref.at[k], packed_hbm.at[k], sems.at[4]).start()
    store_wd.wait()
    pltpu.make_async_copy(packed_ref, packed_hbm, sems.at[4]).wait()


def dense_step(scale, a3, gathered, head, sums, advantage, values, actions, behavior):
    frames = a3.shape[1]
    shards, shard_rows, _ = gathered.shape
    rows = 32
    here = pl.BlockSpec(memory_space=pltpu.VMEM)
    away = pl.BlockSpec(memory_space=pl.ANY)
    return pl.pallas_call(
        lambda *refs: dense_body(scale, *refs),
        in_specs=[away, away] + [here] * 6,
        out_specs=[away, away] + [here] * 4,
        out_shape=[
            jax.ShapeDtypeStruct((shards, 4 * shard_rows, 128), F32),
            jax.ShapeDtypeStruct((FEATURES, HID), BF16),
            jax.ShapeDtypeStruct((HID, frames), BF16),
            jax.ShapeDtypeStruct((rows, HID), F32),
            jax.ShapeDtypeStruct((rows, 1), F32),
            jax.ShapeDtypeStruct((1, 1), F32),
        ],
        scratch_shapes=[
            pltpu.VMEM((max(shards * shard_rows, TOP + 1 + FEATURES) + 2 * LEAD - TOP, HID), F32),
            pltpu.VMEM(a3.shape, BF16),
            pltpu.VMEM(gathered.shape, BF16),
            pltpu.VMEM((FEATURES, HID), BF16),
            pltpu.VMEM((shards, 4 * shard_rows, 128), F32),
            pltpu.SemaphoreType.DMA((5,)),
        ],
        compiler_params=pltpu.CompilerParams(vmem_limit_bytes=VMEM_LIMIT),
        name="dense_step",
    )(a3, gathered, head, sums, advantage, values, actions, behavior)


def fold(g_ref, width, rows):
    step = HID // width
    lane = lax.broadcasted_iota(jnp.int32, (1, 128), 1)
    columns = []
    for m in range(4):
        total = 0.0
        for t in range(128 // width):
            piece = g_ref[pl.ds(m * 128 // width + t, rows, stride=step), :]
            piece = jnp.where(lane < width, piece, 0.0)
            total = total + (pltpu.roll(piece, width * t, 1) if t else piece)
        columns.append(total)
    return columns


def upper_body(
    a1_hbm,
    a2_ref,
    a3_ref,
    wd_ref,
    d_hidden_ref,
    t3_ref,
    d2_ref,
    packed_ref,
    r2_ref,
    r3_ref,
    a1_ref,
    d3_ref,
    g2_ref,
    g3_ref,
    sems,
):
    step = pl.program_id(0)
    lanes = pl.ds(pl.multiple_of(256 * step, 256), 256)
    load_a1 = pltpu.make_async_copy(a1_hbm.at[:, :, :, lanes], a1_ref, sems.at[0])
    load_a1.start()

    @pl.when(step == 0)
    def _():
        for ref in (r2_ref, r3_ref):
            ref[...] = jnp.zeros(ref.shape, F32)
        for p in (0, 1, 9, 10):
            d3_ref[p] = jnp.zeros((8, C3, 256), BF16)

    for p in (0, 10):
        d2_ref[p] = jnp.zeros((11, C2, 256), BF16)

    def edge(p, carry):
        d2_ref[p, 0] = jnp.zeros((C2, 256), BF16)
        d2_ref[p, 10] = jnp.zeros((C2, 256), BF16)
        return carry

    lax.fori_loop(1, 10, edge, 0)

    zero = jnp.zeros((), BF16)
    for p in range(7):
        back = mm(wd_ref[448 * p : 448 * p + 448], d_hidden_ref[...]).reshape(7, C3, 256)
        d3_ref[p + 2, 0:7] = jnp.where(a3_ref[p] > 0, back.astype(BF16), zero)
        d3_ref[p + 2, 7] = jnp.zeros((C3, 256), BF16)

    left = [a2_ref[p : p + 3, 4 * g : 4 * g + 6].reshape(1152, 256) for p in range(7) for g in range(2)]
    right = [d3_ref[p + 2, 4 * g : 4 * g + 4].reshape(256, 256) for p in range(7) for g in range(2)]
    left = jnp.concatenate(left, axis=1)
    left = jnp.concatenate([left, jnp.ones((16, left.shape[1]), BF16)], axis=0)
    r3_ref[...] += mm_nt(left, jnp.concatenate(right, axis=1))

    def three_input(y, carry):
        parts = []
        for x in range(9):
            if x < 7:
                parts.append(mm(t3_ref[...], d3_ref[pl.ds(y, 3), x].reshape(192, 256)))
            back = 0.0
            for j in range(3):
                if 0 <= x - j < 7:
                    back = back + parts[x - j][64 * j : 64 * j + 64]
            d2_ref[y + 1, x + 1] = jnp.where(a2_ref[y, x] > 0, back.astype(BF16), zero)
        return carry

    lax.fori_loop(0, 9, three_input, 0, unroll=3)
    load_a1.wait()

    def two_weights(r, carry):
        left, right = [], []
        for k in range(3):
            p = 3 * r + k
            for g in range(3):
                left.append(a1_ref[pl.ds(2 * p, 4), 6 * g : 6 * g + 8].reshape(1024, 256))
                right.append(d2_ref[p + 1, 1 + 3 * g : 4 + 3 * g].reshape(192, 256))
        left = jnp.concatenate(left, axis=1)
        left = jnp.concatenate([left, jnp.ones((16, left.shape[1]), BF16)], axis=0)
        r2_ref[:, 0:192] += mm_nt(left, jnp.concatenate(right, axis=1))
        return carry

    lax.fori_loop(0, 3, two_weights, 0)

    @pl.when(step == pl.num_programs(0) - 1)
    def _():
        g2_ref[...] = jnp.zeros(g2_ref.shape, F32)
        g3_ref[...] = jnp.zeros(g3_ref.shape, F32)
        for i in range(4):
            k = 256 * i
            total = r2_ref[k : k + 128, 0:128]
            total = total + pltpu.roll(r2_ref[k + 64 : k + 192, 0:128], 64, 1)
            g2_ref[128 * i : 128 * i + 128] = total + r2_ref[k + 128 : k + 256, 128:256]
        for i in range(3):
            k = 384 * i
            total = r3_ref[k : k + 192, 0:128]
            total = total + pltpu.roll(r3_ref[k + 64 : k + 256, 0:128], 64, 1)
            total = total + r3_ref[k + 128 : k + 320, 128:256]
            total = total + pltpu.roll(r3_ref[k + 192 : k + 384, 128:256], 64, 1)
            g3_ref[192 * i : 192 * i + 192] = total
        row = r2_ref[1024:1032]
        row = row[:, 0:128] + pltpu.roll(row[:, 0:128], 64, 1) + row[:, 128:256]
        g2_ref[512:513] = row[0:1]
        row = r3_ref[1152:1160]
        row = row[:, 0:128] + row[:, 128:256]
        g3_ref[576:577] = (row + pltpu.roll(row, 64, 1))[0:1]
        lane = lax.broadcasted_iota(jnp.int32, (1, HID), 1)
        packed_ref[...] = jnp.zeros(packed_ref.shape, F32)
        for ref, rows, base, phase in ((g2_ref, 72, 16, 32), (g3_ref, 80, 80, 96)):
            turned = pltpu.roll(jnp.concatenate(fold(ref, 64, rows), axis=1), phase, 1)
            for j in range(4):
                cols = slice(128 * j, 128 * j + 128)
                here = pl.ds(4 * base + j, rows, stride=4)
                packed_ref[here, :] += jnp.where(lane >= phase, turned, 0.0)[:, cols]
                if j == 0:
                    below = pl.ds(4 * base + 4, rows, stride=4)
                    packed_ref[below, :] += jnp.where(lane < phase, turned, 0.0)[:, cols]


def upper_backward(a1, a2, a3, w_dense, d_hidden, t3):
    frames = a1.shape[3]
    return pl.pallas_call(
        upper_body,
        grid=(frames // 256,),
        in_specs=[
            pl.BlockSpec(memory_space=pl.ANY),
            pl.BlockSpec((9, 10, C2, 256), lambda j: (0, 0, 0, j)),
            pl.BlockSpec((7, 7, C3, 256), lambda j: (0, 0, 0, j)),
            whole((FEATURES, HID)),
            pl.BlockSpec((HID, 256), lambda j: (0, j)),
            whole((192, 192)),
        ],
        out_specs=[
            pl.BlockSpec((11, 11, C2, 256), lambda j: (0, 0, 0, j)),
            whole((4 * BLOCK_ROWS, 128)),
        ],
        out_shape=[
            jax.ShapeDtypeStruct((11, 11, C2, frames), BF16),
            jax.ShapeDtypeStruct((4 * BLOCK_ROWS, 128), F32),
        ],
        scratch_shapes=[
            pltpu.VMEM((1040, 256), F32),
            pltpu.VMEM((1168, 256), F32),
            pltpu.VMEM((20, 20, C1, 256), BF16),
            pltpu.VMEM((11, 8, C3, 256), BF16),
            pltpu.VMEM((640, 128), F32),
            pltpu.VMEM((640, 128), F32),
            pltpu.SemaphoreType.DMA((1,)),
        ],
        compiler_params=pltpu.CompilerParams(vmem_limit_bytes=VMEM_LIMIT),
        name="upper_backward",
    )(a1, a2, a3, w_dense, d_hidden, t3)


def lower_body(
    x0, x1, x2, x3, x4, a1_ref, d2_ref, t2_ref, packed_ref, r1_ref, g1_ref, d1_ref
):
    x_refs = (x0, x1, x2, x3, x4)
    t = pl.program_id(1)

    @pl.when((pl.program_id(0) == 0) & (t == 0))
    def _():
        r1_ref[...] = jnp.zeros(r1_ref.shape, F32)

    zero = jnp.zeros((), BF16)
    for h in range(2):
        held = None
        for n in range(10):
            back = held
            if n < 9:
                got = mm(t2_ref[...], d2_ref[pl.ds(2 * t + h, 2), n + 1].reshape(128, 256))
                back = got[0:128] if n == 0 else held + got[0:128]
                held = got[128:256]
            for x in range(2):
                for y in range(2):
                    k = 32 * (2 * x + y)
                    kept = a1_ref[2 * h + y, 2 * n + x] > 0
                    masked = jnp.where(kept, back[k : k + 32].astype(BF16), zero)
                    row = 128 * (n % 2) + k
                    d1_ref[h, row : row + 32, 256 * (n // 2) : 256 * (n // 2) + 256] = masked
        window = jnp.concatenate(
            [pixel_window(x_refs, 2 * h, 64 * n, 80) for n in range(5)], axis=1
        )
        window = jnp.concatenate([window, jnp.ones((16, window.shape[1]), BF16)], axis=0)
        r1_ref[...] += mm_nt(window, d1_ref[h])

    @pl.when((pl.program_id(0) == pl.num_programs(0) - 1) & (t == 4))
    def _():
        g1_ref[...] = jnp.zeros(g1_ref.shape, F32)
        for i in range(8):
            total = 0.0
            for p in range(2):
                for q in range(4):
                    k = (i + 4 * p) * 80 + 16 * q
                    col = 128 * (q // 2)
                    turn = 64 * (q % 2) + 32 * p
                    slab = r1_ref[k : k + 32, col : col + 128]
                    total = total + (pltpu.roll(slab, 128 - turn, 1) if turn else slab)
            g1_ref[32 * i : 32 * i + 32] = total
        row = r1_ref[960:968, 0:128] + r1_ref[960:968, 128:256]
        row = row + pltpu.roll(row, 64, 1)
        g1_ref[256:257] = (row + pltpu.roll(row, 96, 1))[0:1]
        packed_ref[...] = jnp.zeros(packed_ref.shape, F32)
        for j, part in enumerate(fold(g1_ref, 32, 24)):
            packed_ref[pl.ds(j, 24, stride=4), :] = part


def lower_backward(x, a1, d2, t2):
    envs = x.shape[0]
    return pl.pallas_call(
        lower_body,
        grid=(envs // 2, 5),
        in_specs=pixel_specs()
        + [
            pl.BlockSpec((4, 20, C1, 256), lambda j, t: (t, 0, 0, j)),
            pl.BlockSpec((11, 11, C2, 256), lambda j, t: (0, 0, 0, j)),
            whole((256, 128)),
        ],
        out_specs=whole((4 * BLOCK_ROWS, 128)),
        out_shape=jax.ShapeDtypeStruct((4 * BLOCK_ROWS, 128), F32),
        scratch_shapes=[
            pltpu.VMEM((976, 256), F32),
            pltpu.VMEM((384, 128), F32),
            pltpu.VMEM((2, 256, 1280), BF16),
        ],
        compiler_params=pltpu.CompilerParams(vmem_limit_bytes=VMEM_LIMIT),
        name="lower_backward",
    )(x, x, x, x, x, a1, d2, t2)


def swap(value, lanes, step):
    return lax.ppermute(value, "dp", [(i, i ^ step) for i in range(lanes)])


def halving_order(lanes):
    return [1 << k for k in range(lanes.bit_length() - 1)]


def sum_everywhere(value, lanes):
    for step in halving_order(lanes):
        value = value + swap(value, lanes, step)
    return value


def scatter_sum(blocks, lanes, place):
    for step in halving_order(lanes):
        pairs = blocks.reshape((blocks.shape[0] // 2, 2) + blocks.shape[1:])
        high = (place // step) % 2 == 1
        kept = jnp.where(high, pairs[:, 1], pairs[:, 0])
        sent = jnp.where(high, pairs[:, 0], pairs[:, 1])
        blocks = kept + swap(sent, lanes, step)
    return blocks[0]


def gather_blocks(block, beside, lanes, place):
    blocks = block[None]
    arrived = []
    for k, step in enumerate(reversed(halving_order(lanes))):
        other = swap(blocks, lanes, step)
        if k < len(beside):
            other, part = lax.optimization_barrier((other, beside[k]))
            arrived.append(part)
        if step == 1:
            return blocks, other, arrived
        high = (place // step) % 2 == 1
        blocks = jnp.stack(
            [jnp.where(high, other, blocks), jnp.where(high, blocks, other)], axis=1
        ).reshape((2 * blocks.shape[0],) + blocks.shape[1:])


def first_rows_everywhere(master, sums, lanes, place):
    rows = master.shape[0] // HID
    owners = -(-(TOP + 1) // rows)
    order = halving_order(lanes)
    if owners == 1:
        block = master[: BLOCK_ROWS * HID].reshape(BLOCK_ROWS, HID).astype(BF16)
        row = lax.broadcasted_iota(jnp.int32, (BLOCK_ROWS, 1), 0)
        block = jnp.where((place == 0) & (row <= TOP), block, jnp.zeros((), BF16))
        steps = list(reversed(order))
        left = list(order)
        while steps:
            now, steps = steps[:2], steps[2:]
            jumps = now if len(now) == 1 else [now[0], now[1], now[0] + now[1]]
            total = block
            for jump in jumps:
                pairs = [(i, i + jump) for i in range(0, lanes, 2 * now[0])]
                total = total + lax.ppermute(block, "dp", pairs)
            summed = sums + swap(sums, lanes, left.pop(0))
            block, sums = lax.optimization_barrier((total, summed))
        return block, sums, left
    local = master.reshape(rows, HID).astype(BF16)
    block = jnp.zeros((owners, rows, HID), BF16)
    block = jnp.where(jnp.arange(owners)[:, None, None] == place, local[None], block)
    block = sum_everywhere(block, lanes).reshape(owners * rows, HID)[: TOP + 1]
    return jnp.pad(block, ((0, BLOCK_ROWS - TOP - 1), (0, 0))), sums, order


def finish_blocks(own_len):
    block = min(208, -(-own_len // 8) * 8)
    return block, -(-own_len // block)


def facts_body(dense_ref, piece_ref, loss_ref, message_ref, *part_refs):
    dense = dense_ref[...]
    piece = piece_ref[...]
    start = 0
    for ref in part_refs:
        ref[...] = dense[start : start + ref.shape[0]]
        start += ref.shape[0]
    squares = jnp.sum(dense * dense, axis=0, keepdims=True)
    squares = squares + jnp.sum(piece * piece, axis=0, keepdims=True)
    squares = jnp.sum(squares, axis=1, keepdims=True)
    height = piece.shape[0]
    message_ref[0:height] = piece
    row = lax.broadcasted_iota(jnp.int32, (8, 128), 0)
    message_ref[height : height + 8] = jnp.where(row == 0, squares, loss_ref[...])


def facts_message(dense, piece, loss):
    own_len = dense.shape[0]
    block, steps = finish_blocks(own_len)
    first = block * (steps // 2)
    lengths = [length for length in (first, own_len - first) if length]
    shapes = [(piece.shape[0] + 8, 128)] + [(length, 128) for length in lengths]
    message, *parts = pl.pallas_call(
        facts_body,
        out_shape=[jax.ShapeDtypeStruct(shape, F32) for shape in shapes],
        name="facts_message",
    )(dense, piece, loss)
    return message, parts


def finish_body(
    parts,
    own_len,
    switch,
    place_ref,
    scalars_ref,
    near_ref,
    far_ref,
    low_other_ref,
    high_other_ref,
    mine_ref,
    first_ref,
    other_first_ref,
    second_ref,
    other_second_ref,
    master_ref,
    momentum_ref,
    clipped_ref,
    first_out,
    second_out,
    moved_ref,
    momentum_out,
    final_ref,
    low_ref,
    norm_ref,
    loss_ref,
    extra_ref,
):
    height = near_ref.shape[2] - 8
    place = place_ref[0]
    first_step = pl.program_id(0) == 0

    @pl.when(first_step)
    def _():
        extra_ref[...] = jnp.zeros(extra_ref.shape, F32)

    for start, stop, target in parts:
        for owner in range(target // own_len, (target + stop - start - 1) // own_len + 1):
            shift = target - start - owner * own_len
            low = max(start, -shift)
            high = min(stop, own_len - shift)

            @pl.when(first_step & (place == owner))
            def _(owner=owner, shift=shift, low=low, high=high):
                for k in range(low // height, (high - 1) // height + 1):
                    a = max(low, k * height)
                    b = min(high, (k + 1) * height)
                    source = near_ref if k % 2 == owner % 2 else far_ref
                    for g in range(2):
                        extra_ref[g, a + shift : b + shift] = source[
                            k // 2, g, a - k * height : b - k * height
                        ]

    block = master_ref.shape[0]
    here = pl.ds(pl.multiple_of(block * pl.program_id(0), 8), block)

    factors = []
    for g in range(2):
        facts = jnp.sum(near_ref[:, g, height : height + 8, :], axis=0)
        facts = facts + jnp.sum(far_ref[:, g, height : height + 8, :], axis=0)
        norm = jnp.sqrt(facts[0:1, 0:1])
        factors.append(jnp.minimum(1.0, CLIP_NORM / (norm + 1e-06)))
        if g == 0:
            norm_ref[...] = norm
            loss_ref[...] = facts[1:2, 0:1]
    master = master_ref[...]

    def inner_step(g, dense, one_ref, two_ref):
        clipped = (dense + extra_ref[g, here]) * factors[g]
        first_next = BETA_ONE * one_ref[...] + (1.0 - BETA_ONE) * clipped
        second_next = BETA_TWO * two_ref[...] + (1.0 - BETA_TWO) * clipped * clipped
        first_hat = first_next / scalars_ref[0]
        second_hat = second_next / scalars_ref[1]
        inner = master - LEARN_RATE * (
            first_hat / (jnp.sqrt(second_hat) + ADAM_EPSILON) + WEIGHT_DECAY * master
        )
        return clipped, first_next, second_next, master - inner

    clipped, first_next, second_next, drift = inner_step(0, mine_ref[...], first_ref, second_ref)
    clipped_ref[:, 0, :] = clipped
    first_out[:, 0, :] = first_next
    second_out[:, 0, :] = second_next
    other = jnp.where(pl.program_id(0) < switch, low_other_ref[...], high_other_ref[...])
    _, _, _, other_drift = inner_step(1, other, other_first_ref, other_second_ref)
    moved = (drift + other_drift) / 2.0
    moved_ref[...] = moved
    momentum_next = OUTER_MOMENTUM * momentum_ref[...] + moved
    momentum_out[...] = momentum_next
    final = master - OUTER_RATE * (moved + OUTER_MOMENTUM * momentum_next)
    final_ref[...] = final
    low_ref[...] = final.astype(BF16)


def finish(parts, place, scalars, near, far, others, *arrays):
    own_len = arrays[0].shape[0]
    block, steps = finish_blocks(own_len)
    scalar = pl.BlockSpec(memory_space=pltpu.SMEM)

    def spec(array):
        if len(array.shape) == 3:
            return pl.BlockSpec((block, 1, 128), lambda k: (k, 0, 0))
        return pl.BlockSpec((block, 128), lambda k: (k, 0))

    outs = [jax.ShapeDtypeStruct((own_len, 1, 128), F32)] * 3
    outs += [jax.ShapeDtypeStruct((own_len, 128), F32)] * 3
    outs += [jax.ShapeDtypeStruct((own_len, 128), BF16)]
    return pl.pallas_call(
        lambda *refs: finish_body(parts, own_len, steps // 2, *refs),
        grid=(steps,),
        in_specs=[scalar, scalar, whole(near.shape), whole(far.shape)]
        + [
            pl.BlockSpec((block, 128), lambda k: (jnp.minimum(k, max(steps // 2 - 1, 0)), 0)),
            pl.BlockSpec((block, 128), lambda k: (jnp.maximum(k - steps // 2, 0), 0)),
        ]
        + [spec(array) for array in arrays],
        out_specs=[spec(array) for array in outs] + [whole((1, 1))] * 2,
        out_shape=outs + [jax.ShapeDtypeStruct((1, 1), F32)] * 2,
        scratch_shapes=[pltpu.VMEM((2, block * steps, 128), F32)],
        name="finish",
    )(place, scalars, near, far, *others, *arrays)


def on_device(
    frames,
    actions,
    rewards,
    old_values,
    next_values,
    terminal,
    truncated,
    behavior_logprob,
    master,
    first_moment,
    second_moment,
    outer_momentum,
    step_count,
):
    lanes = lax.axis_size("dp")
    place = lax.axis_index("dp")
    shard_len = master.shape[0]
    rows = shard_len // HID
    groups = lax.axis_size("group")
    assert groups == 2 and rows * HID == shard_len and frames.shape[2] == 128

    def other_group(value):
        return lax.ppermute(value, "group", [(0, 1), (1, 0)])

    master_rows = master.reshape(rows, HID)
    low_rows = master_rows.astype(BF16)
    gathered = lax.all_gather(low_rows, "dp", axis=0)

    advantage, sums = trajectory_advantages(
        rewards[0], old_values[0], next_values[0], terminal[0], truncated[0]
    )
    envs_here, steps_here = advantage.shape
    batch = envs_here * steps_here
    total_frames = batch * lanes
    block, sums, left = first_rows_everywhere(master, sums, lanes, place)
    while len(left) > 2:
        sums = sums + swap(sums, lanes, left.pop(0))
    x = frames[0].transpose(0, 2, 3, 1)
    came = swap(sums, lanes, left.pop(0)) if left else jnp.zeros_like(sums)
    t1, b1, t2, b2, t3, b3, back3, back2 = conv_weights(block)
    t1, came = lax.optimization_barrier((t1, came))
    sums = sums + came
    came = swap(sums, lanes, left.pop(0)) if left else jnp.zeros_like(sums)
    a1, a2, a3 = conv_forward(x, t1, b1, t2, b2, t3, b3)
    a3, came = lax.optimization_barrier((a3, came))
    sums = sums + came

    tail = TOP + FEATURES + 1
    head_owner = tail // rows
    head_flat = gathered[head_owner:].reshape((lanes - head_owner) * rows, HID)
    head_flat = head_flat[tail - head_owner * rows :].reshape(-1)[PHASE : PHASE + HEAD_LEN]
    head = jnp.pad(head_flat.reshape(HID + 1, ACTIONS + 1), ((0, 7), (0, 127 - ACTIONS)))
    packed_dense, w_dense, d_hidden, g_head, g_head_bias, loss_local = dense_step(
        1.0 / total_frames,
        a3.reshape(FEATURES, batch),
        gathered,
        head,
        sums,
        advantage,
        old_values[0],
        actions[0],
        behavior_logprob[0],
    )
    dense_owned = lax.psum_scatter(packed_dense, "dp", scatter_dimension=0, tiled=False)
    d_hidden, first_sent, second_sent = lax.optimization_barrier(
        (d_hidden, first_moment, second_moment)
    )
    d2, upper = upper_backward(a1, a2, a3, w_dense, d_hidden, back3)
    first_flat = first_sent.reshape(shard_len)
    second_flat = second_sent.reshape(shard_len)
    d2, other_first, other_second = lax.optimization_barrier(
        (d2, other_group(first_flat), other_group(second_flat))
    )
    lower = lower_backward(x, a1, d2, back2)

    tail_rows = lanes * rows - tail
    head_part = jnp.concatenate(
        [
            jnp.zeros((PHASE,), F32),
            jnp.roll(g_head[: ACTIONS + 1].T, -PHASE, axis=0).reshape(-1),
            g_head_bias[: ACTIONS + 1, 0],
            jnp.zeros((tail_rows * HID - PHASE - HEAD_LEN,), F32),
        ]
    ).reshape(4 * tail_rows, 128)
    real = 4 * (BLOCK_ROWS + tail_rows)
    count = -(-real // (8 * lanes)) * 8 * lanes
    head_part = jnp.pad(head_part, ((0, count - real), (0, 0)))
    small = jnp.concatenate([lower + upper, head_part], axis=0)
    piece = scatter_sum(small.reshape(lanes, count // lanes, 128), lanes, place)
    message, dense_parts = facts_message(dense_owned, piece, loss_local)
    both = jnp.stack([message, other_group(message)])
    both, *dense_parts = lax.optimization_barrier((both, *dense_parts))
    near, far, dense_parts = gather_blocks(
        both, [other_group(part) for part in dense_parts], lanes, place
    )

    own_len = 4 * rows
    moment_step = step_count[0].astype(F32)
    scalars = jnp.stack(
        [1.0 - jnp.power(BETA_ONE, moment_step), 1.0 - jnp.power(BETA_TWO, moment_step)]
    )
    parts = ((0, 4 * (TOP + 1), 0), (4 * BLOCK_ROWS, real, 4 * tail))

    def view(value):
        return value.reshape(own_len, 128)

    results = finish(
        parts,
        place.reshape(1),
        scalars,
        near,
        far,
        (dense_parts[0], dense_parts[-1]),
        dense_owned,
        view(first_flat),
        view(other_first),
        view(second_flat),
        view(other_second),
        view(master),
        view(outer_momentum),
    )
    clipped, first_next, second_next, moved, momentum_next, final, final_low, norm, loss = results
    return (
        clipped.reshape(1, shard_len),
        norm.reshape(1),
        loss.reshape(1),
        first_next.reshape(1, shard_len),
        second_next.reshape(1, shard_len),
        moved.reshape(shard_len),
        momentum_next.reshape(shard_len),
        final.reshape(shard_len),
        final_low.reshape(shard_len),
    )


def solution(mesh):
    return jax.shard_map(
        on_device,
        mesh=mesh,
        in_specs=(
            P("group", "dp", None, None, None),
            P("group", "dp", None),
            P("group", "dp", None),
            P("group", "dp", None),
            P("group", "dp", None),
            P("group", "dp", None),
            P("group", "dp", None),
            P("group", "dp", None),
            P("dp"),
            P("group", "dp"),
            P("group", "dp"),
            P("dp"),
            P(),
        ),
        out_specs=(
            P("group", "dp"),
            P("group"),
            P("group"),
            P("group", "dp"),
            P("group", "dp"),
            P("dp"),
            P("dp"),
            P("dp"),
            P("dp"),
        ),
        check_vma=False,
    )
```

```python
import math

import jax
import jax.numpy as jnp
from jax import lax
from jax.experimental import pallas as pl
from jax.experimental.pallas import tpu as pltpu
from jax.sharding import PartitionSpec as P

C1 = 32
C2 = 64
C3 = 64
HID = 512
ACTIONS = 18
PARAMS = 1693875
FEATURES = 49 * C3
CONV_LEN = 256 * C1 + C1 + 16 * C1 * C2 + C2 + 9 * C2 * C3 + C3
TOP = CONV_LEN // HID
LEAD = (TOP + 8) // 8 * 8
BLOCK_ROWS = LEAD + 8
PHASE = CONV_LEN % HID
HEAD_LEN = HID * (ACTIONS + 1) + ACTIONS + 1

BETA_ONE = 0.9
BETA_TWO = 0.999
ADAM_EPSILON = 1e-08
LEARN_RATE = 0.005
WEIGHT_DECAY = 0.01
CLIP_NORM = 0.5
OUTER_RATE = 0.7
OUTER_MOMENTUM = 0.9
DISCOUNT = 0.99
TRACE_DECAY = 0.95
RATIO_CLIP = 0.1
VALUE_COEF = 0.5
ENTROPY_COEF = 0.01

F32 = jnp.float32
BF16 = jnp.bfloat16
VMEM_LIMIT = 63 * 1024 * 1024


def mm(a, b):
    return jnp.dot(a, b, preferred_element_type=F32)


def mm_nt(a, b):
    return lax.dot_general(a, b, (((1,), (1,)), ((), ())), preferred_element_type=F32)


def mm_tn(a, b):
    return lax.dot_general(a, b, (((0,), (0,)), ((), ())), preferred_element_type=F32)


def advantage_body(rewards_ref, values_ref, next_ref, terminal_ref, truncated_ref, out_ref, sums_ref):
    values = values_ref[...]
    steps = values.shape[1]
    lane = lax.broadcasted_iota(jnp.int32, values.shape, 1)
    alive = 1.0 - terminal_ref[...].astype(F32)
    cutoff = truncated_ref[...].astype(F32)
    following = jnp.where(lane < steps - 1, pltpu.roll(values, steps - 1, 1), next_ref[...])
    following = cutoff * next_ref[...] + (1.0 - cutoff) * following
    series = rewards_ref[...] + DISCOUNT * alive * following - values
    keeping = DISCOUNT * TRACE_DECAY * alive * (1.0 - cutoff)
    step = 1
    while step < steps:
        inside = lane < steps - step
        series = series + keeping * jnp.where(inside, pltpu.roll(series, steps - step, 1), 0.0)
        keeping = keeping * jnp.where(inside, pltpu.roll(keeping, steps - step, 1), 0.0)
        step *= 2
    out_ref[...] = series
    first = jnp.sum(jnp.sum(series, axis=0, keepdims=True), axis=1, keepdims=True)
    square = jnp.sum(jnp.sum(series * series, axis=0, keepdims=True), axis=1, keepdims=True)
    place = lax.broadcasted_iota(jnp.int32, (8, 128), 0)
    sums_ref[...] = jnp.where(place == 0, first, square)


def trajectory_advantages(rewards, values, next_values, terminal, truncated):
    return pl.pallas_call(
        advantage_body,
        out_shape=[
            jax.ShapeDtypeStruct(rewards.shape, F32),
            jax.ShapeDtypeStruct((8, 128), F32),
        ],
        name="advantages",
    )(rewards, values, next_values, terminal, truncated)


def unfold(block, phase, width, rows):
    lane = lax.broadcasted_iota(jnp.int32, (1, HID), 1)
    if phase:
        turned = pltpu.roll(block, HID - phase, 1)
        block = jnp.where(lane < HID - phase, turned[:rows], turned[1 : rows + 1])
    pieces = []
    for k in range(HID // width):
        start = k * width // 128 * 128
        piece = block[:rows, start : start + 128]
        turn = k * width % 128
        pieces.append(pltpu.roll(piece, 128 - turn, 1) if turn else piece)
    return pieces


def weights_body(
    conv_ref,
    t1_ref,
    b1_ref,
    t2_ref,
    b2_ref,
    t3_ref,
    b3_ref,
    back3_ref,
    back2_ref,
    wide_ref,
    w1_ref,
    w2_ref,
    w3_ref,
):
    wide_ref[...] = conv_ref[...].astype(F32)
    for k, piece in enumerate(unfold(wide_ref[0:24], 0, C1, 24)):
        w1_ref[pl.ds(k, 24, stride=16), :] = piece
    for k, piece in enumerate(unfold(wide_ref[16:96], 32, C2, 72)):
        w2_ref[pl.ds(k, 72, stride=8), :] = piece
    for k, piece in enumerate(unfold(wide_ref[80:168], 96, C3, 80)):
        w3_ref[pl.ds(k, 80, stride=8), :] = piece
    w1 = w1_ref[...].T
    w2 = w2_ref[...].T
    w3 = w3_ref[...].T
    w1_low = w1.astype(BF16)
    w2_low = w2.astype(BF16)
    w3_low = w3.astype(BF16)
    t1_ref[...] = jnp.zeros(t1_ref.shape, BF16)
    for q in range(2):
        for p in range(2):
            row = 64 * q + 32 * p
            for i in range(8):
                lane = (i + 4 * p) * 16
                k = 32 * i + 16 * q
                t1_ref[row : row + 32, lane : lane + 16] = w1_low[0:32, k : k + 16]
    for p in range(2):
        b1_ref[32 * p : 32 * p + 32] = jnp.broadcast_to(w1[0:32, 256:257], (32, 256))
    b2_ref[...] = jnp.broadcast_to(w2[0:64, 512:513], (64, 256))
    b3_ref[...] = jnp.broadcast_to(w3[0:64, 576:577], (64, 256))
    for q in range(2):
        for i in range(4):
            k = 128 * i + 64 * q
            t2_ref[64 * q : 64 * q + 64, 64 * i : 64 * i + 64] = w2_low[0:64, k : k + 64]
    for j in range(3):
        for i in range(3):
            here = (slice(64 * j, 64 * j + 64), slice(64 * i, 64 * i + 64))
            k = (3 * i + j) * 64
            t3_ref[here] = w3_low[0:64, k : k + 64]
            k = (3 * (2 - i) + j) * 64
            back3_ref[here] = w3_ref[k : k + 64, 0:64].astype(BF16)
    for x in range(4):
        for y in range(2):
            for r in range(2):
                k = ((y + 2 - 2 * r) * 4 + x) * 32
                row = 32 * (2 * x + y)
                back2_ref[row : row + 32, 64 * r : 64 * r + 64] = w2_ref[k : k + 32, 0:64].astype(
                    BF16
                )


def conv_weights(block):
    shapes = [
        ((128, 192), BF16),
        ((64, 256), F32),
        ((128, 256), BF16),
        ((64, 256), F32),
        ((192, 192), BF16),
        ((64, 256), F32),
        ((192, 192), BF16),
        ((256, 128), BF16),
    ]
    return pl.pallas_call(
        weights_body,
        out_shape=[jax.ShapeDtypeStruct(shape, kind) for shape, kind in shapes],
        scratch_shapes=[
            pltpu.VMEM((BLOCK_ROWS, HID), F32),
            pltpu.VMEM((384, 128), F32),
            pltpu.VMEM((640, 128), F32),
            pltpu.VMEM((640, 128), F32),
        ],
        compiler_params=pltpu.CompilerParams(vmem_limit_bytes=VMEM_LIMIT),
        name="conv_weights",
    )(block)


def pixel_window(x_refs, first, start, width):
    sides = []
    for e in range(2):
        parts = [x_refs[first + k][e, :, start : start + width, :] for k in range(3)]
        sides.append(jnp.concatenate(parts, axis=0).reshape(12 * width, 128))
    return jnp.concatenate(sides, axis=1)


def forward_body(
    x_hbm,
    t1_ref,
    b1_ref,
    t2_ref,
    b2_ref,
    t3_ref,
    b3_ref,
    a1_hbm,
    a2_ref,
    a3_ref,
    x_ref,
    a1_ref,
    x_sems,
    sem,
):
    pair = pl.program_id(0)
    lanes = pl.ds(pl.multiple_of(256 * pair, 256), 256)

    def load(j, c):
        part = pl.ds(12 * c, 12)
        return pltpu.make_async_copy(
            x_hbm.at[pl.ds(2 * j, 2), part], x_ref.at[j, :, part], x_sems.at[7 * j + c]
        )

    @pl.when(pair == 0)
    def _():
        for j in range(x_ref.shape[0]):
            for c in range(7):
                load(j, c).start()

    def low(value, bias_ref):
        return jnp.maximum(value + bias_ref[...], 0.0).astype(BF16)

    ready = 0
    for m in range(10):
        while m % 2 == 0 and 12 * ready < 8 * m + 20:
            load(pair, ready).wait()
            ready += 1
        held = None
        for n in range(21):
            window = jnp.concatenate(
                [
                    x_ref[pair, e, 8 * m : 8 * m + 12, 16 * n : 16 * n + 16, :].reshape(192, 128)
                    for e in range(2)
                ],
                axis=1,
            )
            got = mm(t1_ref[...], window)
            if n > 0:
                out = low(held + got[64:128], b1_ref)
                a1_ref[2 * m : 2 * m + 2, n - 1] = out.reshape(2, C1, 256)
            held = got[0:64]
        if m % 2 == 1:
            here = pl.ds(2 * m - 2, 4)
            pltpu.make_async_copy(a1_ref.at[here], a1_hbm.at[here, :, :, lanes], sem.at[0]).start()

    def conv_two(p, carry):
        held = None
        for n in range(10):
            window = a1_ref[pl.ds(2 * p, 4), 2 * n : 2 * n + 2].reshape(256, 256)
            got = mm(t2_ref[...], window)
            if n > 0:
                a2_ref[p, n - 1] = low(held + got[64:128], b2_ref)
            held = got[0:64]
        a2_ref[p, 9] = jnp.zeros((C2, 256), BF16)
        return carry

    lax.fori_loop(0, 9, conv_two, 0, unroll=3)

    for p in range(7):
        held, older = None, None
        for x in range(9):
            got = mm(t3_ref[...], a2_ref[p : p + 3, x].reshape(192, 256))
            if x > 1:
                a3_ref[p, x - 2] = low(older + got[128:192], b3_ref)
            older = held + got[64:128] if x > 0 else None
            held = got[0:64]
    pltpu.make_async_copy(a1_ref, a1_hbm.at[:, :, :, lanes], sem.at[0]).wait()


def whole(shape):
    return pl.BlockSpec(shape, lambda *j: (0,) * len(shape), pipeline_mode=pl.Buffered(1))


def pixel_specs():
    def spec(k):
        return pl.BlockSpec((2, 4, 336, 128), lambda j, t: (j, 4 * t + k, 0, 0))

    return [spec(k) for k in range(5)]


def conv_forward(x, t1, b1, t2, b2, t3, b3):
    envs = x.shape[0]
    frames = envs * 128
    return pl.pallas_call(
        forward_body,
        grid=(envs // 2,),
        in_specs=[
            pl.BlockSpec(memory_space=pl.ANY),
            whole((128, 192)),
            whole((64, 256)),
            whole((128, 256)),
            whole((64, 256)),
            whole((192, 192)),
            whole((64, 256)),
        ],
        out_specs=[
            pl.BlockSpec(memory_space=pl.ANY),
            pl.BlockSpec((9, 10, C2, 256), lambda j: (0, 0, 0, j)),
            pl.BlockSpec((7, 7, C3, 256), lambda j: (0, 0, 0, j)),
        ],
        out_shape=[
            jax.ShapeDtypeStruct((20, 20, C1, frames), BF16),
            jax.ShapeDtypeStruct((9, 10, C2, frames), BF16),
            jax.ShapeDtypeStruct((7, 7, C3, frames), BF16),
        ],
        scratch_shapes=[
            pltpu.VMEM((envs // 2, 2, 84, 336, 128), BF16),
            pltpu.VMEM((20, 20, C1, 256), BF16),
            pltpu.SemaphoreType.DMA((7 * envs // 2,)),
            pltpu.SemaphoreType.DMA((1,)),
        ],
        compiler_params=pltpu.CompilerParams(vmem_limit_bytes=VMEM_LIMIT),
        name="conv_forward",
    )(x, t1, b1, t2, b2, t3, b3)


def dense_body(
    scale,
    a3_hbm,
    gathered_hbm,
    head_ref,
    sums_ref,
    advantage_ref,
    values_ref,
    actions_ref,
    behavior_ref,
    packed_hbm,
    wd_hbm,
    d_hidden_ref,
    gwh_ref,
    gbh_ref,
    loss_ref,
    wide_ref,
    a3_ref,
    gathered_ref,
    wd_ref,
    packed_ref,
    sems,
):
    shards, rows, _ = gathered_ref.shape
    halves = [slice(0, shards // 2), slice(shards // 2, shards)]
    loads = []
    for h, part in enumerate(halves):
        loads.append(
            pltpu.make_async_copy(gathered_hbm.at[part], gathered_ref.at[part], sems.at[h])
        )
        loads[h].start()
    load_a3 = pltpu.make_async_copy(a3_hbm, a3_ref, sems.at[2])
    load_a3.start()
    late = lax.broadcasted_iota(jnp.int32, (1, HID), 1) >= PHASE
    for h, part in enumerate(halves):
        loads[h].wait()
        for k in range(part.start, part.stop):
            if rows * k <= TOP + 1 + FEATURES and rows * (k + 1) > TOP:
                wide_ref[rows * k : rows * k + rows] = gathered_ref[k].astype(F32)
    for i in range(0, FEATURES, 448):
        wd_ref[i : i + 448] = jnp.where(
            late, wide_ref[TOP + i : TOP + i + 448], wide_ref[TOP + 1 + i : TOP + 449 + i]
        ).astype(BF16)
    store_wd = pltpu.make_async_copy(wd_ref, wd_hbm, sems.at[3])
    store_wd.start()
    bias = jnp.where(
        late,
        wide_ref[TOP + FEATURES : TOP + 1 + FEATURES],
        wide_ref[TOP + 1 + FEATURES : TOP + 2 + FEATURES],
    )
    bias = jnp.broadcast_to(bias, (8, HID)).T[:, 0:1]
    load_a3.wait()
    hidden_pre = mm_tn(wd_ref[...], a3_ref[...]) + bias
    hidden = jnp.maximum(hidden_pre, 0.0).astype(BF16)
    head = head_ref[...].astype(F32).T
    weights = pltpu.roll(head[0:32, 0:HID], PHASE, 1).astype(BF16)
    out = mm(weights, hidden) + head[0:32, HID : HID + 1]
    row = lax.broadcasted_iota(jnp.int32, out.shape, 0)
    is_logit = row < ACTIONS
    logits = jnp.where(is_logit, out, -jnp.inf)
    top = jnp.max(logits, axis=0, keepdims=True)
    shifted = out - top
    exps = jnp.where(is_logit, jnp.exp(shifted), 0.0)
    total = jnp.sum(exps, axis=0, keepdims=True)
    log_probs = jnp.where(is_logit, shifted - jnp.log(total), 0.0)
    probs = jnp.where(is_logit, jnp.exp(log_probs), 0.0)
    value = jnp.sum(jnp.where(row == ACTIONS, out, 0.0), axis=0, keepdims=True)

    def flat(array):
        return jnp.concatenate([array[e : e + 1] for e in range(array.shape[0])], axis=1)

    advantage = flat(advantage_ref[...])
    sums = sums_ref[...]
    mean = sums[0:1, 0:1] * scale
    spread = sums[1:2, 0:1] * scale - mean * mean
    normed = (advantage - mean) * lax.rsqrt(spread + 1e-05)
    returns = advantage + flat(values_ref[...])
    chosen = row == flat(actions_ref[...])
    taken = jnp.sum(jnp.where(chosen, log_probs, 0.0), axis=0, keepdims=True)
    ratio = jnp.exp(taken - flat(behavior_ref[...]))
    low = 1.0 - RATIO_CLIP
    high = 1.0 + RATIO_CLIP
    clipped = jnp.clip(ratio, low, high)
    plain = ratio * normed
    cut = clipped * normed
    entropy = -jnp.sum(probs * log_probs, axis=0, keepdims=True)
    error = value - returns
    losses = -jnp.minimum(plain, cut) + 0.5 * VALUE_COEF * error * error - ENTROPY_COEF * entropy
    loss_ref[...] = jnp.sum(losses, axis=1, keepdims=True) * scale
    plain_share = jnp.where(plain < cut, 1.0, jnp.where(plain == cut, 0.5, 0.0))
    inside = jnp.where(
        (ratio > low) & (ratio < high), 1.0, jnp.where((ratio == low) | (ratio == high), 0.5, 0.0)
    )
    d_taken = -scale * normed * ratio * (plain_share + (1.0 - plain_share) * inside)
    d_logits = d_taken * (jnp.where(chosen, 1.0, 0.0) - probs) + (scale * ENTROPY_COEF) * probs * (
        log_probs + entropy
    )
    d_value = scale * VALUE_COEF * error
    d_out = jnp.where(is_logit, d_logits, jnp.where(row == ACTIONS, d_value, 0.0)).astype(BF16)
    gwh_ref[...] = mm_nt(d_out, hidden)
    gbh_ref[...] = jnp.sum(d_out.astype(F32), axis=1, keepdims=True)
    back = mm_tn(weights, d_out)
    d_hidden = jnp.where(hidden > 0, back, 0.0).astype(BF16)
    d_hidden_ref[...] = d_hidden
    last = LEAD + FEATURES
    wide_ref[0:LEAD] = jnp.zeros((LEAD, HID), F32)
    wide_ref[last:] = jnp.zeros((wide_ref.shape[0] - last, HID), F32)
    ones = jnp.ones((8, d_hidden.shape[1]), BF16)
    wide_ref[last : last + 1] = mm_nt(ones, d_hidden)[0:1]
    done = 0
    for i in range(0, FEATURES, 448):
        wide_ref[LEAD + i : LEAD + i + 448] = mm_nt(a3_ref[i : i + 448], d_hidden)
        for k in range(done, shards):
            first = rows * k + LEAD - TOP - 1
            if first + rows >= LEAD + i + 448 and i + 448 < FEATURES:
                break
            done = k + 1
            for j in range(4):
                cols = slice(128 * j, 128 * j + 128)
                early_part = wide_ref[first : first + rows, cols]
                if 128 * j + 128 <= PHASE:
                    part = early_part
                elif 128 * j >= PHASE:
                    part = wide_ref[first + 1 : first + 1 + rows, cols]
                else:
                    part = jnp.where(
                        late[:, cols], wide_ref[first + 1 : first + 1 + rows, cols], early_part
                    )
                packed_ref[k, pl.ds(j, rows, stride=4), :] = part
            pltpu.make_async_copy(packed_ref.at[k], packed_hbm.at[k], sems.at[4]).start()
    store_wd.wait()
    pltpu.make_async_copy(packed_ref, packed_hbm, sems.at[4]).wait()


def dense_step(scale, a3, gathered, head, sums, advantage, values, actions, behavior):
    frames = a3.shape[1]
    shards, shard_rows, _ = gathered.shape
    rows = 32
    here = pl.BlockSpec(memory_space=pltpu.VMEM)
    away = pl.BlockSpec(memory_space=pl.ANY)
    return pl.pallas_call(
        lambda *refs: dense_body(scale, *refs),
        in_specs=[away, away] + [here] * 6,
        out_specs=[away, away] + [here] * 4,
        out_shape=[
            jax.ShapeDtypeStruct((shards, 4 * shard_rows, 128), F32),
            jax.ShapeDtypeStruct((FEATURES, HID), BF16),
            jax.ShapeDtypeStruct((HID, frames), BF16),
            jax.ShapeDtypeStruct((rows, HID), F32),
            jax.ShapeDtypeStruct((rows, 1), F32),
            jax.ShapeDtypeStruct((1, 1), F32),
        ],
        scratch_shapes=[
            pltpu.VMEM((max(shards * shard_rows, TOP + 1 + FEATURES) + 2 * LEAD - TOP, HID), F32),
            pltpu.VMEM(a3.shape, BF16),
            pltpu.VMEM(gathered.shape, BF16),
            pltpu.VMEM((FEATURES, HID), BF16),
            pltpu.VMEM((shards, 4 * shard_rows, 128), F32),
            pltpu.SemaphoreType.DMA((5,)),
        ],
        compiler_params=pltpu.CompilerParams(vmem_limit_bytes=VMEM_LIMIT),
        name="dense_step",
    )(a3, gathered, head, sums, advantage, values, actions, behavior)


def fold(g_ref, width, rows):
    step = HID // width
    lane = lax.broadcasted_iota(jnp.int32, (1, 128), 1)
    columns = []
    for m in range(4):
        total = 0.0
        for t in range(128 // width):
            piece = g_ref[pl.ds(m * 128 // width + t, rows, stride=step), :]
            piece = jnp.where(lane < width, piece, 0.0)
            total = total + (pltpu.roll(piece, width * t, 1) if t else piece)
        columns.append(total)
    return columns


def upper_body(
    a1_hbm,
    a2_ref,
    a3_ref,
    wd_ref,
    d_hidden_ref,
    t3_ref,
    d2_ref,
    packed_ref,
    r2_ref,
    r3_ref,
    a1_ref,
    d3_ref,
    g2_ref,
    g3_ref,
    sems,
):
    step = pl.program_id(0)
    lanes = pl.ds(pl.multiple_of(256 * step, 256), 256)
    load_a1 = pltpu.make_async_copy(a1_hbm.at[:, :, :, lanes], a1_ref, sems.at[0])
    load_a1.start()

    @pl.when(step == 0)
    def _():
        for ref in (r2_ref, r3_ref):
            ref[...] = jnp.zeros(ref.shape, F32)
        for p in (0, 1, 9, 10):
            d3_ref[p] = jnp.zeros((8, C3, 256), BF16)

    for p in (0, 10):
        d2_ref[p, 1:10] = jnp.zeros((9, C2, 256), BF16)
    zero = jnp.zeros((), BF16)
    for p in range(7):
        back = mm(wd_ref[448 * p : 448 * p + 448], d_hidden_ref[...]).reshape(7, C3, 256)
        d3_ref[p + 2, 0:7] = jnp.where(a3_ref[p] > 0, back.astype(BF16), zero)
        d3_ref[p + 2, 7] = jnp.zeros((C3, 256), BF16)

    left = [a2_ref[p : p + 3, 4 * g : 4 * g + 6].reshape(1152, 256) for p in range(7) for g in range(2)]
    right = [d3_ref[p + 2, 4 * g : 4 * g + 4].reshape(256, 256) for p in range(7) for g in range(2)]
    left = jnp.concatenate(left, axis=1)
    left = jnp.concatenate([left, jnp.ones((16, left.shape[1]), BF16)], axis=0)
    r3_ref[...] += mm_nt(left, jnp.concatenate(right, axis=1))

    def three_input(y, carry):
        parts = []
        for x in range(9):
            if x < 7:
                parts.append(mm(t3_ref[...], d3_ref[pl.ds(y, 3), x].reshape(192, 256)))
            back = 0.0
            for j in range(3):
                if 0 <= x - j < 7:
                    back = back + parts[x - j][64 * j : 64 * j + 64]
            d2_ref[y + 1, x + 1] = jnp.where(a2_ref[y, x] > 0, back.astype(BF16), zero)
        return carry

    lax.fori_loop(0, 9, three_input, 0, unroll=3)
    load_a1.wait()

    def two_weights(r, carry):
        left, right = [], []
        for k in range(3):
            p = 3 * r + k
            for g in range(3):
                left.append(a1_ref[pl.ds(2 * p, 4), 6 * g : 6 * g + 8].reshape(1024, 256))
                right.append(d2_ref[p + 1, 1 + 3 * g : 4 + 3 * g].reshape(192, 256))
        left = jnp.concatenate(left, axis=1)
        left = jnp.concatenate([left, jnp.ones((16, left.shape[1]), BF16)], axis=0)
        r2_ref[:, 0:192] += mm_nt(left, jnp.concatenate(right, axis=1))
        return carry

    lax.fori_loop(0, 3, two_weights, 0)

    @pl.when(step == pl.num_programs(0) - 1)
    def _():
        g2_ref[...] = jnp.zeros(g2_ref.shape, F32)
        g3_ref[...] = jnp.zeros(g3_ref.shape, F32)
        for i in range(4):
            k = 256 * i
            total = r2_ref[k : k + 128, 0:128]
            total = total + pltpu.roll(r2_ref[k + 64 : k + 192, 0:128], 64, 1)
            g2_ref[128 * i : 128 * i + 128] = total + r2_ref[k + 128 : k + 256, 128:256]
        for i in range(3):
            k = 384 * i
            total = r3_ref[k : k + 192, 0:128]
            total = total + pltpu.roll(r3_ref[k + 64 : k + 256, 0:128], 64, 1)
            total = total + r3_ref[k + 128 : k + 320, 128:256]
            total = total + pltpu.roll(r3_ref[k + 192 : k + 384, 128:256], 64, 1)
            g3_ref[192 * i : 192 * i + 192] = total
        row = r2_ref[1024:1032]
        row = row[:, 0:128] + pltpu.roll(row[:, 0:128], 64, 1) + row[:, 128:256]
        g2_ref[512:513] = row[0:1]
        row = r3_ref[1152:1160]
        row = row[:, 0:128] + row[:, 128:256]
        g3_ref[576:577] = (row + pltpu.roll(row, 64, 1))[0:1]
        lane = lax.broadcasted_iota(jnp.int32, (1, HID), 1)
        packed_ref[...] = jnp.zeros(packed_ref.shape, F32)
        for ref, rows, base, phase in ((g2_ref, 72, 16, 32), (g3_ref, 80, 80, 96)):
            turned = pltpu.roll(jnp.concatenate(fold(ref, 64, rows), axis=1), phase, 1)
            for j in range(4):
                cols = slice(128 * j, 128 * j + 128)
                here = pl.ds(4 * base + j, rows, stride=4)
                packed_ref[here, :] += jnp.where(lane >= phase, turned, 0.0)[:, cols]
                if j == 0:
                    below = pl.ds(4 * base + 4, rows, stride=4)
                    packed_ref[below, :] += jnp.where(lane < phase, turned, 0.0)[:, cols]


def upper_backward(a1, a2, a3, w_dense, d_hidden, t3):
    frames = a1.shape[3]
    return pl.pallas_call(
        upper_body,
        grid=(frames // 256,),
        in_specs=[
            pl.BlockSpec(memory_space=pl.ANY),
            pl.BlockSpec((9, 10, C2, 256), lambda j: (0, 0, 0, j)),
            pl.BlockSpec((7, 7, C3, 256), lambda j: (0, 0, 0, j)),
            whole((FEATURES, HID)),
            pl.BlockSpec((HID, 256), lambda j: (0, j)),
            whole((192, 192)),
        ],
        out_specs=[
            pl.BlockSpec((11, 11, C2, 256), lambda j: (0, 0, 0, j)),
            whole((4 * BLOCK_ROWS, 128)),
        ],
        out_shape=[
            jax.ShapeDtypeStruct((11, 11, C2, frames), BF16),
            jax.ShapeDtypeStruct((4 * BLOCK_ROWS, 128), F32),
        ],
        scratch_shapes=[
            pltpu.VMEM((1040, 256), F32),
            pltpu.VMEM((1168, 256), F32),
            pltpu.VMEM((20, 20, C1, 256), BF16),
            pltpu.VMEM((11, 8, C3, 256), BF16),
            pltpu.VMEM((640, 128), F32),
            pltpu.VMEM((640, 128), F32),
            pltpu.SemaphoreType.DMA((1,)),
        ],
        compiler_params=pltpu.CompilerParams(vmem_limit_bytes=VMEM_LIMIT),
        name="upper_backward",
    )(a1, a2, a3, w_dense, d_hidden, t3)


def lower_body(
    x0, x1, x2, x3, x4, a1_ref, d2_ref, t2_ref, packed_ref, r1_ref, g1_ref, d1_ref
):
    x_refs = (x0, x1, x2, x3, x4)
    t = pl.program_id(1)

    @pl.when((pl.program_id(0) == 0) & (t == 0))
    def _():
        r1_ref[...] = jnp.zeros(r1_ref.shape, F32)

    zero = jnp.zeros((), BF16)
    for h in range(2):
        held = None
        for n in range(10):
            back = held
            if n < 9:
                got = mm(t2_ref[...], d2_ref[pl.ds(2 * t + h, 2), n + 1].reshape(128, 256))
                back = got[0:128] if n == 0 else held + got[0:128]
                held = got[128:256]
            for x in range(2):
                for y in range(2):
                    k = 32 * (2 * x + y)
                    kept = a1_ref[2 * h + y, 2 * n + x] > 0
                    masked = jnp.where(kept, back[k : k + 32].astype(BF16), zero)
                    row = 128 * (n % 2) + k
                    d1_ref[h, row : row + 32, 256 * (n // 2) : 256 * (n // 2) + 256] = masked
        window = jnp.concatenate(
            [pixel_window(x_refs, 2 * h, 64 * n, 80) for n in range(5)], axis=1
        )
        window = jnp.concatenate([window, jnp.ones((16, window.shape[1]), BF16)], axis=0)
        r1_ref[...] += mm_nt(window, d1_ref[h])

    @pl.when((pl.program_id(0) == pl.num_programs(0) - 1) & (t == 4))
    def _():
        g1_ref[...] = jnp.zeros(g1_ref.shape, F32)
        for i in range(8):
            total = 0.0
            for p in range(2):
                for q in range(4):
                    k = (i + 4 * p) * 80 + 16 * q
                    col = 128 * (q // 2)
                    turn = 64 * (q % 2) + 32 * p
                    slab = r1_ref[k : k + 32, col : col + 128]
                    total = total + (pltpu.roll(slab, 128 - turn, 1) if turn else slab)
            g1_ref[32 * i : 32 * i + 32] = total
        row = r1_ref[960:968, 0:128] + r1_ref[960:968, 128:256]
        row = row + pltpu.roll(row, 64, 1)
        g1_ref[256:257] = (row + pltpu.roll(row, 96, 1))[0:1]
        packed_ref[...] = jnp.zeros(packed_ref.shape, F32)
        for j, part in enumerate(fold(g1_ref, 32, 24)):
            packed_ref[pl.ds(j, 24, stride=4), :] = part


def lower_backward(x, a1, d2, t2):
    envs = x.shape[0]
    return pl.pallas_call(
        lower_body,
        grid=(envs // 2, 5),
        in_specs=pixel_specs()
        + [
            pl.BlockSpec((4, 20, C1, 256), lambda j, t: (t, 0, 0, j)),
            pl.BlockSpec((11, 11, C2, 256), lambda j, t: (0, 0, 0, j)),
            whole((256, 128)),
        ],
        out_specs=whole((4 * BLOCK_ROWS, 128)),
        out_shape=jax.ShapeDtypeStruct((4 * BLOCK_ROWS, 128), F32),
        scratch_shapes=[
            pltpu.VMEM((976, 256), F32),
            pltpu.VMEM((384, 128), F32),
            pltpu.VMEM((2, 256, 1280), BF16),
        ],
        compiler_params=pltpu.CompilerParams(vmem_limit_bytes=VMEM_LIMIT),
        name="lower_backward",
    )(x, x, x, x, x, a1, d2, t2)


def swap(value, lanes, step):
    return lax.ppermute(value, "dp", [(i, i ^ step) for i in range(lanes)])


def other_group(value):
    return lax.ppermute(value, "group", [(0, 1), (1, 0)])


def halving_order(lanes):
    return [1 << k for k in range(lanes.bit_length() - 1)]


def sum_everywhere(value, lanes):
    for step in halving_order(lanes):
        value = value + swap(value, lanes, step)
    return value


def scatter_sum(blocks, lanes, place):
    for step in halving_order(lanes):
        pairs = blocks.reshape((blocks.shape[0] // 2, 2) + blocks.shape[1:])
        high = (place // step) % 2 == 1
        kept = jnp.where(high, pairs[:, 1], pairs[:, 0])
        sent = jnp.where(high, pairs[:, 0], pairs[:, 1])
        blocks = kept + swap(sent, lanes, step)
    return blocks[0]


def gather_blocks(block, beside, lanes, place):
    arrived = []
    for k, step in enumerate(reversed(halving_order(lanes))):
        if k == 0:
            both = [(i, (i ^ step) ^ lanes) for i in range(2 * lanes)]
            blocks = jnp.stack([block, other_group(block)])[None]
            other = jnp.stack(
                [swap(block, lanes, step), lax.ppermute(block, ("group", "dp"), both)]
            )[None]
        else:
            other = swap(blocks, lanes, step)
        if 0 < k <= len(beside):
            other, part = lax.optimization_barrier((other, beside[k - 1]))
            arrived.append(part)
        if step == 1:
            return blocks, other, arrived
        high = (place // step) % 2 == 1
        blocks = jnp.stack(
            [jnp.where(high, other, blocks), jnp.where(high, blocks, other)], axis=1
        ).reshape((2 * blocks.shape[0],) + blocks.shape[1:])


def first_rows_everywhere(master, sums, lanes, place):
    rows = master.shape[0] // HID
    owners = -(-(TOP + 1) // rows)
    order = halving_order(lanes)
    if owners == 1:
        block = master[: BLOCK_ROWS * HID].reshape(BLOCK_ROWS, HID).astype(BF16)
        row = lax.broadcasted_iota(jnp.int32, (BLOCK_ROWS, 1), 0)
        block = jnp.where((place == 0) & (row <= TOP), block, jnp.zeros((), BF16))
        steps = list(reversed(order))
        left = list(order)
        while steps:
            now, steps = steps[:2], steps[2:]
            jumps = now if len(now) == 1 else [now[0], now[1], now[0] + now[1]]
            total = block
            for jump in jumps:
                pairs = [(i, i + jump) for i in range(0, lanes, 2 * now[0])]
                total = total + lax.ppermute(block, "dp", pairs)
            summed = sums + swap(sums, lanes, left.pop(0))
            block, sums = lax.optimization_barrier((total, summed))
        return block, sums, left
    local = master.reshape(rows, HID).astype(BF16)
    block = jnp.zeros((owners, rows, HID), BF16)
    block = jnp.where(jnp.arange(owners)[:, None, None] == place, local[None], block)
    block = sum_everywhere(block, lanes).reshape(owners * rows, HID)[: TOP + 1]
    return jnp.pad(block, ((0, BLOCK_ROWS - TOP - 1), (0, 0))), sums, order


def finish_blocks(own_len):
    block = min(208, -(-own_len // 8) * 8)
    return block, -(-own_len // block)


def facts_body(dense_ref, piece_ref, loss_ref, message_ref, *part_refs):
    dense = dense_ref[...]
    piece = piece_ref[...]
    start = 0
    for ref in part_refs:
        ref[...] = dense[start : start + ref.shape[0]]
        start += ref.shape[0]
    squares = jnp.sum(dense * dense, axis=0, keepdims=True)
    squares = squares + jnp.sum(piece * piece, axis=0, keepdims=True)
    squares = jnp.sum(squares, axis=1, keepdims=True)
    height = piece.shape[0]
    message_ref[0:height] = piece
    row = lax.broadcasted_iota(jnp.int32, (8, 128), 0)
    message_ref[height : height + 8] = jnp.where(row == 0, squares, loss_ref[...])


def facts_message(dense, piece, loss):
    own_len = dense.shape[0]
    block, steps = finish_blocks(own_len)
    first = block * (steps // 2)
    lengths = [length for length in (first, own_len - first) if length]
    shapes = [(piece.shape[0] + 8, 128)] + [(length, 128) for length in lengths]
    message, *parts = pl.pallas_call(
        facts_body,
        out_shape=[jax.ShapeDtypeStruct(shape, F32) for shape in shapes],
        name="facts_message",
    )(dense, piece, loss)
    return message, parts


def finish_body(
    parts,
    own_len,
    switch,
    place_ref,
    scalars_ref,
    near_ref,
    far_ref,
    low_other_ref,
    high_other_ref,
    mine_ref,
    first_ref,
    other_first_ref,
    second_ref,
    other_second_ref,
    master_ref,
    momentum_ref,
    clipped_ref,
    first_out,
    second_out,
    moved_ref,
    momentum_out,
    final_ref,
    low_ref,
    norm_ref,
    loss_ref,
    extra_ref,
):
    height = near_ref.shape[2] - 8
    place = place_ref[0]
    first_step = pl.program_id(0) == 0

    @pl.when(first_step)
    def _():
        extra_ref[...] = jnp.zeros(extra_ref.shape, F32)

    for start, stop, target in parts:
        for owner in range(target // own_len, (target + stop - start - 1) // own_len + 1):
            shift = target - start - owner * own_len
            low = max(start, -shift)
            high = min(stop, own_len - shift)

            @pl.when(first_step & (place == owner))
            def _(owner=owner, shift=shift, low=low, high=high):
                for k in range(low // height, (high - 1) // height + 1):
                    a = max(low, k * height)
                    b = min(high, (k + 1) * height)
                    source = near_ref if k % 2 == owner % 2 else far_ref
                    for g in range(2):
                        extra_ref[g, a + shift : b + shift] = source[
                            k // 2, g, a - k * height : b - k * height
                        ]

    block = master_ref.shape[0]
    here = pl.ds(pl.multiple_of(block * pl.program_id(0), 8), block)

    factors = []
    for g in range(2):
        facts = jnp.sum(near_ref[:, g, height : height + 8, :], axis=0)
        facts = facts + jnp.sum(far_ref[:, g, height : height + 8, :], axis=0)
        norm = jnp.sqrt(facts[0:1, 0:1])
        factors.append(jnp.minimum(1.0, CLIP_NORM / (norm + 1e-06)))
        if g == 0:
            norm_ref[...] = norm
            loss_ref[...] = facts[1:2, 0:1]
    master = master_ref[...]

    def inner_step(g, dense, one_ref, two_ref):
        clipped = (dense + extra_ref[g, here]) * factors[g]
        first_next = BETA_ONE * one_ref[...] + (1.0 - BETA_ONE) * clipped
        second_next = BETA_TWO * two_ref[...] + (1.0 - BETA_TWO) * clipped * clipped
        first_hat = first_next / scalars_ref[0]
        second_hat = second_next / scalars_ref[1]
        inner = master - LEARN_RATE * (
            first_hat / (jnp.sqrt(second_hat) + ADAM_EPSILON) + WEIGHT_DECAY * master
        )
        return clipped, first_next, second_next, master - inner

    clipped, first_next, second_next, drift = inner_step(0, mine_ref[...], first_ref, second_ref)
    clipped_ref[:, 0, :] = clipped
    first_out[:, 0, :] = first_next
    second_out[:, 0, :] = second_next
    other = jnp.where(pl.program_id(0) < switch, low_other_ref[...], high_other_ref[...])
    _, _, _, other_drift = inner_step(1, other, other_first_ref, other_second_ref)
    moved = (drift + other_drift) / 2.0
    moved_ref[...] = moved
    momentum_next = OUTER_MOMENTUM * momentum_ref[...] + moved
    momentum_out[...] = momentum_next
    final = master - OUTER_RATE * (moved + OUTER_MOMENTUM * momentum_next)
    final_ref[...] = final
    low_ref[...] = final.astype(BF16)


def finish(parts, place, scalars, near, far, others, *arrays):
    own_len = arrays[0].shape[0]
    block, steps = finish_blocks(own_len)
    scalar = pl.BlockSpec(memory_space=pltpu.SMEM)

    def spec(array):
        if len(array.shape) == 3:
            return pl.BlockSpec((block, 1, 128), lambda k: (k, 0, 0))
        return pl.BlockSpec((block, 128), lambda k: (k, 0))

    outs = [jax.ShapeDtypeStruct((own_len, 1, 128), F32)] * 3
    outs += [jax.ShapeDtypeStruct((own_len, 128), F32)] * 3
    outs += [jax.ShapeDtypeStruct((own_len, 128), BF16)]
    return pl.pallas_call(
        lambda *refs: finish_body(parts, own_len, steps // 2, *refs),
        grid=(steps,),
        in_specs=[scalar, scalar, whole(near.shape), whole(far.shape)]
        + [
            pl.BlockSpec((block, 128), lambda k: (jnp.minimum(k, max(steps // 2 - 1, 0)), 0)),
            pl.BlockSpec((block, 128), lambda k: (jnp.maximum(k - steps // 2, 0), 0)),
        ]
        + [spec(array) for array in arrays],
        out_specs=[spec(array) for array in outs] + [whole((1, 1))] * 2,
        out_shape=outs + [jax.ShapeDtypeStruct((1, 1), F32)] * 2,
        scratch_shapes=[pltpu.VMEM((2, block * steps, 128), F32)],
        name="finish",
    )(place, scalars, near, far, *others, *arrays)


def on_device(
    frames,
    actions,
    rewards,
    old_values,
    next_values,
    terminal,
    truncated,
    behavior_logprob,
    master,
    first_moment,
    second_moment,
    outer_momentum,
    step_count,
):
    lanes = lax.axis_size("dp")
    place = lax.axis_index("dp")
    shard_len = master.shape[0]
    rows = shard_len // HID
    groups = lax.axis_size("group")
    assert groups == 2 and rows * HID == shard_len and frames.shape[2] == 128

    master_rows = master.reshape(rows, HID)
    low_rows = master_rows.astype(BF16)
    gathered = lax.all_gather(low_rows, "dp", axis=0)

    advantage, sums = trajectory_advantages(
        rewards[0], old_values[0], next_values[0], terminal[0], truncated[0]
    )
    envs_here, steps_here = advantage.shape
    batch = envs_here * steps_here
    total_frames = batch * lanes
    block, sums, left = first_rows_everywhere(master, sums, lanes, place)
    moment_step = step_count[0].astype(F32)
    scalars = jnp.stack(
        [1.0 - jnp.power(BETA_ONE, moment_step), 1.0 - jnp.power(BETA_TWO, moment_step)]
    )
    block, scalars = lax.optimization_barrier((block, scalars))
    while len(left) > 2:
        sums = sums + swap(sums, lanes, left.pop(0))
    x = frames[0].transpose(0, 2, 3, 1)
    came = swap(sums, lanes, left.pop(0)) if left else jnp.zeros_like(sums)
    t1, b1, t2, b2, t3, b3, back3, back2 = conv_weights(block)
    t1, came = lax.optimization_barrier((t1, came))
    sums = sums + came
    came = swap(sums, lanes, left.pop(0)) if left else jnp.zeros_like(sums)
    a1, a2, a3 = conv_forward(x, t1, b1, t2, b2, t3, b3)
    a3, came = lax.optimization_barrier((a3, came))
    sums = sums + came

    tail = TOP + FEATURES + 1
    head_owner = tail // rows
    head_flat = gathered[head_owner:].reshape((lanes - head_owner) * rows, HID)
    head_flat = head_flat[tail - head_owner * rows :].reshape(-1)[PHASE : PHASE + HEAD_LEN]
    head = jnp.pad(head_flat.reshape(HID + 1, ACTIONS + 1), ((0, 7), (0, 127 - ACTIONS)))
    packed_dense, w_dense, d_hidden, g_head, g_head_bias, loss_local = dense_step(
        1.0 / total_frames,
        a3.reshape(FEATURES, batch),
        gathered,
        head,
        sums,
        advantage,
        old_values[0],
        actions[0],
        behavior_logprob[0],
    )
    dense_owned = lax.psum_scatter(packed_dense, "dp", scatter_dimension=0, tiled=False)
    d_hidden, first_sent, second_sent = lax.optimization_barrier(
        (d_hidden, first_moment, second_moment)
    )
    d2, upper = upper_backward(a1, a2, a3, w_dense, d_hidden, back3)
    first_flat = first_sent.reshape(shard_len)
    second_flat = second_sent.reshape(shard_len)
    d2, other_first, other_second = lax.optimization_barrier(
        (d2, other_group(first_flat), other_group(second_flat))
    )
    lower = lower_backward(x, a1, d2, back2)

    tail_rows = lanes * rows - tail
    head_part = jnp.concatenate(
        [
            jnp.zeros((PHASE,), F32),
            jnp.roll(g_head[: ACTIONS + 1].T, -PHASE, axis=0).reshape(-1),
            g_head_bias[: ACTIONS + 1, 0],
            jnp.zeros((tail_rows * HID - PHASE - HEAD_LEN,), F32),
        ]
    ).reshape(4 * tail_rows, 128)
    real = 4 * (BLOCK_ROWS + tail_rows)
    count = -(-real // (8 * lanes)) * 8 * lanes
    head_part = jnp.pad(head_part, ((0, count - real), (0, 0)))
    small = jnp.concatenate([lower + upper, head_part], axis=0)
    piece = scatter_sum(small.reshape(lanes, count // lanes, 128), lanes, place)
    message, dense_parts = facts_message(dense_owned, piece, loss_local)
    near, far, dense_parts = gather_blocks(
        message, [other_group(part) for part in dense_parts], lanes, place
    )

    own_len = 4 * rows
    parts = ((0, 4 * (TOP + 1), 0), (4 * BLOCK_ROWS, real, 4 * tail))

    def view(value):
        return value.reshape(own_len, 128)

    results = finish(
        parts,
        place.reshape(1),
        scalars,
        near,
        far,
        (dense_parts[0], dense_parts[-1]),
        dense_owned,
        view(first_flat),
        view(other_first),
        view(second_flat),
        view(other_second),
        view(master),
        view(outer_momentum),
    )
    clipped, first_next, second_next, moved, momentum_next, final, final_low, norm, loss = results
    return (
        clipped.reshape(1, shard_len),
        norm.reshape(1),
        loss.reshape(1),
        first_next.reshape(1, shard_len),
        second_next.reshape(1, shard_len),
        moved.reshape(shard_len),
        momentum_next.reshape(shard_len),
        final.reshape(shard_len),
        final_low.reshape(shard_len),
    )


def solution(mesh):
    return jax.shard_map(
        on_device,
        mesh=mesh,
        in_specs=(
            P("group", "dp", None, None, None),
            P("group", "dp", None),
            P("group", "dp", None),
            P("group", "dp", None),
            P("group", "dp", None),
            P("group", "dp", None),
            P("group", "dp", None),
            P("group", "dp", None),
            P("dp"),
            P("group", "dp"),
            P("group", "dp"),
            P("dp"),
            P(),
        ),
        out_specs=(
            P("group", "dp"),
            P("group"),
            P("group"),
            P("group", "dp"),
            P("group", "dp"),
            P("dp"),
            P("dp"),
            P("dp"),
            P("dp"),
        ),
        check_vma=False,
    )
```

```python
import math

import jax
import jax.numpy as jnp
from jax import lax
from jax.experimental import pallas as pl
from jax.experimental.pallas import tpu as pltpu
from jax.sharding import PartitionSpec as P

C1 = 32
C2 = 64
C3 = 64
HID = 512
ACTIONS = 18
PARAMS = 1693875
FEATURES = 49 * C3
CONV_LEN = 256 * C1 + C1 + 16 * C1 * C2 + C2 + 9 * C2 * C3 + C3
TOP = CONV_LEN // HID
LEAD = (TOP + 8) // 8 * 8
BLOCK_ROWS = LEAD + 8
PHASE = CONV_LEN % HID
HEAD_LEN = HID * (ACTIONS + 1) + ACTIONS + 1

BETA_ONE = 0.9
BETA_TWO = 0.999
ADAM_EPSILON = 1e-08
LEARN_RATE = 0.005
WEIGHT_DECAY = 0.01
CLIP_NORM = 0.5
OUTER_RATE = 0.7
OUTER_MOMENTUM = 0.9
DISCOUNT = 0.99
TRACE_DECAY = 0.95
RATIO_CLIP = 0.1
VALUE_COEF = 0.5
ENTROPY_COEF = 0.01

F32 = jnp.float32
BF16 = jnp.bfloat16
VMEM_LIMIT = 63 * 1024 * 1024


def mm(a, b):
    return jnp.dot(a, b, preferred_element_type=F32)


def mm_nt(a, b):
    return lax.dot_general(a, b, (((1,), (1,)), ((), ())), preferred_element_type=F32)


def mm_tn(a, b):
    return lax.dot_general(a, b, (((0,), (0,)), ((), ())), preferred_element_type=F32)


def advantage_body(rewards_ref, values_ref, next_ref, terminal_ref, truncated_ref, out_ref, sums_ref):
    values = values_ref[...]
    steps = values.shape[1]
    lane = lax.broadcasted_iota(jnp.int32, values.shape, 1)
    alive = 1.0 - terminal_ref[...].astype(F32)
    cutoff = truncated_ref[...].astype(F32)
    following = jnp.where(lane < steps - 1, pltpu.roll(values, steps - 1, 1), next_ref[...])
    following = cutoff * next_ref[...] + (1.0 - cutoff) * following
    series = rewards_ref[...] + DISCOUNT * alive * following - values
    keeping = DISCOUNT * TRACE_DECAY * alive * (1.0 - cutoff)
    step = 1
    while step < steps:
        inside = lane < steps - step
        series = series + keeping * jnp.where(inside, pltpu.roll(series, steps - step, 1), 0.0)
        keeping = keeping * jnp.where(inside, pltpu.roll(keeping, steps - step, 1), 0.0)
        step *= 2
    out_ref[...] = series
    first = jnp.sum(jnp.sum(series, axis=0, keepdims=True), axis=1, keepdims=True)
    square = jnp.sum(jnp.sum(series * series, axis=0, keepdims=True), axis=1, keepdims=True)
    place = lax.broadcasted_iota(jnp.int32, (8, 128), 0)
    sums_ref[...] = jnp.where(place == 0, first, square)


def trajectory_advantages(rewards, values, next_values, terminal, truncated):
    return pl.pallas_call(
        advantage_body,
        out_shape=[
            jax.ShapeDtypeStruct(rewards.shape, F32),
            jax.ShapeDtypeStruct((8, 128), F32),
        ],
        name="advantages",
    )(rewards, values, next_values, terminal, truncated)


def unfold(block, phase, width, rows):
    lane = lax.broadcasted_iota(jnp.int32, (1, HID), 1)
    if phase:
        turned = pltpu.roll(block, HID - phase, 1)
        block = jnp.where(lane < HID - phase, turned[:rows], turned[1 : rows + 1])
    pieces = []
    for k in range(HID // width):
        start = k * width // 128 * 128
        piece = block[:rows, start : start + 128]
        turn = k * width % 128
        pieces.append(pltpu.roll(piece, 128 - turn, 1) if turn else piece)
    return pieces


def weights_body(
    conv_ref,
    t1_ref,
    b1_ref,
    t2_ref,
    b2_ref,
    t3_ref,
    b3_ref,
    back3_ref,
    back2_ref,
    wide_ref,
    w1_ref,
    w2_ref,
    w3_ref,
):
    wide_ref[...] = conv_ref[...].astype(F32)
    for k, piece in enumerate(unfold(wide_ref[0:24], 0, C1, 24)):
        w1_ref[pl.ds(k, 24, stride=16), :] = piece
    for k, piece in enumerate(unfold(wide_ref[16:96], 32, C2, 72)):
        w2_ref[pl.ds(k, 72, stride=8), :] = piece
    for k, piece in enumerate(unfold(wide_ref[80:168], 96, C3, 80)):
        w3_ref[pl.ds(k, 80, stride=8), :] = piece
    w1 = w1_ref[...].T
    w2 = w2_ref[...].T
    w3 = w3_ref[...].T
    w1_low = w1.astype(BF16)
    w2_low = w2.astype(BF16)
    w3_low = w3.astype(BF16)
    t1_ref[...] = jnp.zeros(t1_ref.shape, BF16)
    for q in range(2):
        for p in range(2):
            row = 64 * q + 32 * p
            for i in range(8):
                lane = (i + 4 * p) * 16
                k = 32 * i + 16 * q
                t1_ref[row : row + 32, lane : lane + 16] = w1_low[0:32, k : k + 16]
    for p in range(2):
        b1_ref[32 * p : 32 * p + 32] = jnp.broadcast_to(w1[0:32, 256:257], (32, 256))
    b2_ref[...] = jnp.broadcast_to(w2[0:64, 512:513], (64, 256))
    b3_ref[...] = jnp.broadcast_to(w3[0:64, 576:577], (64, 256))
    for q in range(2):
        for i in range(4):
            k = 128 * i + 64 * q
            t2_ref[64 * q : 64 * q + 64, 64 * i : 64 * i + 64] = w2_low[0:64, k : k + 64]
    for j in range(3):
        for i in range(3):
            here = (slice(64 * j, 64 * j + 64), slice(64 * i, 64 * i + 64))
            k = (3 * i + j) * 64
            t3_ref[here] = w3_low[0:64, k : k + 64]
            k = (3 * (2 - i) + j) * 64
            back3_ref[here] = w3_ref[k : k + 64, 0:64].astype(BF16)
    for x in range(4):
        for y in range(2):
            for r in range(2):
                k = ((y + 2 - 2 * r) * 4 + x) * 32
                row = 32 * (2 * x + y)
                back2_ref[row : row + 32, 64 * r : 64 * r + 64] = w2_ref[k : k + 32, 0:64].astype(
                    BF16
                )


def conv_weights(block):
    shapes = [
        ((128, 192), BF16),
        ((64, 256), F32),
        ((128, 256), BF16),
        ((64, 256), F32),
        ((192, 192), BF16),
        ((64, 256), F32),
        ((192, 192), BF16),
        ((256, 128), BF16),
    ]
    return pl.pallas_call(
        weights_body,
        out_shape=[jax.ShapeDtypeStruct(shape, kind) for shape, kind in shapes],
        scratch_shapes=[
            pltpu.VMEM((BLOCK_ROWS, HID), F32),
            pltpu.VMEM((384, 128), F32),
            pltpu.VMEM((640, 128), F32),
            pltpu.VMEM((640, 128), F32),
        ],
        compiler_params=pltpu.CompilerParams(vmem_limit_bytes=VMEM_LIMIT),
        name="conv_weights",
    )(block)


def pixel_window(x_refs, first, start, width):
    sides = []
    for e in range(2):
        parts = [x_refs[first + k][e, :, start : start + width, :] for k in range(3)]
        sides.append(jnp.concatenate(parts, axis=0).reshape(12 * width, 128))
    return jnp.concatenate(sides, axis=1)


def forward_body(
    x_hbm,
    t1_ref,
    b1_ref,
    t2_ref,
    b2_ref,
    t3_ref,
    b3_ref,
    a1_hbm,
    a2_ref,
    a3_ref,
    x_ref,
    a1_ref,
    x_sems,
    sem,
):
    pair = pl.program_id(0)
    lanes = pl.ds(pl.multiple_of(256 * pair, 256), 256)

    def load(j, c):
        part = pl.ds(12 * c, 12)
        return pltpu.make_async_copy(
            x_hbm.at[pl.ds(2 * j, 2), part], x_ref.at[j, :, part], x_sems.at[7 * j + c]
        )

    @pl.when(pair == 0)
    def _():
        for j in range(x_ref.shape[0]):
            for c in range(7):
                load(j, c).start()

    def low(value, bias_ref):
        return jnp.maximum(value + bias_ref[...], 0.0).astype(BF16)

    ready = 0
    for m in range(10):
        while m % 2 == 0 and 12 * ready < 8 * m + 20:
            load(pair, ready).wait()
            ready += 1
        held = None
        for n in range(21):
            window = jnp.concatenate(
                [
                    x_ref[pair, e, 8 * m : 8 * m + 12, 16 * n : 16 * n + 16, :].reshape(192, 128)
                    for e in range(2)
                ],
                axis=1,
            )
            got = mm(t1_ref[...], window)
            if n > 0:
                out = low(held + got[64:128], b1_ref)
                a1_ref[2 * m : 2 * m + 2, n - 1] = out.reshape(2, C1, 256)
            held = got[0:64]
        if m % 2 == 1:
            here = pl.ds(2 * m - 2, 4)
            pltpu.make_async_copy(a1_ref.at[here], a1_hbm.at[here, :, :, lanes], sem.at[0]).start()

    def conv_two(p, carry):
        held = None
        for n in range(10):
            window = a1_ref[pl.ds(2 * p, 4), 2 * n : 2 * n + 2].reshape(256, 256)
            got = mm(t2_ref[...], window)
            if n > 0:
                a2_ref[p, n - 1] = low(held + got[64:128], b2_ref)
            held = got[0:64]
        a2_ref[p, 9] = jnp.zeros((C2, 256), BF16)
        return carry

    lax.fori_loop(0, 9, conv_two, 0, unroll=3)

    for p in range(7):
        held, older = None, None
        for x in range(9):
            got = mm(t3_ref[...], a2_ref[p : p + 3, x].reshape(192, 256))
            if x > 1:
                a3_ref[p, x - 2] = low(older + got[128:192], b3_ref)
            older = held + got[64:128] if x > 0 else None
            held = got[0:64]
    pltpu.make_async_copy(a1_ref, a1_hbm.at[:, :, :, lanes], sem.at[0]).wait()


def whole(shape):
    return pl.BlockSpec(shape, lambda *j: (0,) * len(shape), pipeline_mode=pl.Buffered(1))


def pixel_specs():
    def spec(k):
        return pl.BlockSpec((2, 4, 336, 128), lambda j, t: (j, 4 * t + k, 0, 0))

    return [spec(k) for k in range(5)]


def conv_forward(x, t1, b1, t2, b2, t3, b3):
    envs = x.shape[0]
    frames = envs * 128
    return pl.pallas_call(
        forward_body,
        grid=(envs // 2,),
        in_specs=[
            pl.BlockSpec(memory_space=pl.ANY),
            whole((128, 192)),
            whole((64, 256)),
            whole((128, 256)),
            whole((64, 256)),
            whole((192, 192)),
            whole((64, 256)),
        ],
        out_specs=[
            pl.BlockSpec(memory_space=pl.ANY),
            pl.BlockSpec((9, 10, C2, 256), lambda j: (0, 0, 0, j)),
            pl.BlockSpec((7, 7, C3, 256), lambda j: (0, 0, 0, j)),
        ],
        out_shape=[
            jax.ShapeDtypeStruct((20, 20, C1, frames), BF16),
            jax.ShapeDtypeStruct((9, 10, C2, frames), BF16),
            jax.ShapeDtypeStruct((7, 7, C3, frames), BF16),
        ],
        scratch_shapes=[
            pltpu.VMEM((envs // 2, 2, 84, 336, 128), BF16),
            pltpu.VMEM((20, 20, C1, 256), BF16),
            pltpu.SemaphoreType.DMA((7 * envs // 2,)),
            pltpu.SemaphoreType.DMA((1,)),
        ],
        compiler_params=pltpu.CompilerParams(vmem_limit_bytes=VMEM_LIMIT),
        name="conv_forward",
    )(x, t1, b1, t2, b2, t3, b3)


def dense_body(
    scale,
    a3_hbm,
    gathered_hbm,
    head_ref,
    sums_ref,
    advantage_ref,
    values_ref,
    actions_ref,
    behavior_ref,
    packed_hbm,
    wd_hbm,
    d_hidden_ref,
    gwh_ref,
    gbh_ref,
    loss_ref,
    wide_ref,
    a3_ref,
    gathered_ref,
    wd_ref,
    packed_ref,
    sems,
):
    shards, rows, _ = gathered_ref.shape
    halves = [slice(0, shards // 2), slice(shards // 2, shards)]
    loads = []
    for h, part in enumerate(halves):
        loads.append(
            pltpu.make_async_copy(gathered_hbm.at[part], gathered_ref.at[part], sems.at[h])
        )
        loads[h].start()
    load_a3 = pltpu.make_async_copy(a3_hbm, a3_ref, sems.at[2])
    load_a3.start()
    late = lax.broadcasted_iota(jnp.int32, (1, HID), 1) >= PHASE
    for h, part in enumerate(halves):
        loads[h].wait()
        for k in range(part.start, part.stop):
            if rows * k <= TOP + 1 + FEATURES and rows * (k + 1) > TOP:
                wide_ref[rows * k : rows * k + rows] = gathered_ref[k].astype(F32)
    for i in range(0, FEATURES, 448):
        wd_ref[i : i + 448] = jnp.where(
            late, wide_ref[TOP + i : TOP + i + 448], wide_ref[TOP + 1 + i : TOP + 449 + i]
        ).astype(BF16)
    store_wd = pltpu.make_async_copy(wd_ref, wd_hbm, sems.at[3])
    store_wd.start()
    bias = jnp.where(
        late,
        wide_ref[TOP + FEATURES : TOP + 1 + FEATURES],
        wide_ref[TOP + 1 + FEATURES : TOP + 2 + FEATURES],
    )
    bias = jnp.broadcast_to(bias, (8, HID)).T[:, 0:1]
    load_a3.wait()
    hidden_pre = mm_tn(wd_ref[...], a3_ref[...]) + bias
    hidden = jnp.maximum(hidden_pre, 0.0).astype(BF16)
    head = head_ref[...].astype(F32).T
    weights = pltpu.roll(head[0:32, 0:HID], PHASE, 1).astype(BF16)
    out = mm(weights, hidden) + head[0:32, HID : HID + 1]
    row = lax.broadcasted_iota(jnp.int32, out.shape, 0)
    is_logit = row < ACTIONS
    logits = jnp.where(is_logit, out, -jnp.inf)
    top = jnp.max(logits, axis=0, keepdims=True)
    shifted = out - top
    exps = jnp.where(is_logit, jnp.exp(shifted), 0.0)
    total = jnp.sum(exps, axis=0, keepdims=True)
    log_probs = jnp.where(is_logit, shifted - jnp.log(total), 0.0)
    probs = jnp.where(is_logit, jnp.exp(log_probs), 0.0)
    value = jnp.sum(jnp.where(row == ACTIONS, out, 0.0), axis=0, keepdims=True)

    def flat(array):
        return jnp.concatenate([array[e : e + 1] for e in range(array.shape[0])], axis=1)

    advantage = flat(advantage_ref[...])
    sums = sums_ref[...]
    mean = sums[0:1, 0:1] * scale
    spread = sums[1:2, 0:1] * scale - mean * mean
    normed = (advantage - mean) * lax.rsqrt(spread + 1e-05)
    returns = advantage + flat(values_ref[...])
    chosen = row == flat(actions_ref[...])
    taken = jnp.sum(jnp.where(chosen, log_probs, 0.0), axis=0, keepdims=True)
    ratio = jnp.exp(taken - flat(behavior_ref[...]))
    low = 1.0 - RATIO_CLIP
    high = 1.0 + RATIO_CLIP
    clipped = jnp.clip(ratio, low, high)
    plain = ratio * normed
    cut = clipped * normed
    entropy = -jnp.sum(probs * log_probs, axis=0, keepdims=True)
    error = value - returns
    losses = -jnp.minimum(plain, cut) + 0.5 * VALUE_COEF * error * error - ENTROPY_COEF * entropy
    loss_ref[...] = jnp.sum(losses, axis=1, keepdims=True) * scale
    plain_share = jnp.where(plain < cut, 1.0, jnp.where(plain == cut, 0.5, 0.0))
    inside = jnp.where(
        (ratio > low) & (ratio < high), 1.0, jnp.where((ratio == low) | (ratio == high), 0.5, 0.0)
    )
    d_taken = -scale * normed * ratio * (plain_share + (1.0 - plain_share) * inside)
    d_logits = d_taken * (jnp.where(chosen, 1.0, 0.0) - probs) + (scale * ENTROPY_COEF) * probs * (
        log_probs + entropy
    )
    d_value = scale * VALUE_COEF * error
    d_out = jnp.where(is_logit, d_logits, jnp.where(row == ACTIONS, d_value, 0.0)).astype(BF16)
    gwh_ref[...] = mm_nt(d_out, hidden)
    gbh_ref[...] = jnp.sum(d_out.astype(F32), axis=1, keepdims=True)
    back = mm_tn(weights, d_out)
    d_hidden = jnp.where(hidden > 0, back, 0.0).astype(BF16)
    d_hidden_ref[...] = d_hidden
    last = LEAD + FEATURES
    wide_ref[0:LEAD] = jnp.zeros((LEAD, HID), F32)
    wide_ref[last:] = jnp.zeros((wide_ref.shape[0] - last, HID), F32)
    ones = jnp.ones((8, d_hidden.shape[1]), BF16)
    wide_ref[last : last + 1] = mm_nt(ones, d_hidden)[0:1]
    done = 0
    for i in range(0, FEATURES, 448):
        wide_ref[LEAD + i : LEAD + i + 448] = mm_nt(a3_ref[i : i + 448], d_hidden)
        for k in range(done, shards):
            first = rows * k + LEAD - TOP - 1
            if first + rows >= LEAD + i + 448 and i + 448 < FEATURES:
                break
            done = k + 1
            for j in range(4):
                cols = slice(128 * j, 128 * j + 128)
                early_part = wide_ref[first : first + rows, cols]
                if 128 * j + 128 <= PHASE:
                    part = early_part
                elif 128 * j >= PHASE:
                    part = wide_ref[first + 1 : first + 1 + rows, cols]
                else:
                    part = jnp.where(
                        late[:, cols], wide_ref[first + 1 : first + 1 + rows, cols], early_part
                    )
                packed_ref[k, pl.ds(j, rows, stride=4), :] = part
            pltpu.make_async_copy(packed_ref.at[k], packed_hbm.at[k], sems.at[4]).start()
    store_wd.wait()
    pltpu.make_async_copy(packed_ref, packed_hbm, sems.at[4]).wait()


def dense_step(scale, a3, gathered, head, sums, advantage, values, actions, behavior):
    frames = a3.shape[1]
    shards, shard_rows, _ = gathered.shape
    rows = 32
    here = pl.BlockSpec(memory_space=pltpu.VMEM)
    away = pl.BlockSpec(memory_space=pl.ANY)
    return pl.pallas_call(
        lambda *refs: dense_body(scale, *refs),
        in_specs=[away, away] + [here] * 6,
        out_specs=[away, away] + [here] * 4,
        out_shape=[
            jax.ShapeDtypeStruct((shards, 4 * shard_rows, 128), F32),
            jax.ShapeDtypeStruct((FEATURES, HID), BF16),
            jax.ShapeDtypeStruct((HID, frames), BF16),
            jax.ShapeDtypeStruct((rows, HID), F32),
            jax.ShapeDtypeStruct((rows, 1), F32),
            jax.ShapeDtypeStruct((1, 1), F32),
        ],
        scratch_shapes=[
            pltpu.VMEM((max(shards * shard_rows, TOP + 1 + FEATURES) + 2 * LEAD - TOP, HID), F32),
            pltpu.VMEM(a3.shape, BF16),
            pltpu.VMEM(gathered.shape, BF16),
            pltpu.VMEM((FEATURES, HID), BF16),
            pltpu.VMEM((shards, 4 * shard_rows, 128), F32),
            pltpu.SemaphoreType.DMA((5,)),
        ],
        compiler_params=pltpu.CompilerParams(vmem_limit_bytes=VMEM_LIMIT),
        name="dense_step",
    )(a3, gathered, head, sums, advantage, values, actions, behavior)


def fold(g_ref, width, rows):
    step = HID // width
    lane = lax.broadcasted_iota(jnp.int32, (1, 128), 1)
    columns = []
    for m in range(4):
        total = 0.0
        for t in range(128 // width):
            piece = g_ref[pl.ds(m * 128 // width + t, rows, stride=step), :]
            piece = jnp.where(lane < width, piece, 0.0)
            total = total + (pltpu.roll(piece, width * t, 1) if t else piece)
        columns.append(total)
    return columns


def upper_body(
    a1_hbm,
    a2_ref,
    a3_ref,
    wd_ref,
    d_hidden_ref,
    t3_ref,
    d2_ref,
    packed_ref,
    r2_ref,
    r3_ref,
    a1_ref,
    d3_ref,
    g2_ref,
    g3_ref,
    sems,
):
    step = pl.program_id(0)
    lanes = pl.ds(pl.multiple_of(256 * step, 256), 256)
    load_a1 = pltpu.make_async_copy(a1_hbm.at[:, :, :, lanes], a1_ref, sems.at[0])
    load_a1.start()

    @pl.when(step == 0)
    def _():
        for ref in (r2_ref, r3_ref):
            ref[...] = jnp.zeros(ref.shape, F32)
        for p in (0, 1, 9, 10):
            d3_ref[p] = jnp.zeros((8, C3, 256), BF16)

    for p in (0, 10):
        d2_ref[p, 1:10] = jnp.zeros((9, C2, 256), BF16)
    zero = jnp.zeros((), BF16)
    for p in range(7):
        back = mm(wd_ref[448 * p : 448 * p + 448], d_hidden_ref[...]).reshape(7, C3, 256)
        d3_ref[p + 2, 0:7] = jnp.where(a3_ref[p] > 0, back.astype(BF16), zero)
        d3_ref[p + 2, 7] = jnp.zeros((C3, 256), BF16)

    left = [a2_ref[p : p + 3, 4 * g : 4 * g + 6].reshape(1152, 256) for p in range(7) for g in range(2)]
    right = [d3_ref[p + 2, 4 * g : 4 * g + 4].reshape(256, 256) for p in range(7) for g in range(2)]
    left = jnp.concatenate(left, axis=1)
    left = jnp.concatenate([left, jnp.ones((16, left.shape[1]), BF16)], axis=0)
    r3_ref[...] += mm_nt(left, jnp.concatenate(right, axis=1))

    def three_input(y, carry):
        parts = []
        for x in range(9):
            if x < 7:
                parts.append(mm(t3_ref[...], d3_ref[pl.ds(y, 3), x].reshape(192, 256)))
            back = 0.0
            for j in range(3):
                if 0 <= x - j < 7:
                    back = back + parts[x - j][64 * j : 64 * j + 64]
            d2_ref[y + 1, x + 1] = jnp.where(a2_ref[y, x] > 0, back.astype(BF16), zero)
        return carry

    lax.fori_loop(0, 9, three_input, 0, unroll=3)
    load_a1.wait()

    def two_weights(r, carry):
        left, right = [], []
        for k in range(3):
            p = 3 * r + k
            for g in range(3):
                left.append(a1_ref[pl.ds(2 * p, 4), 6 * g : 6 * g + 8].reshape(1024, 256))
                right.append(d2_ref[p + 1, 1 + 3 * g : 4 + 3 * g].reshape(192, 256))
        left = jnp.concatenate(left, axis=1)
        left = jnp.concatenate([left, jnp.ones((16, left.shape[1]), BF16)], axis=0)
        r2_ref[:, 0:192] += mm_nt(left, jnp.concatenate(right, axis=1))
        return carry

    lax.fori_loop(0, 3, two_weights, 0)

    @pl.when(step == pl.num_programs(0) - 1)
    def _():
        g2_ref[...] = jnp.zeros(g2_ref.shape, F32)
        g3_ref[...] = jnp.zeros(g3_ref.shape, F32)
        for i in range(4):
            k = 256 * i
            total = r2_ref[k : k + 128, 0:128]
            total = total + pltpu.roll(r2_ref[k + 64 : k + 192, 0:128], 64, 1)
            g2_ref[128 * i : 128 * i + 128] = total + r2_ref[k + 128 : k + 256, 128:256]
        for i in range(3):
            k = 384 * i
            total = r3_ref[k : k + 192, 0:128]
            total = total + pltpu.roll(r3_ref[k + 64 : k + 256, 0:128], 64, 1)
            total = total + r3_ref[k + 128 : k + 320, 128:256]
            total = total + pltpu.roll(r3_ref[k + 192 : k + 384, 128:256], 64, 1)
            g3_ref[192 * i : 192 * i + 192] = total
        row = r2_ref[1024:1032]
        row = row[:, 0:128] + pltpu.roll(row[:, 0:128], 64, 1) + row[:, 128:256]
        g2_ref[512:513] = row[0:1]
        row = r3_ref[1152:1160]
        row = row[:, 0:128] + row[:, 128:256]
        g3_ref[576:577] = (row + pltpu.roll(row, 64, 1))[0:1]
        lane = lax.broadcasted_iota(jnp.int32, (1, HID), 1)
        packed_ref[...] = jnp.zeros(packed_ref.shape, F32)
        for ref, rows, base, phase in ((g2_ref, 72, 16, 32), (g3_ref, 80, 80, 96)):
            turned = pltpu.roll(jnp.concatenate(fold(ref, 64, rows), axis=1), phase, 1)
            for j in range(4):
                cols = slice(128 * j, 128 * j + 128)
                here = pl.ds(4 * base + j, rows, stride=4)
                packed_ref[here, :] += jnp.where(lane >= phase, turned, 0.0)[:, cols]
                if j == 0:
                    below = pl.ds(4 * base + 4, rows, stride=4)
                    packed_ref[below, :] += jnp.where(lane < phase, turned, 0.0)[:, cols]


def upper_backward(a1, a2, a3, w_dense, d_hidden, t3):
    frames = a1.shape[3]
    return pl.pallas_call(
        upper_body,
        grid=(frames // 256,),
        in_specs=[
            pl.BlockSpec(memory_space=pl.ANY),
            pl.BlockSpec((9, 10, C2, 256), lambda j: (0, 0, 0, j)),
            pl.BlockSpec((7, 7, C3, 256), lambda j: (0, 0, 0, j)),
            whole((FEATURES, HID)),
            pl.BlockSpec((HID, 256), lambda j: (0, j)),
            whole((192, 192)),
        ],
        out_specs=[
            pl.BlockSpec((11, 11, C2, 256), lambda j: (0, 0, 0, j)),
            whole((4 * BLOCK_ROWS, 128)),
        ],
        out_shape=[
            jax.ShapeDtypeStruct((11, 11, C2, frames), BF16),
            jax.ShapeDtypeStruct((4 * BLOCK_ROWS, 128), F32),
        ],
        scratch_shapes=[
            pltpu.VMEM((1040, 256), F32),
            pltpu.VMEM((1168, 256), F32),
            pltpu.VMEM((20, 20, C1, 256), BF16),
            pltpu.VMEM((11, 8, C3, 256), BF16),
            pltpu.VMEM((640, 128), F32),
            pltpu.VMEM((640, 128), F32),
            pltpu.SemaphoreType.DMA((1,)),
        ],
        compiler_params=pltpu.CompilerParams(vmem_limit_bytes=VMEM_LIMIT),
        name="upper_backward",
    )(a1, a2, a3, w_dense, d_hidden, t3)


def lower_body(
    x0, x1, x2, x3, x4, a1_ref, d2_ref, t2_ref, packed_ref, r1_ref, g1_ref, d1_ref
):
    x_refs = (x0, x1, x2, x3, x4)
    t = pl.program_id(1)

    @pl.when((pl.program_id(0) == 0) & (t == 0))
    def _():
        r1_ref[...] = jnp.zeros(r1_ref.shape, F32)

    zero = jnp.zeros((), BF16)
    for h in range(2):
        held = None
        for n in range(10):
            back = held
            if n < 9:
                got = mm(t2_ref[...], d2_ref[pl.ds(2 * t + h, 2), n + 1].reshape(128, 256))
                back = got[0:128] if n == 0 else held + got[0:128]
                held = got[128:256]
            for x in range(2):
                for y in range(2):
                    k = 32 * (2 * x + y)
                    kept = a1_ref[2 * h + y, 2 * n + x] > 0
                    masked = jnp.where(kept, back[k : k + 32].astype(BF16), zero)
                    row = 128 * (n % 2) + k
                    d1_ref[h, row : row + 32, 256 * (n // 2) : 256 * (n // 2) + 256] = masked
        window = jnp.concatenate(
            [pixel_window(x_refs, 2 * h, 64 * n, 80) for n in range(5)], axis=1
        )
        window = jnp.concatenate([window, jnp.ones((16, window.shape[1]), BF16)], axis=0)
        r1_ref[...] += mm_nt(window, d1_ref[h])

    @pl.when((pl.program_id(0) == pl.num_programs(0) - 1) & (t == 4))
    def _():
        g1_ref[...] = jnp.zeros(g1_ref.shape, F32)
        for i in range(8):
            total = 0.0
            for p in range(2):
                for q in range(4):
                    k = (i + 4 * p) * 80 + 16 * q
                    col = 128 * (q // 2)
                    turn = 64 * (q % 2) + 32 * p
                    slab = r1_ref[k : k + 32, col : col + 128]
                    total = total + (pltpu.roll(slab, 128 - turn, 1) if turn else slab)
            g1_ref[32 * i : 32 * i + 32] = total
        row = r1_ref[960:968, 0:128] + r1_ref[960:968, 128:256]
        row = row + pltpu.roll(row, 64, 1)
        g1_ref[256:257] = (row + pltpu.roll(row, 96, 1))[0:1]
        packed_ref[...] = jnp.zeros(packed_ref.shape, F32)
        for j, part in enumerate(fold(g1_ref, 32, 24)):
            packed_ref[pl.ds(j, 24, stride=4), :] = part


def lower_backward(x, a1, d2, t2):
    envs = x.shape[0]
    return pl.pallas_call(
        lower_body,
        grid=(envs // 2, 5),
        in_specs=pixel_specs()
        + [
            pl.BlockSpec((4, 20, C1, 256), lambda j, t: (t, 0, 0, j)),
            pl.BlockSpec((11, 11, C2, 256), lambda j, t: (0, 0, 0, j)),
            whole((256, 128)),
        ],
        out_specs=whole((4 * BLOCK_ROWS, 128)),
        out_shape=jax.ShapeDtypeStruct((4 * BLOCK_ROWS, 128), F32),
        scratch_shapes=[
            pltpu.VMEM((976, 256), F32),
            pltpu.VMEM((384, 128), F32),
            pltpu.VMEM((2, 256, 1280), BF16),
        ],
        compiler_params=pltpu.CompilerParams(vmem_limit_bytes=VMEM_LIMIT),
        name="lower_backward",
    )(x, x, x, x, x, a1, d2, t2)


def swap(value, lanes, step):
    return lax.ppermute(value, "dp", [(i, i ^ step) for i in range(lanes)])


def other_group(value):
    return lax.ppermute(value, "group", [(0, 1), (1, 0)])


def halving_order(lanes):
    return [1 << k for k in range(lanes.bit_length() - 1)]


def sum_everywhere(value, lanes):
    for step in halving_order(lanes):
        value = value + swap(value, lanes, step)
    return value


def scatter_sum(blocks, lanes, place):
    for step in halving_order(lanes):
        pairs = blocks.reshape((blocks.shape[0] // 2, 2) + blocks.shape[1:])
        high = (place // step) % 2 == 1
        kept = jnp.where(high, pairs[:, 1], pairs[:, 0])
        sent = jnp.where(high, pairs[:, 0], pairs[:, 1])
        blocks = kept + swap(sent, lanes, step)
    return blocks[0]


def gather_blocks(block, beside, lanes, place):
    arrived = []
    for k, step in enumerate(reversed(halving_order(lanes))):
        if k == 0:
            both = [(i, (i ^ step) ^ lanes) for i in range(2 * lanes)]
            blocks = jnp.stack([block, other_group(block)])[None]
            other = jnp.stack(
                [swap(block, lanes, step), lax.ppermute(block, ("group", "dp"), both)]
            )[None]
        else:
            other = swap(blocks, lanes, step)
        if 0 < k <= len(beside):
            other, part = lax.optimization_barrier((other, beside[k - 1]))
            arrived.append(part)
        if step == 1:
            return blocks, other, arrived
        high = (place // step) % 2 == 1
        blocks = jnp.stack(
            [jnp.where(high, other, blocks), jnp.where(high, blocks, other)], axis=1
        ).reshape((2 * blocks.shape[0],) + blocks.shape[1:])


def first_rows_everywhere(master, sums, lanes, place):
    rows = master.shape[0] // HID
    owners = -(-(TOP + 1) // rows)
    order = halving_order(lanes)
    if owners == 1:
        block = master[: BLOCK_ROWS * HID].reshape(BLOCK_ROWS, HID).astype(BF16)
        row = lax.broadcasted_iota(jnp.int32, (BLOCK_ROWS, 1), 0)
        block = jnp.where((place == 0) & (row <= TOP), block, jnp.zeros((), BF16))
        steps = list(reversed(order))
        left = order[1:2] + list(reversed(order[2:])) + order[:1]
        while steps:
            now, steps = steps[:2], steps[2:]
            jumps = now if len(now) == 1 else [now[0], now[1], now[0] + now[1]]
            total = block
            for jump in jumps:
                pairs = [(i, i + jump) for i in range(0, lanes, 2 * now[0])]
                total = total + lax.ppermute(block, "dp", pairs)
            summed = sums + swap(sums, lanes, left.pop(0))
            block, sums = lax.optimization_barrier((total, summed))
        return block, sums, left
    local = master.reshape(rows, HID).astype(BF16)
    block = jnp.zeros((owners, rows, HID), BF16)
    block = jnp.where(jnp.arange(owners)[:, None, None] == place, local[None], block)
    block = sum_everywhere(block, lanes).reshape(owners * rows, HID)[: TOP + 1]
    return jnp.pad(block, ((0, BLOCK_ROWS - TOP - 1), (0, 0))), sums, order


def finish_blocks(own_len):
    block = min(208, -(-own_len // 8) * 8)
    return block, -(-own_len // block)


def facts_body(dense_ref, piece_ref, loss_ref, message_ref, *part_refs):
    dense = dense_ref[...]
    piece = piece_ref[...]
    start = 0
    for ref in part_refs:
        ref[...] = dense[start : start + ref.shape[0]]
        start += ref.shape[0]
    squares = jnp.sum(dense * dense, axis=0, keepdims=True)
    squares = squares + jnp.sum(piece * piece, axis=0, keepdims=True)
    squares = jnp.sum(squares, axis=1, keepdims=True)
    height = piece.shape[0]
    message_ref[0:height] = piece
    row = lax.broadcasted_iota(jnp.int32, (8, 128), 0)
    message_ref[height : height + 8] = jnp.where(row == 0, squares, loss_ref[...])


def facts_message(dense, piece, loss):
    own_len = dense.shape[0]
    block, steps = finish_blocks(own_len)
    first = block * (steps // 2)
    lengths = [length for length in (first, own_len - first) if length]
    shapes = [(piece.shape[0] + 8, 128)] + [(length, 128) for length in lengths]
    message, *parts = pl.pallas_call(
        facts_body,
        out_shape=[jax.ShapeDtypeStruct(shape, F32) for shape in shapes],
        name="facts_message",
    )(dense, piece, loss)
    return message, parts


def finish_body(
    parts,
    own_len,
    switch,
    place_ref,
    scalars_ref,
    near_ref,
    far_ref,
    low_other_ref,
    high_other_ref,
    mine_ref,
    first_ref,
    other_first_ref,
    second_ref,
    other_second_ref,
    master_ref,
    momentum_ref,
    clipped_ref,
    first_out,
    second_out,
    moved_ref,
    momentum_out,
    final_ref,
    low_ref,
    norm_ref,
    loss_ref,
    extra_ref,
):
    height = near_ref.shape[2] - 8
    place = place_ref[0]
    first_step = pl.program_id(0) == 0

    @pl.when(first_step)
    def _():
        extra_ref[...] = jnp.zeros(extra_ref.shape, F32)

    for start, stop, target in parts:
        for owner in range(target // own_len, (target + stop - start - 1) // own_len + 1):
            shift = target - start - owner * own_len
            low = max(start, -shift)
            high = min(stop, own_len - shift)

            @pl.when(first_step & (place == owner))
            def _(owner=owner, shift=shift, low=low, high=high):
                for k in range(low // height, (high - 1) // height + 1):
                    a = max(low, k * height)
                    b = min(high, (k + 1) * height)
                    source = near_ref if k % 2 == owner % 2 else far_ref
                    for g in range(2):
                        extra_ref[g, a + shift : b + shift] = source[
                            k // 2, g, a - k * height : b - k * height
                        ]

    block = master_ref.shape[0]
    here = pl.ds(pl.multiple_of(block * pl.program_id(0), 8), block)

    factors = []
    for g in range(2):
        facts = jnp.sum(near_ref[:, g, height : height + 8, :], axis=0)
        facts = facts + jnp.sum(far_ref[:, g, height : height + 8, :], axis=0)
        norm = jnp.sqrt(facts[0:1, 0:1])
        factors.append(jnp.minimum(1.0, CLIP_NORM / (norm + 1e-06)))
        if g == 0:
            norm_ref[...] = norm
            loss_ref[...] = facts[1:2, 0:1]
    master = master_ref[...]

    def inner_step(g, dense, one_ref, two_ref):
        clipped = (dense + extra_ref[g, here]) * factors[g]
        first_next = BETA_ONE * one_ref[...] + (1.0 - BETA_ONE) * clipped
        second_next = BETA_TWO * two_ref[...] + (1.0 - BETA_TWO) * clipped * clipped
        first_hat = first_next / scalars_ref[0]
        second_hat = second_next / scalars_ref[1]
        inner = master - LEARN_RATE * (
            first_hat / (jnp.sqrt(second_hat) + ADAM_EPSILON) + WEIGHT_DECAY * master
        )
        return clipped, first_next, second_next, master - inner

    clipped, first_next, second_next, drift = inner_step(0, mine_ref[...], first_ref, second_ref)
    clipped_ref[:, 0, :] = clipped
    first_out[:, 0, :] = first_next
    second_out[:, 0, :] = second_next
    other = jnp.where(pl.program_id(0) < switch, low_other_ref[...], high_other_ref[...])
    _, _, _, other_drift = inner_step(1, other, other_first_ref, other_second_ref)
    moved = (drift + other_drift) / 2.0
    moved_ref[...] = moved
    momentum_next = OUTER_MOMENTUM * momentum_ref[...] + moved
    momentum_out[...] = momentum_next
    final = master - OUTER_RATE * (moved + OUTER_MOMENTUM * momentum_next)
    final_ref[...] = final
    low_ref[...] = final.astype(BF16)


def finish(parts, place, scalars, near, far, others, *arrays):
    own_len = arrays[0].shape[0]
    block, steps = finish_blocks(own_len)
    scalar = pl.BlockSpec(memory_space=pltpu.SMEM)

    def spec(array):
        if len(array.shape) == 3:
            return pl.BlockSpec((block, 1, 128), lambda k: (k, 0, 0))
        return pl.BlockSpec((block, 128), lambda k: (k, 0))

    outs = [jax.ShapeDtypeStruct((own_len, 1, 128), F32)] * 3
    outs += [jax.ShapeDtypeStruct((own_len, 128), F32)] * 3
    outs += [jax.ShapeDtypeStruct((own_len, 128), BF16)]
    return pl.pallas_call(
        lambda *refs: finish_body(parts, own_len, steps // 2, *refs),
        grid=(steps,),
        in_specs=[scalar, scalar, whole(near.shape), whole(far.shape)]
        + [
            pl.BlockSpec((block, 128), lambda k: (jnp.minimum(k, max(steps // 2 - 1, 0)), 0)),
            pl.BlockSpec((block, 128), lambda k: (jnp.maximum(k - steps // 2, 0), 0)),
        ]
        + [spec(array) for array in arrays],
        out_specs=[spec(array) for array in outs] + [whole((1, 1))] * 2,
        out_shape=outs + [jax.ShapeDtypeStruct((1, 1), F32)] * 2,
        scratch_shapes=[pltpu.VMEM((2, block * steps, 128), F32)],
        name="finish",
    )(place, scalars, near, far, *others, *arrays)


def on_device(
    frames,
    actions,
    rewards,
    old_values,
    next_values,
    terminal,
    truncated,
    behavior_logprob,
    master,
    first_moment,
    second_moment,
    outer_momentum,
    step_count,
):
    lanes = lax.axis_size("dp")
    place = lax.axis_index("dp")
    shard_len = master.shape[0]
    rows = shard_len // HID
    groups = lax.axis_size("group")
    assert groups == 2 and rows * HID == shard_len and frames.shape[2] == 128

    master_rows = master.reshape(rows, HID)
    low_rows = master_rows.astype(BF16)
    gathered = lax.all_gather(low_rows, "dp", axis=0)

    advantage, sums = trajectory_advantages(
        rewards[0], old_values[0], next_values[0], terminal[0], truncated[0]
    )
    envs_here, steps_here = advantage.shape
    batch = envs_here * steps_here
    total_frames = batch * lanes
    block, sums, left = first_rows_everywhere(master, sums, lanes, place)
    moment_step = step_count[0].astype(F32)
    scalars = jnp.stack(
        [1.0 - jnp.power(BETA_ONE, moment_step), 1.0 - jnp.power(BETA_TWO, moment_step)]
    )
    block, scalars = lax.optimization_barrier((block, scalars))
    while len(left) > 2:
        sums = sums + swap(sums, lanes, left.pop(0))
    x = frames[0].transpose(0, 2, 3, 1)
    came = swap(sums, lanes, left.pop(0)) if left else jnp.zeros_like(sums)
    t1, b1, t2, b2, t3, b3, back3, back2 = conv_weights(block)
    t1, came = lax.optimization_barrier((t1, came))
    sums = sums + came
    came = swap(sums, lanes, left.pop(0)) if left else jnp.zeros_like(sums)
    a1, a2, a3 = conv_forward(x, t1, b1, t2, b2, t3, b3)
    a3, came = lax.optimization_barrier((a3, came))
    sums = sums + came

    tail = TOP + FEATURES + 1
    head_owner = tail // rows
    head_flat = gathered[head_owner:].reshape((lanes - head_owner) * rows, HID)
    head_flat = head_flat[tail - head_owner * rows :].reshape(-1)[PHASE : PHASE + HEAD_LEN]
    head = jnp.pad(head_flat.reshape(HID + 1, ACTIONS + 1), ((0, 7), (0, 127 - ACTIONS)))
    packed_dense, w_dense, d_hidden, g_head, g_head_bias, loss_local = dense_step(
        1.0 / total_frames,
        a3.reshape(FEATURES, batch),
        gathered,
        head,
        sums,
        advantage,
        old_values[0],
        actions[0],
        behavior_logprob[0],
    )
    dense_owned = lax.psum_scatter(packed_dense, "dp", scatter_dimension=0, tiled=False)
    d_hidden, first_sent, second_sent = lax.optimization_barrier(
        (d_hidden, first_moment, second_moment)
    )
    d2, upper = upper_backward(a1, a2, a3, w_dense, d_hidden, back3)
    first_flat = first_sent.reshape(shard_len)
    second_flat = second_sent.reshape(shard_len)
    d2, other_first, other_second = lax.optimization_barrier(
        (d2, other_group(first_flat), other_group(second_flat))
    )
    lower = lower_backward(x, a1, d2, back2)

    tail_rows = lanes * rows - tail
    head_part = jnp.concatenate(
        [
            jnp.zeros((PHASE,), F32),
            jnp.roll(g_head[: ACTIONS + 1].T, -PHASE, axis=0).reshape(-1),
            g_head_bias[: ACTIONS + 1, 0],
            jnp.zeros((tail_rows * HID - PHASE - HEAD_LEN,), F32),
        ]
    ).reshape(4 * tail_rows, 128)
    real = 4 * (BLOCK_ROWS + tail_rows)
    count = -(-real // (8 * lanes)) * 8 * lanes
    head_part = jnp.pad(head_part, ((0, count - real), (0, 0)))
    small = jnp.concatenate([lower + upper, head_part], axis=0)
    piece = scatter_sum(small.reshape(lanes, count // lanes, 128), lanes, place)
    message, dense_parts = facts_message(dense_owned, piece, loss_local)
    near, far, dense_parts = gather_blocks(
        message, [other_group(part) for part in dense_parts], lanes, place
    )

    own_len = 4 * rows
    parts = ((0, 4 * (TOP + 1), 0), (4 * BLOCK_ROWS, real, 4 * tail))

    def view(value):
        return value.reshape(own_len, 128)

    results = finish(
        parts,
        place.reshape(1),
        scalars,
        near,
        far,
        (dense_parts[0], dense_parts[-1]),
        dense_owned,
        view(first_flat),
        view(other_first),
        view(second_flat),
        view(other_second),
        view(master),
        view(outer_momentum),
    )
    clipped, first_next, second_next, moved, momentum_next, final, final_low, norm, loss = results
    return (
        clipped.reshape(1, shard_len),
        norm.reshape(1),
        loss.reshape(1),
        first_next.reshape(1, shard_len),
        second_next.reshape(1, shard_len),
        moved.reshape(shard_len),
        momentum_next.reshape(shard_len),
        final.reshape(shard_len),
        final_low.reshape(shard_len),
    )


def solution(mesh):
    return jax.shard_map(
        on_device,
        mesh=mesh,
        in_specs=(
            P("group", "dp", None, None, None),
            P("group", "dp", None),
            P("group", "dp", None),
            P("group", "dp", None),
            P("group", "dp", None),
            P("group", "dp", None),
            P("group", "dp", None),
            P("group", "dp", None),
            P("dp"),
            P("group", "dp"),
            P("group", "dp"),
            P("dp"),
            P(),
        ),
        out_specs=(
            P("group", "dp"),
            P("group"),
            P("group"),
            P("group", "dp"),
            P("group", "dp"),
            P("dp"),
            P("dp"),
            P("dp"),
            P("dp"),
        ),
        check_vma=False,
    )
```
